32 devices in a mesh: tm: 2 (over x), segment: 4 (over z), band: 4 (over y, core).
Axes of the slice: x: 2, y: 2, z: 4, core: 2. Of those that a mesh axis runs over, the one named last changes fastest.
Arguments:
- features: bfloat16 [4, 4, 16, 16, 384], P(None, 'tm', 'band'), may hold values from -6 to 6
- conv_weight: bfloat16 [4, 27, 384, 384], P('segment'), may hold values from -0.0625 to 0.0625
- conv_bias: float32 [4, 384], P('segment'), may hold values from -3 to 3
- norm_gain: float32 [4, 384], P('segment'), may hold values from 0.5 to 2
Outputs:
- decoded: bfloat16 [4, 4, 16, 16, 384], P('segment', 'tm', 'band')
The draws below stay inside these ranges and needn't reach their ends.
All inputs are finite; a program needn't handle non-finite values.
Results may differ from the reference program's by a relative error of at most 0.007.
Values may be sent and summed in bfloat16 or wider, within the bound.
No kernel may reach another device: no remote copies, remote signals or barrier semaphores. Data moves between devices by JAX's collectives and lax.ppermute only.
A program may use at most 64 MiB of HBM per device.

```python
import math
import jax
import jax.numpy as jnp
from jax import lax

C = 384
COLS = 16
CLIPS = 4
LAYERS = 4
FRAMES = 4
HEIGHT = 16


def level_of(rng, extent, shards, least, largest):
    level = 1.0
    for position, parts in shards:
        heights = jax.random.uniform(jax.random.fold_in(jax.random.fold_in(rng, 6), position), (parts,), jnp.float32, least / len(shards), largest / len(shards))
        level = level * jnp.repeat(jnp.exp(heights), extent[position] // parts).reshape((-1,) + (1,) * (len(extent) - 1 - position))
    return level


def normal_values(rng, extent, width, reach, split=(), held_as=jnp.bfloat16):
    values = width * jax.random.normal(rng, extent, jnp.float32)
    if split:
        values = values * level_of(rng, extent, split, -0.22, 0.18)
    return jnp.clip(values, -reach, reach).astype(held_as)


def setup_inputs(seed: int = 0) -> dict:
    key_list = jax.random.split(jax.random.key(seed), 5)
    features = normal_values(key_list[0], (CLIPS, FRAMES, HEIGHT, COLS, C), 1.0, 6.0, ((1, 2), (2, 4)))
    conv_weight = normal_values(key_list[1], (LAYERS, 27, C, C), (27 * C) ** -0.5, 0.0625, ((0, 4),))
    conv_bias = normal_values(key_list[2], (LAYERS, C), 0.5, 3.0, ((0, 4),), jnp.float32)
    norm_gain = jnp.clip(jnp.exp(math.log(2.0) - 1.3862944 * jax.random.uniform(key_list[3], (LAYERS, C), jnp.float32) ** level_of(key_list[3], (LAYERS, C), ((0, 4),), -0.2, 0.2)), 0.5, 2.0)
    return {"features": features, "conv_weight": conv_weight, "conv_bias": conv_bias, "norm_gain": norm_gain}


def prepare(field, scale_gain):
    wide = field.astype(jnp.float32)
    meansq = lax.optimization_barrier(jnp.mean(wide * wide, axis=-1, keepdims=True))
    return jax.nn.silu(wide * lax.rsqrt(meansq + 1e-06) * scale_gain).astype(jnp.bfloat16)

def reference(features, conv_weight, conv_bias, norm_gain):
    hidden = features
    for layer_index in range(LAYERS):
        kernel = conv_weight[layer_index]
        shift_bias = conv_bias[layer_index]
        scale_gain = norm_gain[layer_index]

        def one_clip(clip_field):
            ready = prepare(clip_field, scale_gain)
            padded = jnp.pad(ready, ((2, 0), (1, 1), (1, 1), (0, 0)))
            total = jnp.zeros((FRAMES * HEIGHT * COLS, C), jnp.float32)
            for offset_time in range(3):
                for offset_row in range(3):
                    for offset_col in range(3):
                        piece = padded[offset_time:offset_time + FRAMES, offset_row:offset_row + HEIGHT, offset_col:offset_col + COLS]
                        total = total + jnp.dot(piece.reshape(-1, C), kernel[offset_time * 9 + offset_row * 3 + offset_col], preferred_element_type=jnp.float32)
            summed = clip_field.astype(jnp.float32) + total.reshape(clip_field.shape) + shift_bias
            return summed.astype(jnp.bfloat16)
        hidden = lax.map(one_clip, hidden)
    return hidden
```

```python
import functools

import jax
import jax.numpy as jnp
from jax import lax
from jax.experimental import pallas as pl
from jax.experimental.pallas import tpu as pltpu
from jax.sharding import PartitionSpec as P

HALVES = 2
LAG = 2
VMEM = pltpu.VMEM
MESH_AXES = ("tm", "segment", "band")


def whole(space=VMEM):
    return pl.BlockSpec(memory_space=space)


def resident(value):
    return pltpu.with_memory_space_constraint(value, pltpu.VMEM)


def is_active(place, slot, frames):
    number = slot - LAG * place[0]
    return jnp.logical_and(place[2] > 0, jnp.logical_and(number >= 0, number < frames))


def frame_kernel(slot, frames, has_pieces, has_received, finals, half_pos, cols, *refs):
    refs = list(refs)
    place = refs.pop(0)
    pieces = [refs.pop(0) for _ in range(has_pieces)]
    received = refs.pop(0) if has_received else None
    partial, weight, bias, gain = refs[:4]
    refs = refs[4:]
    if finals and half_pos:
        refs = refs[finals:]
    out, spread = refs[:2]
    refs = refs[2:]
    tails = refs[:finals]
    entry = refs[finals]
    size, channels = out.shape

    @pl.when(is_active(place, slot, frames))
    def _():
        if has_pieces:
            step = size // has_pieces

            @pl.when(place[0] == 0)
            def _():
                for number, piece in enumerate(pieces):
                    entry[pl.ds(number * step, step), :] = piece[...]

        if has_received:

            @pl.when(place[0] > 0)
            def _():
                entry[...] = received[...]

        wide = entry[...].astype(jnp.float32)
        meansq = jnp.sum(wide * wide, axis=-1, keepdims=True) * (1.0 / channels)
        normed = wide * lax.rsqrt(meansq + 1e-06) * gain[...]
        ready = normed / (1.0 + jnp.exp(-normed))
        column = lax.broadcasted_iota(jnp.int32, ready.shape, 0) & (cols - 1)
        before = jnp.where(column == 0, 0.0, pltpu.roll(ready, 1, 0))
        after = jnp.where(column == cols - 1, 0.0, pltpu.roll(ready, size - 1, 0))
        edge = jnp.zeros((cols, 3 * channels), jnp.bfloat16)
        spread[pl.ds(0, cols), :] = edge
        spread[pl.ds(size + cols, cols), :] = edge
        for number, value in enumerate((before, ready, after)):
            spread[pl.ds(cols, size), pl.ds(number * channels, channels)] = value.astype(jnp.bfloat16)
        total = partial[...] + wide + bias[...]
        for row in range(3):
            total += jnp.dot(
                spread[pl.ds(row * cols, size), :], weight[2, row], preferred_element_type=jnp.float32
            )
        out[...] = total.astype(jnp.bfloat16)
        if finals:
            length = tails[0].shape[1]
            for number, tail in enumerate(tails):
                start = pl.multiple_of((place[1] + number) * length, length)
                tail[half_pos] = out[pl.ds(start, length), :]


def history_kernel(slot, frames, cols, place, spread, near, far, weight, near_out, far_out):
    size = near.shape[0]

    @pl.when(is_active(place, slot, frames))
    def _():
        total = far[...]
        later = jnp.zeros(far.shape, jnp.float32)
        for row in range(3):
            ready = spread[pl.ds(row * cols, size), :]
            total += jnp.dot(ready, weight[1, row], preferred_element_type=jnp.float32)
            later += jnp.dot(ready, weight[0, row], preferred_element_type=jnp.float32)
        near_out[...] = total
        far_out[...] = later


def local(features, conv_weight, conv_bias, norm_gain):
    times, segments, bands = (lax.axis_size(name) for name in MESH_AXES)
    time, position, band = (lax.axis_index(name) for name in MESH_AXES)
    clips, own_frames, own_rows, cols, channels = features.shape
    frames = own_frames * times
    rows = own_rows * bands
    per_half = bands // HALVES
    half_rows = rows // HALVES
    window = half_rows + segments
    pieces = window // own_rows
    assert clips == segments and window % own_rows == 0 and pieces - per_half == bands - pieces
    assert clips % per_half == 0 and clips // per_half <= times
    size = window * cols
    piece = own_rows * cols

    def stream(clip, half):
        return clip // per_half, half * per_half + clip % per_half

    def flat(t, s, b):
        return (t * segments + s) * bands + b

    half = band // per_half
    holds = time < clips // per_half
    place = jnp.stack([position, half, holds.astype(jnp.int32)]).astype(jnp.int32)
    weight = conv_weight[0].reshape(3, 3, 3 * channels, channels)
    weight = resident(weight)
    bias = resident(conv_bias)
    gain = resident(norm_gain)

    mine = lax.dynamic_index_in_dim(features, position, 0, keepdims=False)
    mine = mine.reshape(own_frames, piece, channels)
    entries = []
    for t in range(times):
        group = []
        for number in range(pieces):
            pairs = []
            for clip in range(clips):
                for h in range(HALVES):
                    source = h * (bands - pieces) + number
                    there, at = stream(clip, h)
                    pairs.append((flat(t, clip, source), flat(there, 0, at)))
            group.append(lax.ppermute(mine, MESH_AXES, pairs))
        entries.append(group)

    near = jnp.zeros((size, channels), jnp.float32)
    far = jnp.zeros((size, channels), jnp.float32)
    slots = frames + LAG * (segments - 1)
    moving = {}
    tails = None
    landed = []
    small = 24 << 20
    frame_bytes = size * channels
    frame_cost = pl.CostEstimate(
        flops=2 * size * channels * 9 * channels, transcendentals=size * channels, bytes_accessed=12 * frame_bytes
    )
    past_cost = pl.CostEstimate(
        flops=2 * size * channels * 18 * channels, transcendentals=0, bytes_accessed=12 * frame_bytes
    )
    for slot in range(slots):
        given = []
        if slot < frames:
            given = [resident(value[slot % own_frames]) for value in entries[slot // own_frames]]
        came = [resident(moving.pop(slot - LAG))] if slot >= LAG else []
        last = slot - LAG * (segments - 1)
        finals = per_half if last >= 0 else 0
        half_pos = last % own_frames if last >= 0 else 0
        operands = [place, *given, *came, resident(near), weight, bias, gain]
        aliases = {}
        if finals and half_pos:
            for index, value in enumerate(tails):
                aliases[len(operands)] = 2 + index
                operands.append(resident(value))
        results = pl.pallas_call(
            functools.partial(frame_kernel, slot, frames, len(given), len(came), finals, half_pos, cols),
            out_shape=[
                pltpu.VMEM((size, channels), jnp.bfloat16),
                pltpu.VMEM((size + 2 * cols, 3 * channels), jnp.bfloat16),
            ]
            + [pltpu.VMEM((own_frames, piece, channels), jnp.bfloat16)] * finals,
            in_specs=[whole(pltpu.SMEM)] + [whole()] * (len(operands) - 1),
            out_specs=[whole()] * (2 + finals),
            scratch_shapes=[pltpu.VMEM((size, channels), jnp.bfloat16)],
            input_output_aliases=aliases,
            compiler_params=pltpu.CompilerParams(vmem_limit_bytes=small),
            cost_estimate=frame_cost,
            name="frame",
        )(*operands)
        out, spread = results[:2]
        tails = results[2:]
        pairs = [
            (s, s + 1) for s in range(segments - 1) if 0 <= slot - LAG * s < frames
        ]
        if pairs:
            moving[slot] = lax.ppermute(out, "segment", pairs)
        if finals and half_pos == own_frames - 1:
            there = last // own_frames
            for index in range(per_half):
                pairs = []
                for clip in range(clips):
                    for h in range(HALVES):
                        t, b = stream(clip, h)
                        pairs.append((flat(t, segments - 1, b), flat(there, clip, h * per_half + index)))
                landed.append((there, index, lax.ppermute(tails[index], MESH_AXES, pairs)))
        if slot + 1 < slots:
            near, far = pl.pallas_call(
                functools.partial(history_kernel, slot, frames, cols),
                out_shape=[pltpu.VMEM((size, channels), jnp.float32)] * 2,
                in_specs=[whole(pltpu.SMEM)] + [whole()] * 4,
                out_specs=[whole()] * 2,
                input_output_aliases={2: 0, 3: 1},
                compiler_params=pltpu.CompilerParams(vmem_limit_bytes=small),
                cost_estimate=past_cost,
                name="history",
            )(place, resident(spread), resident(near), resident(far), weight)

    result = landed[0][2]
    for there, index, value in landed[1:]:
        here = jnp.logical_and(time == there, band % per_half == index)
        result = jnp.where(here, value, result)
    return result.reshape(1, own_frames, own_rows, cols, channels)


def solution(mesh):
    return jax.shard_map(
        local,
        mesh=mesh,
        in_specs=(
            P(None, "tm", "band", None, None),
            P("segment", None, None, None),
            P("segment", None),
            P("segment", None),
        ),
        out_specs=P("segment", "tm", "band", None, None),
        check_vma=False,
    )
```

```python
import functools

import jax
import jax.numpy as jnp
from jax import lax
from jax.experimental import pallas as pl
from jax.experimental.pallas import tpu as pltpu
from jax.sharding import PartitionSpec as P

HALVES = 2
LAG = 2
VMEM = pltpu.VMEM
MESH_AXES = ("tm", "segment", "band")


def whole(space=VMEM):
    return pl.BlockSpec(memory_space=space)


def resident(value):
    return pltpu.with_memory_space_constraint(value, pltpu.VMEM)


def is_active(slot, frames, holders):
    number = slot - LAG * lax.axis_index("segment")
    here = jnp.logical_and(number >= 0, number < frames)
    if holders < lax.axis_size("tm"):
        here = jnp.logical_and(here, lax.axis_index("tm") < holders)
    return here


def loader_kernel(*refs):
    count = len(refs) // 2
    sources, targets, sems = refs[:count], refs[count : 2 * count], refs[-1]
    copies = [
        pltpu.make_async_copy(source, target, sems.at[number])
        for number, (source, target) in enumerate(zip(sources, targets))
    ]
    for copy in copies:
        copy.start()
    for copy in copies:
        copy.wait()


def frame_kernel(slot, frames, holders, has_pieces, has_received, finals, half_pos, keep, cols, *refs):
    refs = list(refs)
    leading = lax.axis_index("segment") == 0
    pieces = [refs.pop(0) for _ in range(has_pieces)]
    received = refs.pop(0) if has_received else None
    partial, weight, bias, gain = refs[:4]
    refs = refs[4:]
    if finals and half_pos:
        refs = refs[finals:]
    out = refs.pop(0) if keep[0] else None
    spread = refs.pop(0) if keep[1] else None
    tails = [refs.pop(0) for _ in range(finals)]
    entry = refs.pop(0)
    out = refs.pop(0) if out is None else out
    spread = refs.pop(0) if spread is None else spread
    size, channels = out.shape

    @pl.when(is_active(slot, frames, holders))
    def _():
        if has_pieces:
            step = size // has_pieces

            @pl.when(leading)
            def _():
                for number, piece in enumerate(pieces):
                    entry[pl.ds(number * step, step), :] = piece[...]

        if has_received:

            @pl.when(jnp.logical_not(leading))
            def _():
                entry[...] = received[...]

        wide = entry[...].astype(jnp.float32)
        meansq = jnp.sum(wide * wide, axis=-1, keepdims=True) * (1.0 / channels)
        normed = wide * lax.rsqrt(meansq + 1e-06) * gain[...]
        ready = normed / (1.0 + jnp.exp(-normed))
        column = lax.broadcasted_iota(jnp.int32, ready.shape, 0) & (cols - 1)
        before = jnp.where(column == 0, 0.0, pltpu.roll(ready, 1, 0))
        after = jnp.where(column == cols - 1, 0.0, pltpu.roll(ready, size - 1, 0))
        edge = jnp.zeros((cols, 3 * channels), jnp.bfloat16)
        spread[pl.ds(0, cols), :] = edge
        spread[pl.ds(size + cols, cols), :] = edge
        for number, value in enumerate((before, ready, after)):
            spread[pl.ds(cols, size), pl.ds(number * channels, channels)] = value.astype(jnp.bfloat16)
        total = partial[...] + wide + bias[...]
        for row in range(3):
            total += jnp.dot(
                spread[pl.ds(row * cols, size), :], weight[2, row], preferred_element_type=jnp.float32
            )
        out[...] = total.astype(jnp.bfloat16)
        if finals:
            length = tails[0].shape[1]
            half = lax.axis_index("band") // finals
            for number, tail in enumerate(tails):
                start = pl.multiple_of((half + number) * length, length)
                tail[half_pos] = out[pl.ds(start, length), :]


def history_kernel(slot, frames, holders, cols, spread, near, far, weight, near_out, far_out):
    size = near.shape[0]

    @pl.when(is_active(slot, frames - 1, holders))
    def _():
        total = far[...]
        later = jnp.zeros(far.shape, jnp.float32)
        for row in range(3):
            ready = spread[pl.ds(row * cols, size), :]
            total += jnp.dot(ready, weight[1, row], preferred_element_type=jnp.float32)
            later += jnp.dot(ready, weight[0, row], preferred_element_type=jnp.float32)
        near_out[...] = total
        far_out[...] = later


def local(features, conv_weight, conv_bias, norm_gain):
    times, segments, bands = (lax.axis_size(name) for name in MESH_AXES)
    time, position, band = (lax.axis_index(name) for name in MESH_AXES)
    clips, own_frames, own_rows, cols, channels = features.shape
    frames = own_frames * times
    rows = own_rows * bands
    per_half = bands // HALVES
    half_rows = rows // HALVES
    window = half_rows + segments
    pieces = window // own_rows
    assert clips == segments and window % own_rows == 0 and pieces - per_half == bands - pieces
    assert clips % per_half == 0 and clips // per_half <= times
    size = window * cols
    piece = own_rows * cols

    def stream(clip, half):
        return clip // per_half, half * per_half + clip % per_half

    def flat(t, s, b):
        return (t * segments + s) * bands + b

    holders = clips // per_half
    stored = [conv_weight[0].reshape(3, 3, 3 * channels, channels), conv_bias, norm_gain]
    weight, bias, gain = pl.pallas_call(
        loader_kernel,
        out_shape=[pltpu.VMEM(value.shape, value.dtype) for value in stored],
        in_specs=[whole(pltpu.HBM)] * 3,
        out_specs=[whole()] * 3,
        scratch_shapes=[pltpu.SemaphoreType.DMA((3,))],
        compiler_params=pltpu.CompilerParams(vmem_limit_bytes=1 << 20),
        cost_estimate=pl.CostEstimate(flops=0, transcendentals=0, bytes_accessed=2 * stored[0].size),
        name="loader",
    )(*[pltpu.with_memory_space_constraint(value, pltpu.HBM) for value in stored])
    weight, bias, gain = resident(weight), resident(bias), resident(gain)

    mine = lax.dynamic_index_in_dim(features, position, 0, keepdims=False)
    mine = mine.reshape(own_frames, piece, channels)
    entries = []
    for t in range(times):
        group = []
        for number in range(pieces):
            pairs = []
            for clip in range(clips):
                for h in range(HALVES):
                    source = h * (bands - pieces) + number
                    there, at = stream(clip, h)
                    pairs.append((flat(t, clip, source), flat(there, 0, at)))
            group.append(lax.ppermute(mine, MESH_AXES, pairs))
        entries.append(group)

    near = jnp.zeros((size, channels), jnp.float32)
    far = jnp.zeros((size, channels), jnp.float32)
    slots = frames + LAG * (segments - 1)
    moving = {}
    tails = None
    landed = []
    small = 24 << 20
    frame_bytes = size * channels
    frame_cost = pl.CostEstimate(
        flops=2 * size * channels * 9 * channels, transcendentals=size * channels, bytes_accessed=12 * frame_bytes
    )
    past_cost = pl.CostEstimate(
        flops=2 * size * channels * 18 * channels, transcendentals=0, bytes_accessed=12 * frame_bytes
    )
    for slot in range(slots):
        given = []
        if slot < frames:
            given = [resident(value[slot % own_frames]) for value in entries[slot // own_frames]]
        came = [resident(moving.pop(slot - LAG))] if slot >= LAG else []
        last = slot - LAG * (segments - 1)
        finals = per_half if last >= 0 else 0
        half_pos = last % own_frames if last >= 0 else 0
        operands = [*given, *came, resident(near), weight, bias, gain]
        aliases = {}
        if finals and half_pos:
            for index, value in enumerate(tails):
                aliases[len(operands)] = index
                operands.append(resident(value))
        pairs = [(s, s + 1) for s in range(segments - 1) if 0 <= slot - LAG * s < frames]
        keep = (bool(pairs), slot + 1 < slots)
        shapes = [((size, channels), jnp.bfloat16), ((size + 2 * cols, 3 * channels), jnp.bfloat16)]
        kept = [pltpu.VMEM(*shape) for shape, wanted in zip(shapes, keep) if wanted]
        spare = [pltpu.VMEM(*shape) for shape, wanted in zip(shapes, keep) if not wanted]
        if finals and half_pos:
            aliases = {index: len(kept) + value for index, value in aliases.items()}
        results = pl.pallas_call(
            functools.partial(
                frame_kernel, slot, frames, holders, len(given), len(came), finals, half_pos, keep, cols
            ),
            out_shape=kept + [pltpu.VMEM((own_frames, piece, channels), jnp.bfloat16)] * finals,
            in_specs=[whole()] * len(operands),
            out_specs=[whole()] * (len(kept) + finals),
            scratch_shapes=[pltpu.VMEM((size, channels), jnp.bfloat16)] + spare,
            input_output_aliases=aliases,
            compiler_params=pltpu.CompilerParams(vmem_limit_bytes=small),
            cost_estimate=frame_cost,
            name="frame",
        )(*operands)
        results = list(results)
        out = results.pop(0) if keep[0] else None
        spread = results.pop(0) if keep[1] else None
        tails = results
        if pairs:
            moving[slot] = lax.ppermute(out, "segment", pairs)
        if finals and half_pos == own_frames - 1:
            there = last // own_frames
            for index in range(per_half):
                pairs = []
                for clip in range(clips):
                    for h in range(HALVES):
                        t, b = stream(clip, h)
                        pairs.append((flat(t, segments - 1, b), flat(there, clip, h * per_half + index)))
                landed.append((there, index, lax.ppermute(tails[index], MESH_AXES, pairs)))
        if slot + 1 < slots:
            near, far = pl.pallas_call(
                functools.partial(history_kernel, slot, frames, holders, cols),
                out_shape=[pltpu.VMEM((size, channels), jnp.float32)] * 2,
                in_specs=[whole()] * 4,
                out_specs=[whole()] * 2,
                input_output_aliases={1: 0, 2: 1},
                compiler_params=pltpu.CompilerParams(vmem_limit_bytes=small),
                cost_estimate=past_cost,
                name="history",
            )(resident(spread), resident(near), resident(far), weight)

    result = landed[0][2]
    for there, index, value in landed[1:]:
        here = jnp.logical_and(time == there, band % per_half == index)
        result = jnp.where(here, value, result)
    return result.reshape(1, own_frames, own_rows, cols, channels)


def solution(mesh):
    return jax.shard_map(
        local,
        mesh=mesh,
        in_specs=(
            P(None, "tm", "band", None, None),
            P("segment", None, None, None),
            P("segment", None),
            P("segment", None),
        ),
        out_specs=P("segment", "tm", "band", None, None),
        check_vma=False,
    )
```

```python
import functools

import jax
import jax.numpy as jnp
from jax import lax
from jax.experimental import pallas as pl
from jax.experimental.pallas import tpu as pltpu
from jax.sharding import PartitionSpec as P

HALVES = 2
LAG = 2
TAPS = 3
VMEM_LIMIT = 24 << 20
MESH_AXES = ("tm", "segment", "band")


def whole(space=pltpu.VMEM):
    return pl.BlockSpec(memory_space=space)


def resident(value):
    return pltpu.with_memory_space_constraint(value, pltpu.VMEM)


def working(slot, frames, segments):
    return [s for s in range(segments) if 0 <= slot - LAG * s < frames]


def on_unit(unit, holders):
    here = lax.axis_index("segment") == unit
    if holders < lax.axis_size("tm"):
        here = jnp.logical_and(here, lax.axis_index("tm") < holders)
    return here


def rows_at(start, count, cols):
    return pl.ds(pl.multiple_of(start * cols, cols), count * cols)


def loader_kernel(weight, bias, gain, now, past, bias_out, gain_out, sems):
    channels = weight.shape[-1]
    copies = [(bias, bias_out), (gain, gain_out), (weight.at[2], now)]
    for row in range(TAPS):
        for age in range(2):
            copies.append((weight.at[age, row], past.at[row, :, pl.ds(age * channels, channels)]))
    copies = [
        pltpu.make_async_copy(source, target, sems.at[number])
        for number, (source, target) in enumerate(copies)
    ]
    for copy in copies:
        copy.start()
    for copy in copies:
        copy.wait()


def frame_kernel(cfg, *refs):
    refs = list(refs)
    pieces = [refs.pop(0) for _ in cfg["places"]]
    received = refs.pop(0) if cfg["came"] is not None else None
    partial, weight, bias, gain = refs[:4]
    refs = refs[4:]
    if cfg["joins"]:
        refs = refs[cfg["finals"] :]
    out = refs.pop(0) if cfg["sends"] else None
    spread = refs.pop(0)
    tails = [refs.pop(0) for _ in range(cfg["finals"])]
    entry = refs.pop(0)
    cols, window, segments = cfg["cols"], cfg["window"], cfg["segments"]
    channels = entry.shape[-1]
    half = lax.axis_index("band") // cfg["per_half"]

    def run(unit):
        have = window - unit
        need = have - 1
        size = have * cols
        if unit == 0:
            step = entry.shape[0] // len(pieces)
            spot = lax.axis_index("tm") * cfg["bands"] + lax.axis_index("band")
            for piece, code in zip(pieces, cfg["places"]):
                number = (code >> (2 * spot)) & 3
                entry[pl.ds(pl.multiple_of(number * step, step), step), :] = piece[...]
            source, skip = entry, 0
        else:
            source, skip = received, half * (unit - 1 - cfg["came"])
        wide = source[rows_at(skip, have, cols), :].astype(jnp.float32)
        meansq = jnp.sum(wide * wide, axis=-1, keepdims=True) * (1.0 / channels)
        normed = wide * lax.rsqrt(meansq + 1e-06) * gain[...]
        ready = normed / (1.0 + jnp.exp(-normed))
        column = lax.broadcasted_iota(jnp.int32, ready.shape, 0) & (cols - 1)
        before = jnp.where(column == 0, 0.0, pltpu.roll(ready, 1, 0))
        after = jnp.where(column == cols - 1, 0.0, pltpu.roll(ready, size - 1, 0))
        edge = jnp.zeros((cols, TAPS * channels), jnp.bfloat16)
        spread[pl.ds(0, cols), :] = edge
        spread[pl.ds(size + cols, cols), :] = edge
        for number, value in enumerate((before, ready, after)):
            spread[pl.ds(cols, size), pl.ds(number * channels, channels)] = value.astype(jnp.bfloat16)
        kept = source[rows_at(skip + half, need, cols), :].astype(jnp.float32)
        total = partial[pl.ds(0, need * cols), :] + kept + bias[...]
        for row in range(TAPS):
            total += jnp.dot(
                spread[rows_at(half + row, need, cols), :], weight[row], preferred_element_type=jnp.float32
            )
        value = total.astype(jnp.bfloat16)
        if unit < segments - 1:
            out[rows_at(half * (unit - cfg["lowest"]), need, cols), :] = value
        else:
            length = value.shape[0] // len(tails)
            for number, tail in enumerate(tails):
                tail[cfg["tail_at"]] = value[number * length : (number + 1) * length]

    for unit in cfg["units"]:
        pl.when(on_unit(unit, cfg["holders"]))(functools.partial(run, unit))


def history_kernel(cfg, spread, near, far, weight, near_out, far_out):
    cols, window = cfg["cols"], cfg["window"]
    channels = near.shape[-1]
    half = lax.axis_index("band") // cfg["per_half"]

    def run(unit):
        need = window - unit - 1
        here = pl.ds(0, need * cols)
        total = jnp.zeros((need * cols, 2 * channels), jnp.float32)
        for row in range(TAPS):
            total += jnp.dot(
                spread[rows_at(half + row, need, cols), :], weight[row], preferred_element_type=jnp.float32
            )
        near_out[here, :] = far[here, :] + total[:, channels:]
        far_out[here, :] = total[:, :channels]

    for unit in cfg["later"]:
        pl.when(on_unit(unit, cfg["holders"]))(functools.partial(run, unit))


def entry_plan(times, segments, bands, clips, per_half):
    holders = clips // per_half

    def spot(t, s, b):
        return (t * segments + s) * bands + b

    pairs, places, clip_of = [], [], {}
    for t in range(times):
        near = t if t < holders else 0
        group = [[] for _ in range(TAPS)]
        codes = [0] * TAPS
        for x in range(holders):
            for h in range(HALVES):
                edge, inner, third = (0, 1, 2) if h == 0 else (3, 2, 1)
                for j in range(per_half):
                    own = 2 * h + j
                    other = 2 * h + 1 - j
                    if x == near:
                        steps = [(own, 0), (other, 0), (third, j)]
                    elif j == 0:
                        steps = [(third, 1), (inner, 1), (edge, 0)]
                    else:
                        steps = [(inner, 2), (edge, 1), (third, 2)]
                    there = h * per_half + j
                    for number, (source, segment) in enumerate(steps):
                        group[number].append((spot(t, segment, source), spot(x, 0, there)))
                        codes[number] |= (source - h) << (2 * (x * bands + there))
                        key = (near, number, segment, source)
                        assert clip_of.setdefault(key, x * per_half + j) == x * per_half + j
        for members in group:
            assert len({a for a, _ in members}) == len({b for _, b in members}) == len(members)
        pairs.append(group)
        places.append(codes)
    senders = [[0] * TAPS for _ in range(holders)]
    for (near, number, segment, source), clip in clip_of.items():
        senders[near][number] |= clip << (2 * (segment * bands + source))
    return pairs, places, senders


def local(features, conv_weight, conv_bias, norm_gain):
    times, segments, bands = (lax.axis_size(name) for name in MESH_AXES)
    time, position, band = (lax.axis_index(name) for name in MESH_AXES)
    clips, own_frames, own_rows, cols, channels = features.shape
    frames = own_frames * times
    per_half = bands // HALVES
    window = own_rows * bands // HALVES + segments
    holders = clips // per_half
    piece = own_rows * cols
    assert clips == segments == bands == 4 and holders == 2 <= times and window == TAPS * own_rows

    def stream(clip, half):
        return clip // per_half, half * per_half + clip % per_half

    def spot(t, s, b):
        return (t * segments + s) * bands + b

    pairs, places, senders = entry_plan(times, segments, bands, clips, per_half)
    sender = 2 * (position * bands + band)
    rounds = []
    for number in range(TAPS):
        first, second = (jnp.uint32(senders[near][number]) for near in range(holders))
        code = jnp.where(time == 1, second, first)
        clip = ((code >> sender.astype(jnp.uint32)) & 3).astype(jnp.int32)
        value = lax.dynamic_index_in_dim(features, clip, 0, keepdims=False)
        rounds.append(value.reshape(own_frames, piece, channels))
    entries = [
        [lax.ppermute(rounds[number], MESH_AXES, pairs[t][number]) for number in range(TAPS)]
        for t in range(times)
    ]

    stored = [conv_weight[0].reshape(TAPS, TAPS, TAPS * channels, channels), conv_bias, norm_gain]
    now, past, bias, gain = pl.pallas_call(
        loader_kernel,
        out_shape=[
            pltpu.VMEM((TAPS, TAPS * channels, channels), stored[0].dtype),
            pltpu.VMEM((TAPS, TAPS * channels, 2 * channels), stored[0].dtype),
            pltpu.VMEM(conv_bias.shape, conv_bias.dtype),
            pltpu.VMEM(norm_gain.shape, norm_gain.dtype),
        ],
        in_specs=[whole(pltpu.HBM)] * 3,
        out_specs=[whole()] * 4,
        scratch_shapes=[pltpu.SemaphoreType.DMA((9,))],
        compiler_params=pltpu.CompilerParams(vmem_limit_bytes=1 << 20),
        cost_estimate=pl.CostEstimate(flops=0, transcendentals=0, bytes_accessed=2 * stored[0].size),
        name="loader",
    )(*[pltpu.with_memory_space_constraint(value, pltpu.HBM) for value in stored])
    now, past, bias, gain = (resident(value) for value in (now, past, bias, gain))

    state = ((window - 1) * cols, channels)
    near = jnp.zeros(state, jnp.float32)
    far = jnp.zeros(state, jnp.float32)
    slots = frames + LAG * (segments - 1)
    moving = {}
    tails = []
    landed = []
    for slot in range(slots):
        units = working(slot, frames, segments)
        senders_now = [s for s in units if s < segments - 1]
        last = slot - LAG * (segments - 1)
        finals = per_half if last >= 0 else 0
        alone = last // own_frames == times - 1
        cfg = dict(
            units=units,
            later=[s for s in units if slot - LAG * s < frames - 1],
            sends=bool(senders_now),
            lowest=min(senders_now, default=0),
            places=places[slot // own_frames] if slot < frames else [],
            came=min(working(slot - LAG, frames, segments)) if slot >= LAG else None,
            finals=finals,
            tail_at=0 if alone else last % own_frames,
            joins=finals and not alone and last % own_frames > 0,
            cols=cols,
            window=window,
            segments=segments,
            bands=bands,
            per_half=per_half,
            holders=holders,
        )
        operands = []
        if slot < frames:
            operands += [resident(value[slot % own_frames]) for value in entries[slot // own_frames]]
        if slot >= LAG:
            operands.append(resident(moving.pop(slot - LAG)))
        operands += [resident(near), now, bias, gain]
        shapes = []
        if cfg["sends"]:
            shapes.append(pltpu.VMEM(((window - 1 - cfg["lowest"]) * cols, channels), jnp.bfloat16))
        shapes.append(pltpu.VMEM(((window + 2) * cols, TAPS * channels), jnp.bfloat16))
        aliases = {}
        if cfg["joins"]:
            for index, value in enumerate(tails):
                aliases[len(operands)] = len(shapes) + index
                operands.append(resident(value))
        shapes += [pltpu.VMEM((1 if alone else own_frames, piece, channels), jnp.bfloat16)] * finals
        results = list(
            pl.pallas_call(
                functools.partial(frame_kernel, cfg),
                out_shape=shapes,
                in_specs=[whole()] * len(operands),
                out_specs=[whole()] * len(shapes),
                scratch_shapes=[pltpu.VMEM((window * cols, channels), jnp.bfloat16)],
                input_output_aliases=aliases,
                compiler_params=pltpu.CompilerParams(vmem_limit_bytes=VMEM_LIMIT),
                cost_estimate=pl.CostEstimate(
                    flops=2 * state[0] * 9 * channels * channels,
                    transcendentals=state[0] * channels,
                    bytes_accessed=12 * state[0] * channels,
                ),
                name="frame",
            )(*operands)
        )
        out = results.pop(0) if cfg["sends"] else None
        spread = results.pop(0)
        tails = results
        if cfg["sends"]:
            moving[slot] = lax.ppermute(out, "segment", [(s, s + 1) for s in senders_now])
        if finals and (alone or last % own_frames == own_frames - 1):
            there = last // own_frames
            for index in range(per_half):
                routes = []
                for clip in range(clips):
                    for h in range(HALVES):
                        t, b = stream(clip, h)
                        routes.append((spot(t, segments - 1, b), spot(there, clip, h * per_half + index)))
                landed.append((there, index, lax.ppermute(tails[index], MESH_AXES, routes)))
        if cfg["later"]:
            near, far = pl.pallas_call(
                functools.partial(history_kernel, cfg),
                out_shape=[pltpu.VMEM(state, jnp.float32)] * 2,
                in_specs=[whole()] * 4,
                out_specs=[whole()] * 2,
                input_output_aliases={1: 0, 2: 1},
                compiler_params=pltpu.CompilerParams(vmem_limit_bytes=VMEM_LIMIT),
                cost_estimate=pl.CostEstimate(
                    flops=2 * state[0] * 18 * channels * channels,
                    transcendentals=0,
                    bytes_accessed=12 * state[0] * channels,
                ),
                name="history",
            )(resident(spread), resident(near), resident(far), past)

    result = None
    for t in range(times):
        for index in range(per_half):
            parts = [value for there, number, value in landed if (there, number) == (t, index)]
            value = parts[0] if len(parts) == 1 else jnp.concatenate(parts, axis=0)
            here = jnp.logical_and(time == t, band % per_half == index)
            result = value if result is None else jnp.where(here, value, result)
    return result.reshape(1, own_frames, own_rows, cols, channels)


def solution(mesh):
    return jax.shard_map(
        local,
        mesh=mesh,
        in_specs=(
            P(None, "tm", "band", None, None),
            P("segment", None, None, None),
            P("segment", None),
            P("segment", None),
        ),
        out_specs=P("segment", "tm", "band", None, None),
        check_vma=False,
    )
```

```python
import functools

import jax
import jax.numpy as jnp
from jax import lax
from jax.experimental import pallas as pl
from jax.experimental.pallas import tpu as pltpu
from jax.sharding import PartitionSpec as P

HALVES = 2
DEPTH = 4
TAPS = 3
VMEM_LIMIT = 24 << 20
MESH_AXES = ("tm", "segment", "band")


def whole(space=pltpu.VMEM):
    return pl.BlockSpec(memory_space=space)


def resident(value):
    return pltpu.with_memory_space_constraint(value, pltpu.VMEM)


def working(slot, frames, segments, lag):
    return [s for s in range(segments) if 0 <= slot - lag * s < frames]


def on_unit(unit, holders):
    here = lax.axis_index("segment") == unit
    if holders < lax.axis_size("tm"):
        here = jnp.logical_and(here, lax.axis_index("tm") < holders)
    return here


def rows_at(start, count, cols):
    return pl.ds(pl.multiple_of(start * cols, cols), count * cols)


def pick_kernel(source, target, sem):
    copy = pltpu.make_async_copy(source.at[lax.axis_index("segment")], target, sem)
    copy.start()
    copy.wait()


def loader_kernel(weight, bias, gain, now, past, bias_out, gain_out, sems):
    channels = weight.shape[-1]
    copies = [(bias, bias_out), (gain, gain_out), (weight.at[2], now)]
    for row in range(TAPS):
        for age in range(2):
            copies.append((weight.at[age, row], past.at[row, :, pl.ds(age * channels, channels)]))
    copies = [
        pltpu.make_async_copy(source, target, sems.at[number])
        for number, (source, target) in enumerate(copies)
    ]
    for copy in copies:
        copy.start()
    for copy in copies:
        copy.wait()


def frame_kernel(cfg, *refs):
    refs = list(refs)
    pieces = [refs.pop(0) for _ in range(cfg["pieces"])]
    received = refs.pop(0) if cfg["came"] is not None else None
    partial, weight, bias, gain = refs[:4]
    refs = refs[4:]
    refs = refs[cfg["passing"] :]
    out = refs.pop(0) if cfg["sends"] else None
    spread = refs.pop(0) if cfg["later"] else refs.pop()
    tails = [refs.pop(0) for _ in range(cfg["finals"])]
    entry = refs.pop()
    cols, window, segments = cfg["cols"], cfg["window"], cfg["segments"]
    channels = entry.shape[-1]
    half = lax.axis_index("band") // cfg["per_half"]

    def run(unit):
        have = window - unit
        need = have - 1
        size = have * cols
        if unit == 0:
            step = entry.shape[0] // TAPS
            for number, piece in enumerate(pieces):
                entry[pl.ds(number * step, step), :] = piece[cfg["piece_at"]]
            source, skip = entry, 0
        else:
            source, skip = received, half * (unit - 1 - cfg["came"])
        wide = source[rows_at(skip, have, cols), :].astype(jnp.float32)
        meansq = jnp.sum(wide * wide, axis=-1, keepdims=True) * (1.0 / channels)
        normed = wide * lax.rsqrt(meansq + 1e-06) * gain[...]
        ready = normed / (1.0 + jnp.exp(-normed))
        column = lax.broadcasted_iota(jnp.int32, ready.shape, 0) & (cols - 1)
        before = jnp.where(column == 0, 0.0, pltpu.roll(ready, 1, 0))
        after = jnp.where(column == cols - 1, 0.0, pltpu.roll(ready, size - 1, 0))
        edge = jnp.zeros((cols, TAPS * channels), jnp.bfloat16)
        spread[pl.ds(0, cols), :] = edge
        spread[pl.ds(size + cols, cols), :] = edge
        for number, value in enumerate((before, ready, after)):
            spread[pl.ds(cols, size), pl.ds(number * channels, channels)] = value.astype(jnp.bfloat16)
        kept = source[rows_at(skip + half, need, cols), :].astype(jnp.float32)
        total = partial[pl.ds(0, need * cols), :] + kept + bias[...]
        for row in range(TAPS):
            total += jnp.dot(
                spread[rows_at(half + row, need, cols), :], weight[row], preferred_element_type=jnp.float32
            )
        value = total.astype(jnp.bfloat16)
        if unit < segments - 1:
            out[rows_at(half * (unit - cfg["lowest"]), need, cols), :] = value
        else:
            length = value.shape[0] // len(tails)
            for number, tail in enumerate(tails):
                tail[cfg["tail_at"]] = value[number * length : (number + 1) * length]

    for unit in cfg["units"]:
        pl.when(on_unit(unit, cfg["holders"]))(functools.partial(run, unit))


def history_kernel(cfg, spread, near, far, weight, near_out, far_out):
    cols, window = cfg["cols"], cfg["window"]
    channels = near.shape[-1]
    half = lax.axis_index("band") // cfg["per_half"]

    def run(unit):
        need = window - unit - 1
        here = pl.ds(0, need * cols)
        total = jnp.zeros((need * cols, 2 * channels), jnp.float32)
        for row in range(TAPS):
            total += jnp.dot(
                spread[rows_at(half + row, need, cols), :], weight[row], preferred_element_type=jnp.float32
            )
        near_out[here, :] = far[here, :] + total[:, channels:]
        far_out[here, :] = total[:, :channels]

    for unit in cfg["later"]:
        pl.when(on_unit(unit, cfg["holders"]))(functools.partial(run, unit))


def local(features, conv_weight, conv_bias, norm_gain):
    times, segments, bands = (lax.axis_size(name) for name in MESH_AXES)
    time, position, band = (lax.axis_index(name) for name in MESH_AXES)
    clips, own_frames, own_rows, cols, channels = features.shape
    frames = own_frames * times
    per_half = bands // HALVES
    window = own_rows * bands // HALVES + segments
    holders = clips // per_half
    piece = own_rows * cols
    assert clips == segments == bands == 4 and holders == 2 <= times and window == TAPS * own_rows

    def stream(clip, half):
        return clip // per_half, half * per_half + clip % per_half

    def spot(t, s, b):
        return (t * segments + s) * bands + b

    mine = pl.pallas_call(
        pick_kernel,
        out_shape=pltpu.VMEM((own_frames, piece, channels), features.dtype),
        in_specs=[whole(pltpu.HBM)],
        out_specs=whole(),
        scratch_shapes=[pltpu.SemaphoreType.DMA],
        compiler_params=pltpu.CompilerParams(vmem_limit_bytes=1 << 20),
        name="pick",
    )(pltpu.with_memory_space_constraint(features.reshape(clips, own_frames, piece, channels), pltpu.HBM))
    entries = []
    for t in range(times):
        group = []
        for number in range(TAPS):
            routes = []
            for clip in range(clips):
                for h in range(HALVES):
                    there, at = stream(clip, h)
                    routes.append((spot(t, clip, h + number), spot(there, 0, at)))
            group.append(lax.ppermute(mine, MESH_AXES, routes))
        entries.append(group)

    stored = [conv_weight[0].reshape(TAPS, TAPS, TAPS * channels, channels), conv_bias, norm_gain]
    now, past, bias, gain = pl.pallas_call(
        loader_kernel,
        out_shape=[
            pltpu.VMEM((TAPS, TAPS * channels, channels), stored[0].dtype),
            pltpu.VMEM((TAPS, TAPS * channels, 2 * channels), stored[0].dtype),
            pltpu.VMEM(conv_bias.shape, conv_bias.dtype),
            pltpu.VMEM(norm_gain.shape, norm_gain.dtype),
        ],
        in_specs=[whole(pltpu.HBM)] * 3,
        out_specs=[whole()] * 4,
        scratch_shapes=[pltpu.SemaphoreType.DMA((9,))],
        compiler_params=pltpu.CompilerParams(vmem_limit_bytes=1 << 20),
        name="loader",
    )(*[pltpu.with_memory_space_constraint(value, pltpu.HBM) for value in stored])
    now, past, bias, gain = (resident(value) for value in (now, past, bias, gain))

    state = ((window - 1) * cols, channels)
    near = jnp.zeros(state, jnp.float32)
    far = jnp.zeros(state, jnp.float32)
    lag = min(frames, DEPTH)
    slots = frames + lag * (segments - 1)
    moving = {}
    tails = []
    held = []
    landed = {}
    for slot in range(slots):
        units = working(slot, frames, segments, lag)
        senders_now = [s for s in units if s < segments - 1]
        last = slot - lag * (segments - 1)
        finals = per_half if last >= 0 else 0
        middle = finals and last % own_frames > 0
        cfg = dict(
            units=units,
            later=[s for s in units if slot - lag * s < frames - 1],
            sends=bool(senders_now),
            lowest=min(senders_now, default=0),
            pieces=TAPS if slot < frames else 0,
            piece_at=slot % own_frames,
            came=min(working(slot - lag, frames, segments, lag)) if slot >= lag else None,
            finals=finals,
            tail_at=last % own_frames,
            passing=(finals if middle else 0) + (len(landed) if slot + 1 == slots else len(held)),
            cols=cols,
            window=window,
            segments=segments,
                        per_half=per_half,
            holders=holders,
        )
        operands = []
        if slot < frames:
            operands += [resident(value) for value in entries[slot // own_frames]]
        if slot >= lag:
            operands.append(resident(moving.pop(slot - lag)))
        operands += [resident(near), now, bias, gain]
        shapes = []
        if cfg["sends"]:
            shapes.append(pltpu.VMEM(((window - 1 - cfg["lowest"]) * cols, channels), jnp.bfloat16))
        wide = pltpu.VMEM(((window + 2) * cols, TAPS * channels), jnp.bfloat16)
        if cfg["later"]:
            shapes.append(wide)
        shape = pltpu.VMEM((own_frames, piece, channels), jnp.bfloat16)
        aliases = {}
        if middle:
            for index, value in enumerate(tails):
                aliases[len(operands)] = len(shapes) + index
                operands.append(resident(value))
        shapes += [shape] * finals
        if slot + 1 == slots:
            held = [(*key, value) for key, value in landed.items()]
        for _, _, value in held:
            aliases[len(operands)] = len(shapes)
            operands.append(resident(value))
            shapes.append(shape)
        results = list(
            pl.pallas_call(
                functools.partial(frame_kernel, cfg),
                out_shape=shapes,
                in_specs=[whole()] * len(operands),
                out_specs=[whole()] * len(shapes),
                scratch_shapes=[pltpu.VMEM((window * cols, channels), jnp.bfloat16)] + ([] if cfg["later"] else [wide]),
                input_output_aliases=aliases,
                compiler_params=pltpu.CompilerParams(vmem_limit_bytes=VMEM_LIMIT),
                cost_estimate=pl.CostEstimate(flops=0, transcendentals=0, bytes_accessed=1 << 10),
                name="frame",
            )(*operands)
        )
        out = results.pop(0) if cfg["sends"] else None
        spread = results.pop(0) if cfg["later"] else None
        tails = results[:finals]
        leaving = [(there, index, value) for (there, index, _), value in zip(held, results[finals:])]
        if slot + 1 == slots:
            landed.update({(there, index): value for there, index, value in leaving})
            leaving = []
        held = []
        if cfg["sends"]:
            moving[slot] = lax.ppermute(out, "segment", [(s, s + 1) for s in senders_now])
        if finals and last % own_frames == own_frames - 1:
            there = last // own_frames
            ready = [(there, index, value) for index, value in enumerate(tails)]
            if there == times - 1:
                leaving += ready
            else:
                leaving.append(ready[0])
                held = ready[1:]
        for there, index, value in leaving:
            routes = []
            for clip in range(clips):
                for h in range(HALVES):
                    t, b = stream(clip, h)
                    routes.append((spot(t, segments - 1, b), spot(there, clip, h * per_half + index)))
            landed[there, index] = lax.ppermute(value, MESH_AXES, routes)
        if cfg["later"]:
            near, far = pl.pallas_call(
                functools.partial(history_kernel, cfg),
                out_shape=[pltpu.VMEM(state, jnp.float32)] * 2,
                in_specs=[whole()] * 4,
                out_specs=[whole()] * 2,
                input_output_aliases={1: 0, 2: 1},
                compiler_params=pltpu.CompilerParams(vmem_limit_bytes=VMEM_LIMIT),
                cost_estimate=pl.CostEstimate(flops=0, transcendentals=0, bytes_accessed=1 << 10),
                name="history",
            )(resident(spread), resident(near), resident(far), past)

    result = None
    for (t, index), value in landed.items():
        here = jnp.logical_and(time == t, band % per_half == index)
        result = value if result is None else jnp.where(here, value, result)
    return result.reshape(1, own_frames, own_rows, cols, channels)


def solution(mesh):
    return jax.shard_map(
        local,
        mesh=mesh,
        in_specs=(
            P(None, "tm", "band", None, None),
            P("segment", None, None, None),
            P("segment", None),
            P("segment", None),
        ),
        out_specs=P("segment", "tm", "band", None, None),
        check_vma=False,
    )
```

```python
import functools

import jax
import jax.numpy as jnp
from jax import lax
from jax.experimental import pallas as pl
from jax.experimental.pallas import tpu as pltpu
from jax.sharding import PartitionSpec as P

HALVES = 2
DEPTH = 4
TAPS = 3
VMEM_LIMIT = 24 << 20
MESH_AXES = ("tm", "segment", "band")


def whole(space=pltpu.VMEM):
    return pl.BlockSpec(memory_space=space)


def resident(value):
    return pltpu.with_memory_space_constraint(value, pltpu.VMEM)


def working(slot, frames, segments, lag):
    return [s for s in range(segments) if 0 <= slot - lag * s < frames]


def on_unit(unit, holders):
    here = lax.axis_index("segment") == unit
    if holders < lax.axis_size("tm"):
        here = jnp.logical_and(here, lax.axis_index("tm") < holders)
    return here


def rows_at(start, count, cols):
    return pl.ds(pl.multiple_of(start * cols, cols), count * cols)


def pick_kernel(per_half, holders, source, mine, own, other, sems):
    side = lax.axis_index("tm") & (holders - 1)
    lane = lax.axis_index("band") & (per_half - 1)
    clips = (lax.axis_index("segment"), side * per_half + lane, (holders - 1 - side) * per_half + lane)
    copies = [
        pltpu.make_async_copy(source.at[clip], target, sems.at[number])
        for number, (clip, target) in enumerate(zip(clips, (mine, own, other)))
    ]
    for copy in copies:
        copy.start()
    for copy in copies:
        copy.wait()


def loader_kernel(weight, bias, gain, now, past, bias_out, gain_out, sems):
    channels = weight.shape[-1]
    copies = [(bias, bias_out), (gain, gain_out), (weight.at[2], now)]
    for row in range(TAPS):
        for age in range(2):
            copies.append((weight.at[age, row], past.at[row, :, pl.ds(age * channels, channels)]))
    copies = [
        pltpu.make_async_copy(source, target, sems.at[number])
        for number, (source, target) in enumerate(copies)
    ]
    for copy in copies:
        copy.start()
    for copy in copies:
        copy.wait()


def frame_kernel(cfg, *refs):
    refs = list(refs)
    groups = [[refs.pop(0) for _ in range(TAPS)] for _ in range(cfg["groups"])]
    received = refs.pop(0) if cfg["came"] is not None else None
    partial, weight, bias, gain = refs[:4]
    refs = refs[4:]
    refs = refs[cfg["passing"] :]
    out = refs.pop(0) if cfg["sends"] else None
    spread = refs.pop(0) if cfg["later"] else refs.pop()
    tails = [refs.pop(0) for _ in range(cfg["finals"])]
    entry = refs.pop()
    cols, window, segments = cfg["cols"], cfg["window"], cfg["segments"]
    channels = entry.shape[-1]
    half = lax.axis_index("band") // cfg["per_half"]

    def run(unit):
        have = window - unit
        need = have - 1
        size = have * cols
        if unit == 0:
            step = entry.shape[0] // TAPS

            def place(group):
                for piece, code in zip(group, cfg["places"]):
                    number = (code >> (2 * lax.axis_index("band"))) & 3
                    entry[pl.ds(pl.multiple_of(number * step, step), step), :] = piece[cfg["piece_at"]]

            if len(groups) == 1:
                place(groups[0])
            else:
                near = lax.axis_index("tm") == cfg["time"]
                pl.when(near)(functools.partial(place, groups[0]))
                pl.when(jnp.logical_not(near))(functools.partial(place, groups[1]))
            source, skip = entry, 0
        else:
            source, skip = received, half * (unit - 1 - cfg["came"])
        wide = source[rows_at(skip, have, cols), :].astype(jnp.float32)
        meansq = jnp.sum(wide * wide, axis=-1, keepdims=True) * (1.0 / channels)
        normed = wide * lax.rsqrt(meansq + 1e-06) * gain[...]
        ready = normed / (1.0 + jnp.exp(-normed))
        column = lax.broadcasted_iota(jnp.int32, ready.shape, 0) & (cols - 1)
        before = jnp.where(column == 0, 0.0, pltpu.roll(ready, 1, 0))
        after = jnp.where(column == cols - 1, 0.0, pltpu.roll(ready, size - 1, 0))
        edge = jnp.zeros((cols, TAPS * channels), jnp.bfloat16)
        spread[pl.ds(0, cols), :] = edge
        spread[pl.ds(size + cols, cols), :] = edge
        for number, value in enumerate((before, ready, after)):
            spread[pl.ds(cols, size), pl.ds(number * channels, channels)] = value.astype(jnp.bfloat16)
        kept = source[rows_at(skip + half, need, cols), :].astype(jnp.float32)
        total = partial[pl.ds(0, need * cols), :] + kept + bias[...]
        for row in range(TAPS):
            total += jnp.dot(
                spread[rows_at(half + row, need, cols), :], weight[row], preferred_element_type=jnp.float32
            )
        value = total.astype(jnp.bfloat16)
        if unit < segments - 1:
            out[rows_at(half * (unit - cfg["lowest"]), need, cols), :] = value
        else:
            length = value.shape[0] // len(tails)
            for number, tail in enumerate(tails):
                tail[cfg["tail_at"]] = value[number * length : (number + 1) * length]

    for unit in cfg["units"]:
        pl.when(on_unit(unit, cfg["holders"]))(functools.partial(run, unit))


def history_kernel(cfg, spread, near, far, weight, near_out, far_out):
    cols, window = cfg["cols"], cfg["window"]
    channels = near.shape[-1]
    half = lax.axis_index("band") // cfg["per_half"]

    def run(unit):
        need = window - unit - 1
        here = pl.ds(0, need * cols)
        total = jnp.zeros((need * cols, 2 * channels), jnp.float32)
        for row in range(TAPS):
            total += jnp.dot(
                spread[rows_at(half + row, need, cols), :], weight[row], preferred_element_type=jnp.float32
            )
        near_out[here, :] = far[here, :] + total[:, channels:]
        far_out[here, :] = total[:, :channels]

    for unit in cfg["later"]:
        pl.when(on_unit(unit, cfg["holders"]))(functools.partial(run, unit))


def local(features, conv_weight, conv_bias, norm_gain):
    times, segments, bands = (lax.axis_size(name) for name in MESH_AXES)
    time, position, band = (lax.axis_index(name) for name in MESH_AXES)
    clips, own_frames, own_rows, cols, channels = features.shape
    frames = own_frames * times
    per_half = bands // HALVES
    window = own_rows * bands // HALVES + segments
    holders = clips // per_half
    piece = own_rows * cols
    assert clips == segments == bands == 4 and holders == 2 <= times and window == TAPS * own_rows

    def stream(clip, half):
        return clip // per_half, half * per_half + clip % per_half

    def spot(t, s, b):
        return (t * segments + s) * bands + b

    mine, own, other = pl.pallas_call(
        functools.partial(pick_kernel, per_half, holders),
        out_shape=[pltpu.VMEM((own_frames, piece, channels), features.dtype)] * 3,
        in_specs=[whole(pltpu.HBM)],
        out_specs=[whole()] * 3,
        scratch_shapes=[pltpu.SemaphoreType.DMA((3,))],
        compiler_params=pltpu.CompilerParams(vmem_limit_bytes=1 << 20),
        name="pick",
    )(pltpu.with_memory_space_constraint(features.reshape(clips, own_frames, piece, channels), pltpu.HBM))
    wanted = [[2 * h + j for h in range(HALVES) for j in range(per_half)], [1, 0, 3, 2], [2, 2, 1, 1]]
    places = [sum((b - at // per_half) << (2 * at) for at, b in enumerate(row)) for row in wanted]

    def gather(value, number, members):
        routes = []
        for t, clip in members:
            for h in range(HALVES):
                there, at = stream(clip, h)
                segment = clip if value is mine else 0
                routes.append((spot(t, segment, wanted[number][at]), spot(there, 0, at)))
        assert len({a for a, _ in routes}) == len({b for _, b in routes}) == len(routes)
        return lax.ppermute(value, MESH_AXES, routes)

    sides = [(t, clip) for t in range(holders) for clip in range(clips)]
    beside = [(t, clip) for t, clip in sides if clip // per_half == t]
    across = [(t, clip) for t, clip in sides if clip // per_half != t]
    far_group = [gather(mine, number, across) for number in (1, 2)]
    near_group = [gather(mine, number, beside) for number in (1, 2)]
    far_group = [gather(other, 0, across)] + far_group
    near_group = [own] + near_group
    entries = [[near_group, far_group]] * holders
    for t in range(holders, times):
        entries.append([[gather(mine, number, [(t, clip) for clip in range(clips)]) for number in range(TAPS)]])

    stored = [conv_weight[0].reshape(TAPS, TAPS, TAPS * channels, channels), conv_bias, norm_gain]
    now, past, bias, gain = pl.pallas_call(
        loader_kernel,
        out_shape=[
            pltpu.VMEM((TAPS, TAPS * channels, channels), stored[0].dtype),
            pltpu.VMEM((TAPS, TAPS * channels, 2 * channels), stored[0].dtype),
            pltpu.VMEM(conv_bias.shape, conv_bias.dtype),
            pltpu.VMEM(norm_gain.shape, norm_gain.dtype),
        ],
        in_specs=[whole(pltpu.HBM)] * 3,
        out_specs=[whole()] * 4,
        scratch_shapes=[pltpu.SemaphoreType.DMA((9,))],
        compiler_params=pltpu.CompilerParams(vmem_limit_bytes=1 << 20),
        name="loader",
    )(*[pltpu.with_memory_space_constraint(value, pltpu.HBM) for value in stored])
    now, past, bias, gain = (resident(value) for value in (now, past, bias, gain))

    state = ((window - 1) * cols, channels)
    near = jnp.zeros(state, jnp.float32)
    far = jnp.zeros(state, jnp.float32)
    lag = min(frames, DEPTH)
    slots = frames + lag * (segments - 1)
    moving = {}
    tails = []
    held = []
    landed = {}
    for slot in range(slots):
        units = working(slot, frames, segments, lag)
        senders_now = [s for s in units if s < segments - 1]
        last = slot - lag * (segments - 1)
        finals = per_half if last >= 0 else 0
        middle = finals and last % own_frames > 0
        cfg = dict(
            units=units,
            later=[s for s in units if slot - lag * s < frames - 1],
            sends=bool(senders_now),
            lowest=min(senders_now, default=0),
            groups=len(entries[slot // own_frames]) if slot < frames else 0,
            places=places,
            piece_at=slot % own_frames,
            time=slot // own_frames,
            came=min(working(slot - lag, frames, segments, lag)) if slot >= lag else None,
            finals=finals,
            tail_at=last % own_frames,
            passing=(finals if middle else 0) + (len(landed) if slot + 1 == slots else len(held)),
            cols=cols,
            window=window,
            segments=segments,
                        per_half=per_half,
            holders=holders,
        )
        operands = []
        if slot < frames:
            operands += [resident(value) for group in entries[slot // own_frames] for value in group]
        if slot >= lag:
            operands.append(resident(moving.pop(slot - lag)))
        operands += [resident(near), now, bias, gain]
        shapes = []
        if cfg["sends"]:
            shapes.append(pltpu.VMEM(((window - 1 - cfg["lowest"]) * cols, channels), jnp.bfloat16))
        wide = pltpu.VMEM(((window + 2) * cols, TAPS * channels), jnp.bfloat16)
        if cfg["later"]:
            shapes.append(wide)
        shape = pltpu.VMEM((own_frames, piece, channels), jnp.bfloat16)
        aliases = {}
        if middle:
            for index, value in enumerate(tails):
                aliases[len(operands)] = len(shapes) + index
                operands.append(resident(value))
        shapes += [shape] * finals
        if slot + 1 == slots:
            held = [(*key, value) for key, value in landed.items()]
        for _, _, value in held:
            aliases[len(operands)] = len(shapes)
            operands.append(resident(value))
            shapes.append(shape)
        results = list(
            pl.pallas_call(
                functools.partial(frame_kernel, cfg),
                out_shape=shapes,
                in_specs=[whole()] * len(operands),
                out_specs=[whole()] * len(shapes),
                scratch_shapes=[pltpu.VMEM((window * cols, channels), jnp.bfloat16)] + ([] if cfg["later"] else [wide]),
                input_output_aliases=aliases,
                compiler_params=pltpu.CompilerParams(vmem_limit_bytes=VMEM_LIMIT),
                cost_estimate=pl.CostEstimate(flops=0, transcendentals=0, bytes_accessed=1 << 10),
                name="frame",
            )(*operands)
        )
        out = results.pop(0) if cfg["sends"] else None
        spread = results.pop(0) if cfg["later"] else None
        tails = results[:finals]
        leaving = [(there, index, value) for (there, index, _), value in zip(held, results[finals:])]
        if slot + 1 == slots:
            landed.update({(there, index): value for there, index, value in leaving})
            leaving = []
        held = []
        if cfg["sends"]:
            moving[slot] = lax.ppermute(out, "segment", [(s, s + 1) for s in senders_now])
        if finals and last % own_frames == own_frames - 1:
            there = last // own_frames
            ready = [(there, index, value) for index, value in enumerate(tails)]
            leaving += ready
        for there, index, value in leaving:
            routes = []
            for clip in range(clips):
                for h in range(HALVES):
                    t, b = stream(clip, h)
                    routes.append((spot(t, segments - 1, b), spot(there, clip, h * per_half + index)))
            landed[there, index] = lax.ppermute(value, MESH_AXES, routes)
        if cfg["later"]:
            near, far = pl.pallas_call(
                functools.partial(history_kernel, cfg),
                out_shape=[pltpu.VMEM(state, jnp.float32)] * 2,
                in_specs=[whole()] * 4,
                out_specs=[whole()] * 2,
                input_output_aliases={1: 0, 2: 1},
                compiler_params=pltpu.CompilerParams(vmem_limit_bytes=VMEM_LIMIT),
                cost_estimate=pl.CostEstimate(flops=0, transcendentals=0, bytes_accessed=1 << 10),
                name="history",
            )(resident(spread), resident(near), resident(far), past)

    result = None
    for (t, index), value in landed.items():
        here = jnp.logical_and(time == t, band % per_half == index)
        result = value if result is None else jnp.where(here, value, result)
    return result.reshape(1, own_frames, own_rows, cols, channels)


def solution(mesh):
    return jax.shard_map(
        local,
        mesh=mesh,
        in_specs=(
            P(None, "tm", "band", None, None),
            P("segment", None, None, None),
            P("segment", None),
            P("segment", None),
        ),
        out_specs=P("segment", "tm", "band", None, None),
        check_vma=False,
    )
```

```python
import functools

import jax
import jax.numpy as jnp
from jax import lax
from jax.experimental import pallas as pl
from jax.experimental.pallas import tpu as pltpu
from jax.sharding import PartitionSpec as P

HALVES = 2
DEPTH = 4
TAPS = 3
VMEM_LIMIT = 24 << 20
MESH_AXES = ("tm", "segment", "band")


def whole(space=pltpu.VMEM):
    return pl.BlockSpec(memory_space=space)


def resident(value):
    return pltpu.with_memory_space_constraint(value, pltpu.VMEM)


def working(slot, frames, segments, lag):
    return [s for s in range(segments) if 0 <= slot - lag * s < frames]


def on_unit(unit, holders):
    here = lax.axis_index("segment") == unit
    if holders < lax.axis_size("tm"):
        here = jnp.logical_and(here, lax.axis_index("tm") < holders)
    return here


def rows_at(start, count, cols):
    return pl.ds(pl.multiple_of(start * cols, cols), count * cols)


def pick_kernel(per_half, holders, source, mine, own, sems):
    side = lax.axis_index("tm") & (holders - 1)
    lane = lax.axis_index("band") & (per_half - 1)
    clips = (lax.axis_index("segment"), side * per_half + lane)
    copies = [
        pltpu.make_async_copy(source.at[clip], target, sems.at[number])
        for number, (clip, target) in enumerate(zip(clips, (mine, own)))
    ]
    for copy in copies:
        copy.start()
    for copy in copies:
        copy.wait()


def taps(spread, start, count, cols):
    return jnp.concatenate([spread[rows_at(start + row, count, cols), :] for row in range(TAPS)], axis=1)


def loader_kernel(weight, bias, gain, now, past, bias_out, gain_out, sems):
    channels = weight.shape[-1]
    copies = [(bias, bias_out), (gain, gain_out), (weight.at[2], now)]
    for age in range(2):
        copies.append((weight.at[age], past.at[:, pl.ds(age * channels, channels)]))
    copies = [
        pltpu.make_async_copy(source, target, sems.at[number])
        for number, (source, target) in enumerate(copies)
    ]
    for copy in copies:
        copy.start()
    for copy in copies:
        copy.wait()


def frame_kernel(cfg, *refs):
    refs = list(refs)
    groups = [[refs.pop(0) for _ in range(TAPS)] for _ in range(cfg["groups"])]
    received = refs.pop(0) if cfg["came"] is not None else None
    partial, weight, bias, gain = refs[:4]
    refs = refs[4:]
    refs = refs[cfg["passing"] :]
    out = refs.pop(0) if cfg["sends"] else None
    spread = refs.pop(0) if cfg["later"] else refs.pop()
    tails = [refs.pop(0) for _ in range(cfg["finals"])]
    entry = refs.pop()
    cols, window, segments = cfg["cols"], cfg["window"], cfg["segments"]
    channels = entry.shape[-1]
    half = lax.axis_index("band") // cfg["per_half"]

    def run(unit):
        have = window - unit
        need = have - 1
        size = have * cols
        if unit == 0:
            step = entry.shape[0] // TAPS

            def place(group):
                for piece, code in zip(group, cfg["places"]):
                    number = (code >> (2 * lax.axis_index("band"))) & 3
                    entry[pl.ds(pl.multiple_of(number * step, step), step), :] = piece[cfg["piece_at"]]

            if len(groups) == 1:
                place(groups[0])
            else:
                near = lax.axis_index("tm") == cfg["time"]
                pl.when(near)(functools.partial(place, groups[1]))
                pl.when(jnp.logical_not(near))(functools.partial(place, groups[0]))
            source, skip = entry, 0
        else:
            source, skip = received, half * (unit - 1 - cfg["came"])
        wide = source[rows_at(skip, have, cols), :].astype(jnp.float32)
        meansq = jnp.sum(wide * wide, axis=-1, keepdims=True) * (1.0 / channels)
        normed = wide * lax.rsqrt(meansq + 1e-06) * gain[...]
        ready = normed / (1.0 + jnp.exp(-normed))
        column = lax.broadcasted_iota(jnp.int32, ready.shape, 0) & (cols - 1)
        before = jnp.where(column == 0, 0.0, pltpu.roll(ready, 1, 0))
        after = jnp.where(column == cols - 1, 0.0, pltpu.roll(ready, size - 1, 0))
        edge = jnp.zeros((cols, TAPS * channels), jnp.bfloat16)
        spread[pl.ds(0, cols), :] = edge
        spread[pl.ds(size + cols, cols), :] = edge
        for number, value in enumerate((before, ready, after)):
            spread[pl.ds(cols, size), pl.ds(number * channels, channels)] = value.astype(jnp.bfloat16)
        kept = source[rows_at(skip + half, need, cols), :].astype(jnp.float32)
        total = partial[pl.ds(0, need * cols), :] + kept + bias[...]
        total += jnp.dot(taps(spread, half, need, cols), weight[...], preferred_element_type=jnp.float32)
        value = total.astype(jnp.bfloat16)
        if unit < segments - 1:
            out[rows_at(half * (unit - cfg["lowest"]), need, cols), :] = value
        else:
            length = value.shape[0] // len(tails)
            for number, tail in enumerate(tails):
                tail[cfg["tail_at"]] = value[number * length : (number + 1) * length]

    for unit in cfg["units"]:
        pl.when(on_unit(unit, cfg["holders"]))(functools.partial(run, unit))


def history_kernel(cfg, spread, near, far, weight, near_out, far_out):
    cols, window = cfg["cols"], cfg["window"]
    channels = near.shape[-1]
    half = lax.axis_index("band") // cfg["per_half"]

    def run(unit):
        need = window - unit - 1
        here = pl.ds(0, need * cols)
        total = jnp.dot(taps(spread, half, need, cols), weight[...], preferred_element_type=jnp.float32)
        near_out[here, :] = far[here, :] + total[:, channels:]
        far_out[here, :] = total[:, :channels]

    for unit in cfg["later"]:
        pl.when(on_unit(unit, cfg["holders"]))(functools.partial(run, unit))


def local(features, conv_weight, conv_bias, norm_gain):
    times, segments, bands = (lax.axis_size(name) for name in MESH_AXES)
    time, position, band = (lax.axis_index(name) for name in MESH_AXES)
    clips, own_frames, own_rows, cols, channels = features.shape
    frames = own_frames * times
    per_half = bands // HALVES
    window = own_rows * bands // HALVES + segments
    holders = clips // per_half
    piece = own_rows * cols
    assert clips == segments == bands == 4 and holders == 2 <= times and window == TAPS * own_rows

    def stream(clip, half):
        return clip // per_half, half * per_half + clip % per_half

    def spot(t, s, b):
        return (t * segments + s) * bands + b

    mine, own = pl.pallas_call(
        functools.partial(pick_kernel, per_half, holders),
        out_shape=[pltpu.VMEM((own_frames, piece, channels), features.dtype)] * 2,
        in_specs=[whole(pltpu.HBM)],
        out_specs=[whole()] * 2,
        scratch_shapes=[pltpu.SemaphoreType.DMA((2,))],
        compiler_params=pltpu.CompilerParams(vmem_limit_bytes=1 << 20),
        name="pick",
    )(pltpu.with_memory_space_constraint(features.reshape(clips, own_frames, piece, channels), pltpu.HBM))
    wanted = [[2 * h + j for h in range(HALVES) for j in range(per_half)], [1, 0, 3, 2], [2, 2, 1, 1]]
    places = [sum((b - at // per_half) << (2 * at) for at, b in enumerate(row)) for row in wanted]

    def gather(number, members):
        routes = []
        for t, clip in members:
            for h in range(HALVES):
                there, at = stream(clip, h)
                routes.append((spot(t, clip, wanted[number][at]), spot(there, 0, at)))
        assert len({a for a, _ in routes}) == len({b for _, b in routes}) == len(routes)
        return lax.ppermute(mine, MESH_AXES, routes)

    sides = [(t, clip) for t in range(holders) for clip in range(clips)]
    beside = [(t, clip) for t, clip in sides if clip // per_half == t]
    across = [(t, clip) for t, clip in sides if clip // per_half != t]
    far_group = [gather(number, across) for number in range(TAPS)]
    near_group = [own] + [gather(number, beside) for number in (1, 2)]
    entries = [[far_group, near_group]] * holders
    for t in range(holders, times):
        entries.append([[gather(number, [(t, clip) for clip in range(clips)]) for number in range(TAPS)]])

    stored = [conv_weight[0].reshape(TAPS, TAPS * TAPS * channels, channels), conv_bias, norm_gain]
    now, past, bias, gain = pl.pallas_call(
        loader_kernel,
        out_shape=[
            pltpu.VMEM((TAPS * TAPS * channels, channels), stored[0].dtype),
            pltpu.VMEM((TAPS * TAPS * channels, 2 * channels), stored[0].dtype),
            pltpu.VMEM(conv_bias.shape, conv_bias.dtype),
            pltpu.VMEM(norm_gain.shape, norm_gain.dtype),
        ],
        in_specs=[whole(pltpu.HBM)] * 3,
        out_specs=[whole()] * 4,
        scratch_shapes=[pltpu.SemaphoreType.DMA((5,))],
        compiler_params=pltpu.CompilerParams(vmem_limit_bytes=1 << 20),
        name="loader",
    )(*[pltpu.with_memory_space_constraint(value, pltpu.HBM) for value in stored])
    now, past, bias, gain = (resident(value) for value in (now, past, bias, gain))

    def leave(value, there, index, group):
        routes = []
        for clip in group:
            for h in range(HALVES):
                t, b = stream(clip, h)
                routes.append((spot(t, segments - 1, b), spot(there, clip, h * per_half + index)))
        return lax.ppermute(value, MESH_AXES, routes)

    state = ((window - 1) * cols, channels)
    near = jnp.zeros(state, jnp.float32)
    far = jnp.zeros(state, jnp.float32)
    lag = min(frames, DEPTH)
    slots = frames + lag * (segments - 1)
    moving = {}
    tails = []
    waiting = []
    landed = {}
    for slot in range(slots):
        units = working(slot, frames, segments, lag)
        senders_now = [s for s in units if s < segments - 1]
        last = slot - lag * (segments - 1)
        finals = per_half if last >= 0 else 0
        middle = finals and last % own_frames > 0
        cfg = dict(
            units=units,
            later=[s for s in units if slot - lag * s < frames - 1],
            sends=bool(senders_now),
            lowest=min(senders_now, default=0),
            groups=len(entries[slot // own_frames]) if slot < frames else 0,
            places=places,
            piece_at=slot % own_frames,
            time=slot // own_frames,
            came=min(working(slot - lag, frames, segments, lag)) if slot >= lag else None,
            finals=finals,
            tail_at=last % own_frames,
            passing=(finals if middle else 0) + (len(landed) + len(waiting) if slot + 1 == slots else 0),
            cols=cols,
            window=window,
            segments=segments,
                        per_half=per_half,
            holders=holders,
        )
        operands = []
        if slot < frames:
            operands += [resident(value) for group in entries[slot // own_frames] for value in group]
        if slot >= lag:
            operands.append(resident(moving.pop(slot - lag)))
        operands += [resident(near), now, bias, gain]
        shapes = []
        if cfg["sends"]:
            shapes.append(pltpu.VMEM(((window - 1 - cfg["lowest"]) * cols, channels), jnp.bfloat16))
        wide = pltpu.VMEM(((window + 2) * cols, TAPS * channels), jnp.bfloat16)
        if cfg["later"]:
            shapes.append(wide)
        shape = pltpu.VMEM((own_frames, piece, channels), jnp.bfloat16)
        aliases = {}
        if middle:
            for index, value in enumerate(tails):
                aliases[len(operands)] = len(shapes) + index
                operands.append(resident(value))
        shapes += [shape] * finals
        held = list(landed) if slot + 1 == slots else []
        kept = [landed[key] for key in held] + ([value for _, _, value in waiting] if held else [])
        for value in kept:
            aliases[len(operands)] = len(shapes)
            operands.append(resident(value))
            shapes.append(shape)
        results = list(
            pl.pallas_call(
                functools.partial(frame_kernel, cfg),
                out_shape=shapes,
                in_specs=[whole()] * len(operands),
                out_specs=[whole()] * len(shapes),
                scratch_shapes=[pltpu.VMEM((window * cols, channels), jnp.bfloat16)] + ([] if cfg["later"] else [wide]),
                input_output_aliases=aliases,
                compiler_params=pltpu.CompilerParams(vmem_limit_bytes=VMEM_LIMIT),
                cost_estimate=pl.CostEstimate(flops=0, transcendentals=0, bytes_accessed=1 << 10),
                name="frame",
            )(*operands)
        )
        out = results.pop(0) if cfg["sends"] else None
        spread = results.pop(0) if cfg["later"] else None
        tails = results[:finals]
        if cfg["sends"]:
            moving[slot] = lax.ppermute(out, "segment", [(s, s + 1) for s in senders_now])
        if slot + 1 == slots:
            kept = results[finals:]
            landed.update(zip(held, kept))
            waiting = [(there, index, value) for (there, index, _), value in zip(waiting, kept[len(held) :])]
        if finals and last % own_frames == own_frames - 1:
            there = last // own_frames
            final = there == times - 1
            for index, value in enumerate(tails):
                landed[there, index, 0] = leave(value, there, index, range(clips if final else per_half))
            waiting += [] if final else [(there, index, value) for index, value in enumerate(tails)]
            if final:
                for there, index, value in waiting:
                    landed[there, index, 1] = leave(value, there, index, range(per_half, clips))
        if cfg["later"]:
            near, far = pl.pallas_call(
                functools.partial(history_kernel, cfg),
                out_shape=[pltpu.VMEM(state, jnp.float32)] * 2,
                in_specs=[whole()] * 4,
                out_specs=[whole()] * 2,
                input_output_aliases={1: 0, 2: 1},
                compiler_params=pltpu.CompilerParams(vmem_limit_bytes=VMEM_LIMIT),
                cost_estimate=pl.CostEstimate(flops=0, transcendentals=0, bytes_accessed=1 << 10),
                name="history",
            )(resident(spread), resident(near), resident(far), past)

    result = None
    for (t, index, part), value in landed.items():
        here = jnp.logical_and(time == t, band % per_half == index)
        if t < times - 1:
            here = jnp.logical_and(here, (position >= per_half) == (part == 1))
        result = value if result is None else jnp.where(here, value, result)
    return result.reshape(1, own_frames, own_rows, cols, channels)


def solution(mesh):
    return jax.shard_map(
        local,
        mesh=mesh,
        in_specs=(
            P(None, "tm", "band", None, None),
            P("segment", None, None, None),
            P("segment", None),
            P("segment", None),
        ),
        out_specs=P("segment", "tm", "band", None, None),
        check_vma=False,
    )
```

```python
import functools

import jax
import jax.numpy as jnp
from jax import lax
from jax.experimental import pallas as pl
from jax.experimental.pallas import tpu as pltpu
from jax.sharding import PartitionSpec as P

HALVES = 2
DEPTH = 4
TAPS = 3
VMEM_LIMIT = 24 << 20
MESH_AXES = ("tm", "segment", "band")


def whole(space=pltpu.VMEM):
    return pl.BlockSpec(memory_space=space)


def resident(value):
    return pltpu.with_memory_space_constraint(value, pltpu.VMEM)


def working(slot, frames, segments, lag):
    return [s for s in range(segments) if 0 <= slot - lag * s < frames]


def on_unit(unit, holders):
    here = lax.axis_index("segment") == unit
    if holders < lax.axis_size("tm"):
        here = jnp.logical_and(here, lax.axis_index("tm") < holders)
    return here


def rows_at(start, count, cols):
    return pl.ds(pl.multiple_of(start * cols, cols), count * cols)


def pick_kernel(per_half, holders, source, mine, own, sems):
    side = lax.axis_index("tm") & (holders - 1)
    lane = lax.axis_index("band") & (per_half - 1)
    clips = (lax.axis_index("segment"), side * per_half + lane)
    copies = [
        pltpu.make_async_copy(source.at[clip], target, sems.at[number])
        for number, (clip, target) in enumerate(zip(clips, (mine, own)))
    ]
    for copy in copies:
        copy.start()
    for copy in copies:
        copy.wait()


def taps(spread, start, count, cols):
    return jnp.concatenate([spread[rows_at(start + row, count, cols), :] for row in range(TAPS)], axis=1)


def loader_kernel(weight, bias, gain, now, past, bias_out, gain_out, sems):
    channels = weight.shape[-1]
    copies = [(bias, bias_out), (gain, gain_out), (weight.at[2], now)]
    for age in range(2):
        copies.append((weight.at[age], past.at[:, pl.ds(age * channels, channels)]))
    copies = [
        pltpu.make_async_copy(source, target, sems.at[number])
        for number, (source, target) in enumerate(copies)
    ]
    for copy in copies:
        copy.start()
    for copy in copies:
        copy.wait()


def frame_kernel(cfg, *refs):
    refs = list(refs)
    groups = [refs.pop(0) for _ in range(cfg["groups"])]
    received = refs.pop(0) if cfg["came"] is not None else None
    partial, weight, bias, gain = refs[:4]
    refs = refs[4:]
    refs = refs[cfg["passing"] :]
    out = refs.pop(0) if cfg["sends"] else None
    spread = refs.pop(0 if cfg["later"] else -1)
    tails = [refs.pop(0) for _ in range(cfg["finals"])]
    merged = [refs.pop(0) for _ in range(cfg["keeps"])][cfg["merged"] :][: cfg["finals"]]
    entry = refs.pop(0)
    cols, window, segments = cfg["cols"], cfg["window"], cfg["segments"]
    channels = entry.shape[-1]
    half = lax.axis_index("band") // cfg["per_half"]

    def run(unit):
        have = window - unit
        need = have - 1
        size = have * cols
        if unit == 0:
            step = entry.shape[0] // TAPS

            def place(piece, code):
                number = (code >> (2 * lax.axis_index("band"))) & 3
                entry[pl.ds(pl.multiple_of(number * step, step), step), :] = piece[cfg["piece_at"]]

            pieces, codes = list(groups), list(cfg["places"])
            if len(pieces) > TAPS:
                near = lax.axis_index("tm") == cfg["time"]
                pl.when(near)(functools.partial(place, pieces.pop(0), codes[0]))
                pl.when(jnp.logical_not(near))(functools.partial(place, pieces.pop(0), codes.pop(0)))
            for piece, code in zip(pieces, codes):
                place(piece, code)
            source, skip = entry, 0
        else:
            source, skip = received, half * (unit - 1 - cfg["came"])
        wide = source[rows_at(skip, have, cols), :].astype(jnp.float32)
        meansq = jnp.sum(wide * wide, axis=-1, keepdims=True) * (1.0 / channels)
        normed = wide * lax.rsqrt(meansq + 1e-06) * gain[...]
        ready = normed / (1.0 + jnp.exp(-normed))
        column = lax.broadcasted_iota(jnp.int32, ready.shape, 0) & (cols - 1)
        before = jnp.where(column == 0, 0.0, pltpu.roll(ready, 1, 0))
        after = jnp.where(column == cols - 1, 0.0, pltpu.roll(ready, size - 1, 0))
        edge = jnp.zeros((cols, TAPS * channels), jnp.bfloat16)
        spread[pl.ds(0, cols), :] = edge
        spread[pl.ds(size + cols, cols), :] = edge
        for number, value in enumerate((before, ready, after)):
            spread[pl.ds(cols, size), pl.ds(number * channels, channels)] = value.astype(jnp.bfloat16)
        kept = source[rows_at(skip + half, need, cols), :].astype(jnp.float32)
        total = partial[pl.ds(0, need * cols), :] + kept + bias[...]
        total += jnp.dot(taps(spread, half, need, cols), weight[...], preferred_element_type=jnp.float32)
        value = total.astype(jnp.bfloat16)
        if unit < segments - 1:
            out[rows_at(half * (unit - cfg["lowest"]), need, cols), :] = value
        else:
            length = value.shape[0] // len(tails)
            for number, tail in enumerate(tails):
                tail[cfg["tail_at"]] = value[number * length : (number + 1) * length]

            @pl.when(lax.axis_index("tm") == 0)
            def _():
                for tail, ref in zip(tails, merged):
                    ref[...] = tail[...]

    for unit in cfg["units"]:
        pl.when(on_unit(unit, cfg["holders"]))(functools.partial(run, unit))


def history_kernel(cfg, spread, near, far, weight, near_out, far_out):
    cols, window = cfg["cols"], cfg["window"]
    channels = near.shape[-1]
    half = lax.axis_index("band") // cfg["per_half"]

    def run(unit):
        need = window - unit - 1
        here = pl.ds(0, need * cols)
        total = jnp.dot(taps(spread, half, need, cols), weight[...], preferred_element_type=jnp.float32)
        near_out[here, :] = far[here, :] + total[:, channels:]
        far_out[here, :] = total[:, :channels]

    for unit in cfg["later"]:
        pl.when(on_unit(unit, cfg["holders"]))(functools.partial(run, unit))


def local(features, conv_weight, conv_bias, norm_gain):
    times, segments, bands = (lax.axis_size(name) for name in MESH_AXES)
    time, position, band = (lax.axis_index(name) for name in MESH_AXES)
    clips, own_frames, own_rows, cols, channels = features.shape
    frames = own_frames * times
    per_half = bands // HALVES
    window = own_rows * bands // HALVES + segments
    holders = clips // per_half
    piece = own_rows * cols
    assert clips == segments == bands == 4 and holders == 2 <= times and window == TAPS * own_rows

    def stream(clip, half):
        return clip // per_half, half * per_half + clip % per_half

    def spot(t, s, b):
        return (t * segments + s) * bands + b

    mine, own = pl.pallas_call(
        functools.partial(pick_kernel, per_half, holders),
        out_shape=[pltpu.VMEM((own_frames, piece, channels), features.dtype)] * 2,
        in_specs=[whole(pltpu.HBM)],
        out_specs=[whole()] * 2,
        scratch_shapes=[pltpu.SemaphoreType.DMA((2,))],
        compiler_params=pltpu.CompilerParams(vmem_limit_bytes=1 << 20),
        name="pick",
    )(pltpu.with_memory_space_constraint(features.reshape(clips, own_frames, piece, channels), pltpu.HBM))
    wanted = [[2 * h + j for h in range(HALVES) for j in range(per_half)], [1, 0, 3, 2], [2, 2, 1, 1]]
    places = [sum((b - at // per_half) << (2 * at) for at, b in enumerate(row)) for row in wanted]

    def gather(number, members):
        routes = []
        for t, clip in members:
            for h in range(HALVES):
                there, at = stream(clip, h)
                routes.append((spot(t, clip, wanted[number][at]), spot(there, 0, at)))
        assert len({a for a, _ in routes}) == len({b for _, b in routes}) == len(routes)
        return lax.ppermute(mine, MESH_AXES, routes)

    across = [(t, clip) for t in range(holders) for clip in range(clips) if clip // per_half != t]
    crossed = gather(0, across)
    entries = []
    for t in range(times):
        members = [(t, clip) for clip in range(clips)]
        first = [own, crossed] if t < holders else [gather(0, members)]
        entries.append(first + [gather(number, members) for number in (1, 2)])

    stored = [conv_weight[0].reshape(TAPS, TAPS * TAPS * channels, channels), conv_bias, norm_gain]
    now, past, bias, gain = pl.pallas_call(
        loader_kernel,
        out_shape=[
            pltpu.VMEM((TAPS * TAPS * channels, channels), stored[0].dtype),
            pltpu.VMEM((TAPS * TAPS * channels, 2 * channels), stored[0].dtype),
            pltpu.VMEM(conv_bias.shape, conv_bias.dtype),
            pltpu.VMEM(norm_gain.shape, norm_gain.dtype),
        ],
        in_specs=[whole(pltpu.HBM)] * 3,
        out_specs=[whole()] * 4,
        scratch_shapes=[pltpu.SemaphoreType.DMA((5,))],
        compiler_params=pltpu.CompilerParams(vmem_limit_bytes=1 << 20),
        name="loader",
    )(*[pltpu.with_memory_space_constraint(value, pltpu.HBM) for value in stored])
    now, past, bias, gain = (resident(value) for value in (now, past, bias, gain))

    def leave(value, members):
        routes = []
        for there, index, clip in members:
            for h in range(HALVES):
                t, b = stream(clip, h)
                routes.append((spot(t, segments - 1, b), spot(there, clip, h * per_half + index)))
        assert len({a for a, _ in routes}) == len({b for _, b in routes}) == len(routes)
        return lax.ppermute(value, MESH_AXES, routes)

    state = ((window - 1) * cols, channels)
    near = jnp.zeros(state, jnp.float32)
    far = jnp.zeros(state, jnp.float32)
    lag = min(frames, DEPTH)
    slots = frames + lag * (segments - 1)
    moving = {}
    tails = []
    waiting = []
    landed = {}
    for slot in range(slots):
        units = working(slot, frames, segments, lag)
        senders_now = [s for s in units if s < segments - 1]
        last = slot - lag * (segments - 1)
        finals = per_half if last >= 0 else 0
        middle = finals and last % own_frames > 0
        keeps = len(landed) + len(waiting) if slot + 1 == slots else 0
        cfg = dict(
            units=units,
            later=[s for s in units if slot - lag * s < frames - 1],
            sends=bool(senders_now),
            lowest=min(senders_now, default=0),
            groups=len(entries[slot // own_frames]) if slot < frames else 0,
            places=places,
            piece_at=slot % own_frames,
            time=slot // own_frames,
            came=min(working(slot - lag, frames, segments, lag)) if slot >= lag else None,
            finals=finals,
            tail_at=last % own_frames,
            passing=(finals if middle else 0) + keeps,
            keeps=keeps,
            merged=len(landed),
            cols=cols,
            window=window,
            segments=segments,
                        per_half=per_half,
            holders=holders,
        )
        operands = []
        if slot < frames:
            operands += [resident(value) for value in entries[slot // own_frames]]
        if slot >= lag:
            operands.append(resident(moving.pop(slot - lag)))
        operands += [resident(near), now, bias, gain]
        shapes = []
        if cfg["sends"]:
            shapes.append(pltpu.VMEM(((window - 1 - cfg["lowest"]) * cols, channels), jnp.bfloat16))
        wide = pltpu.VMEM(((window + 2) * cols, TAPS * channels), jnp.bfloat16)
        if cfg["later"]:
            shapes.append(wide)
        shape = pltpu.VMEM((own_frames, piece, channels), jnp.bfloat16)
        aliases = {}
        if middle:
            for index, value in enumerate(tails):
                aliases[len(operands)] = len(shapes) + index
                operands.append(resident(value))
        shapes += [shape] * finals
        held = list(landed) if slot + 1 == slots else []
        kept = [landed[key][0] for key in held] + ([value for _, _, value in waiting] if held else [])
        for value in kept:
            aliases[len(operands)] = len(shapes)
            operands.append(resident(value))
            shapes.append(shape)
        results = list(
            pl.pallas_call(
                functools.partial(frame_kernel, cfg),
                out_shape=shapes,
                in_specs=[whole()] * len(operands),
                out_specs=[whole()] * len(shapes),
                scratch_shapes=[pltpu.VMEM((window * cols, channels), jnp.bfloat16)] + ([] if cfg["later"] else [wide]),
                input_output_aliases=aliases,
                compiler_params=pltpu.CompilerParams(vmem_limit_bytes=VMEM_LIMIT),
                cost_estimate=pl.CostEstimate(flops=0, transcendentals=0, bytes_accessed=1 << 10),
                name="frame",
            )(*operands)
        )
        out = results.pop(0) if cfg["sends"] else None
        spread = results.pop(0) if cfg["later"] else None
        tails = results[:finals]
        if cfg["sends"]:
            moving[slot] = lax.ppermute(out, "segment", [(s, s + 1) for s in senders_now])
        if slot + 1 == slots:
            kept = results[finals:]
            landed.update({key: [value] for key, value in zip(held, kept)})
            waiting = [(there, index, value) for (there, index, _), value in zip(waiting, kept[len(held) :])]
        if finals and last % own_frames == own_frames - 1:
            there = last // own_frames
            final = there == times - 1
            if not final:
                for index, value in enumerate(tails):
                    landed[there, index] = [leave(value, [(there, index, clip) for clip in range(per_half)])]
                waiting += [(there, index, value) for index, value in enumerate(tails)]
            else:
                late = range(per_half, clips)
                pairs_left = [((there, index, value), waiting.pop(0)) for index, value in enumerate(tails)]
                for (_, index, _), (before, _, value) in pairs_left:
                    both = [(there, index, clip) for clip in range(per_half)] + [(before, index, clip) for clip in late]
                    sent = leave(value, both)
                    landed[there, index] = [sent]
                    landed[before, index].append(sent)
                for before, index, value in waiting:
                    landed[before, index].append(leave(value, [(before, index, clip) for clip in late]))
                for (_, index, value), _ in pairs_left:
                    landed[there, index].append(leave(value, [(there, index, clip) for clip in late]))
        if cfg["later"]:
            near, far = pl.pallas_call(
                functools.partial(history_kernel, cfg),
                out_shape=[pltpu.VMEM(state, jnp.float32)] * 2,
                in_specs=[whole()] * 4,
                out_specs=[whole()] * 2,
                input_output_aliases={1: 0, 2: 1},
                compiler_params=pltpu.CompilerParams(vmem_limit_bytes=VMEM_LIMIT),
                cost_estimate=pl.CostEstimate(flops=0, transcendentals=0, bytes_accessed=1 << 10),
                name="history",
            )(resident(spread), resident(near), resident(far), past)

    result = None
    for (t, index), (early, late) in landed.items():
        here = jnp.logical_and(time == t, band % per_half == index)
        value = jnp.where(position < per_half, early, late)
        result = value if result is None else jnp.where(here, value, result)
    return result.reshape(1, own_frames, own_rows, cols, channels)


def solution(mesh):
    return jax.shard_map(
        local,
        mesh=mesh,
        in_specs=(
            P(None, "tm", "band", None, None),
            P("segment", None, None, None),
            P("segment", None),
            P("segment", None),
        ),
        out_specs=P("segment", "tm", "band", None, None),
        check_vma=False,
    )
```

```python
import functools

import jax
import jax.numpy as jnp
from jax import lax
from jax.experimental import pallas as pl
from jax.experimental.pallas import tpu as pltpu
from jax.sharding import PartitionSpec as P

HALVES = 2
DEPTH = 4
TAPS = 3
VMEM_LIMIT = 24 << 20
MESH_AXES = ("tm", "segment", "band")


def whole(space=pltpu.VMEM):
    return pl.BlockSpec(memory_space=space)


def resident(value):
    return pltpu.with_memory_space_constraint(value, pltpu.VMEM)


def in_hbm(value):
    return pltpu.with_memory_space_constraint(value, pltpu.HBM)


def working(slot, frames, segments, lag):
    return [s for s in range(segments) if 0 <= slot - lag * s < frames]


def on_unit(unit, holders):
    here = lax.axis_index("segment") == unit
    if holders < lax.axis_size("tm"):
        here = jnp.logical_and(here, lax.axis_index("tm") < holders)
    return here


def rows_at(start, count, cols):
    return pl.ds(pl.multiple_of(start * cols, cols), count * cols)


def run_copies(copies, sems):
    copies = [
        pltpu.make_async_copy(source, target, sems.at[number]) for number, (source, target) in enumerate(copies)
    ]
    for copy in copies:
        copy.start()
    return copies


def pick_kernel(per_half, holders, source, bias, gain, mine, own, bias_out, gain_out, *refs):
    singles, sems = refs[:-1], refs[-1]
    side = lax.axis_index("tm") & (holders - 1)
    lane = lax.axis_index("band") & (per_half - 1)
    clip = lax.axis_index("segment")
    copies = [(source.at[clip, number], single.at[0]) for number, single in enumerate(singles)]
    copies += [(source.at[clip], mine), (source.at[side * per_half + lane], own), (bias, bias_out), (gain, gain_out)]
    for copy in run_copies(copies, sems):
        copy.wait()


def taps_dot(spread, weight, start, count, cols, copies):
    rows = [spread[rows_at(start + row, count, cols), :] for row in range(TAPS)]
    if not copies:
        return jnp.dot(jnp.concatenate(rows, axis=1), weight[...], preferred_element_type=jnp.float32)
    depth = weight.shape[0] // TAPS
    total = None
    for number, row in enumerate(rows):
        for copy in copies[number :: TAPS]:
            copy.wait()
        part = jnp.dot(row, weight[pl.ds(number * depth, depth), :], preferred_element_type=jnp.float32)
        total = part if total is None else total + part
    return total


def frame_kernel(cfg, *refs):
    refs = list(refs)
    groups = [refs.pop(0) for _ in range(cfg["groups"])]
    received = refs.pop(0) if cfg["came"] is not None else None
    partial, weight, bias, gain = refs[:4]
    refs = refs[4:]
    refs = refs[cfg["passing"] :]
    copies = []
    if cfg["loads"]:
        source, weight, sems = weight, refs.pop(0), refs.pop()
        depth = weight.shape[0] // TAPS
        thirds = [pl.ds(number * depth, depth) for number in range(TAPS)]
        copies = run_copies([(source.at[2, third], weight.at[third]) for third in thirds], sems)
    out = refs.pop(0) if cfg["sends"] else None
    spread = refs.pop(0 if cfg["later"] else -1)
    tails = [refs.pop(0) for _ in range(cfg["finals"])]
    refs = refs[cfg["keeps"] :]
    entry = refs.pop(0)
    cols, window, segments = cfg["cols"], cfg["window"], cfg["segments"]
    channels = entry.shape[-1]
    half = lax.axis_index("band") // cfg["per_half"]

    def run(unit):
        have = window - unit
        need = have - 1
        size = have * cols
        if unit == 0:
            step = entry.shape[0] // TAPS

            def place(piece, code):
                number = (code >> (2 * lax.axis_index("band"))) & 3
                piece, at = piece
                entry[pl.ds(pl.multiple_of(number * step, step), step), :] = piece[at]

            pieces, codes = list(zip(groups, cfg["piece_at"])), list(cfg["places"])
            if len(pieces) > TAPS:
                near = lax.axis_index("tm") == cfg["time"]
                pl.when(near)(functools.partial(place, pieces.pop(0), codes[0]))
                pl.when(jnp.logical_not(near))(functools.partial(place, pieces.pop(0), codes.pop(0)))
            for piece, code in zip(pieces, codes):
                place(piece, code)
            source, skip = entry, 0
        else:
            source, skip = received, half * (unit - 1 - cfg["came"])
        wide = source[rows_at(skip, have, cols), :].astype(jnp.float32)
        meansq = jnp.sum(wide * wide, axis=-1, keepdims=True) * (1.0 / channels)
        normed = wide * lax.rsqrt(meansq + 1e-06) * gain[...]
        ready = normed / (1.0 + jnp.exp(-normed))
        column = lax.broadcasted_iota(jnp.int32, ready.shape, 0) & (cols - 1)
        before = jnp.where(column == 0, 0.0, pltpu.roll(ready, 1, 0))
        after = jnp.where(column == cols - 1, 0.0, pltpu.roll(ready, size - 1, 0))
        edge = jnp.zeros((cols, TAPS * channels), jnp.bfloat16)
        spread[pl.ds(0, cols), :] = edge
        spread[pl.ds(size + cols, cols), :] = edge
        for number, value in enumerate((before, ready, after)):
            spread[pl.ds(cols, size), pl.ds(number * channels, channels)] = value.astype(jnp.bfloat16)
        kept = source[rows_at(skip + half, need, cols), :].astype(jnp.float32)
        total = partial[pl.ds(0, need * cols), :] + kept + bias[...]
        total += taps_dot(spread, weight, half, need, cols, copies)
        value = total.astype(jnp.bfloat16)
        if unit < segments - 1:
            out[rows_at(half * (unit - cfg["lowest"]), need, cols), :] = value
        else:
            length = value.shape[0] // len(tails)
            for number, tail in enumerate(tails):
                tail[cfg["tail_at"]] = value[number * length : (number + 1) * length]

    run_units(cfg, cfg["units"], run, copies)


def run_units(cfg, units, run, copies):
    active = [on_unit(unit, cfg["holders"]) for unit in units]
    for unit, here in zip(units, active):
        pl.when(here)(functools.partial(run, unit))
    if copies:

        @pl.when(jnp.logical_not(functools.reduce(jnp.logical_or, active)))
        def _():
            for copy in copies:
                copy.wait()


def history_kernel(cfg, spread, near, far, weight, near_out, far_out, *refs):
    cols, window = cfg["cols"], cfg["window"]
    channels = near.shape[-1]
    half = lax.axis_index("band") // cfg["per_half"]
    copies = []
    if cfg["loads"]:
        source, (weight, sems) = weight, refs
        depth = weight.shape[0] // TAPS
        copies = run_copies(
            [
                (source.at[age, third], weight.at[third, pl.ds(age * channels, channels)])
                for age in range(2)
                for third in [pl.ds(number * depth, depth) for number in range(TAPS)]
            ],
            sems,
        )

    def run(unit):
        need = window - unit - 1
        here = pl.ds(0, need * cols)
        total = taps_dot(spread, weight, half, need, cols, copies)
        near_out[here, :] = far[here, :] + total[:, channels:]
        far_out[here, :] = total[:, :channels]

    run_units(cfg, cfg["later"], run, copies)


def local(features, conv_weight, conv_bias, norm_gain):
    times, segments, bands = (lax.axis_size(name) for name in MESH_AXES)
    time, position, band = (lax.axis_index(name) for name in MESH_AXES)
    clips, own_frames, own_rows, cols, channels = features.shape
    frames = own_frames * times
    per_half = bands // HALVES
    window = own_rows * bands // HALVES + segments
    holders = clips // per_half
    piece = own_rows * cols
    assert clips == segments == bands == 4 and holders == 2 <= times and window == TAPS * own_rows

    def stream(clip, half):
        return clip // per_half, half * per_half + clip % per_half

    def spot(t, s, b):
        return (t * segments + s) * bands + b

    shape = (own_frames, piece, channels)
    mine, own, bias, gain, *singles = pl.pallas_call(
        functools.partial(pick_kernel, per_half, holders),
        out_shape=[
            pltpu.VMEM(shape, features.dtype),
            pltpu.VMEM(shape, features.dtype),
            pltpu.VMEM(conv_bias.shape, conv_bias.dtype),
            pltpu.VMEM(norm_gain.shape, norm_gain.dtype),
        ]
        + [pltpu.VMEM((1, piece, channels), features.dtype)] * own_frames,
        in_specs=[whole(pltpu.HBM)] * 3,
        out_specs=[whole()] * (4 + own_frames),
        scratch_shapes=[pltpu.SemaphoreType.DMA((4 + own_frames,))],
        compiler_params=pltpu.CompilerParams(vmem_limit_bytes=1 << 20),
        name="pick",
    )(*[in_hbm(value) for value in (features.reshape(clips, *shape), conv_bias, norm_gain)])
    bias, gain = resident(bias), resident(gain)
    weight = in_hbm(conv_weight[0].reshape(TAPS, TAPS * TAPS * channels, channels))
    wanted = [[2 * h + j for h in range(HALVES) for j in range(per_half)], [1, 0, 3, 2], [2, 2, 1, 1]]
    places = [sum((b - at // per_half) << (2 * at) for at, b in enumerate(row)) for row in wanted]

    def gather(value, number, members):
        routes = []
        for t, clip in members:
            for h in range(HALVES):
                there, at = stream(clip, h)
                routes.append((spot(t, clip, wanted[number][at]), spot(there, 0, at)))
        assert len({a for a, _ in routes}) == len({b for _, b in routes}) == len(routes)
        return lax.ppermute(value, MESH_AXES, routes)

    across = [(t, clip) for t in range(holders) for clip in range(clips) if clip // per_half != t]
    entries = []
    crossed = gather(mine, 0, across)
    for t in range(times):
        members = [(t, clip) for clip in range(clips)]
        if t == 0:
            for number, single in enumerate(singles):
                others = [gather(single, part, members) for part in (1, 2)]
                entries.append(([own, crossed, *others], [number, number, 0, 0]))
            continue
        others = [gather(mine, part, members) for part in (1, 2)]
        whole_own = [] if t < holders else [gather(mine, 0, members)]
        for number in range(own_frames):
            if t < holders:
                entries.append(([own, crossed, *others], [number] * 4))
            else:
                entries.append((whole_own + others, [number] * TAPS))

    def leave(value, there, index):
        routes = []
        for clip in range(clips):
            for h in range(HALVES):
                t, b = stream(clip, h)
                routes.append((spot(t, segments - 1, b), spot(there, clip, h * per_half + index)))
        return lax.ppermute(value, MESH_AXES, routes)

    state = ((window - 1) * cols, channels)
    near = jnp.zeros(state, jnp.float32)
    far = jnp.zeros(state, jnp.float32)
    lag = min(frames, DEPTH)
    slots = frames + lag * (segments - 1)
    moving = {}
    tails = []
    landed = {}
    for slot in range(slots):
        units = working(slot, frames, segments, lag)
        senders_now = [s for s in units if s < segments - 1]
        last = slot - lag * (segments - 1)
        finals = per_half if last >= 0 else 0
        middle = finals and last % own_frames > 0
        keeps = len(landed) if slot + 1 == slots else 0
        cfg = dict(
            units=units,
            later=[s for s in units if slot - lag * s < frames - 1],
            sends=bool(senders_now),
            lowest=min(senders_now, default=0),
            groups=len(entries[slot][0]) if slot < frames else 0,
            loads=slot == 0,
            places=places,
            piece_at=entries[slot][1] if slot < frames else [],
            time=slot // own_frames,
            came=min(working(slot - lag, frames, segments, lag)) if slot >= lag else None,
            finals=finals,
            tail_at=last % own_frames,
            passing=(finals if middle else 0) + keeps,
            keeps=keeps,
            cols=cols,
            window=window,
            segments=segments,
                        per_half=per_half,
            holders=holders,
        )
        operands = []
        if slot < frames:
            operands += [resident(value) for value in entries[slot][0]]
        if slot >= lag:
            operands.append(resident(moving.pop(slot - lag)))
        operands += [resident(near), weight if slot == 0 else now, bias, gain]
        shapes = [pltpu.VMEM((TAPS * TAPS * channels, channels), weight.dtype)] if cfg["loads"] else []
        if cfg["sends"]:
            shapes.append(pltpu.VMEM(((window - 1 - cfg["lowest"]) * cols, channels), jnp.bfloat16))
        wide = pltpu.VMEM(((window + 2) * cols, TAPS * channels), jnp.bfloat16)
        if cfg["later"]:
            shapes.append(wide)
        shape = pltpu.VMEM((own_frames, piece, channels), jnp.bfloat16)
        aliases = {}
        if middle:
            for index, value in enumerate(tails):
                aliases[len(operands)] = len(shapes) + index
                operands.append(resident(value))
        shapes += [shape] * finals
        held = list(landed) if keeps else []
        for value in [landed[key] for key in held]:
            aliases[len(operands)] = len(shapes)
            operands.append(resident(value))
            shapes.append(shape)
        results = list(
            pl.pallas_call(
                functools.partial(frame_kernel, cfg),
                out_shape=shapes,
                in_specs=[whole(pltpu.HBM if value is weight else pltpu.VMEM) for value in operands],
                out_specs=[whole()] * len(shapes),
                scratch_shapes=[pltpu.VMEM((window * cols, channels), jnp.bfloat16)]
                + ([] if cfg["later"] else [wide])
                + ([pltpu.SemaphoreType.DMA((TAPS,))] if cfg["loads"] else []),
                input_output_aliases=aliases,
                compiler_params=pltpu.CompilerParams(vmem_limit_bytes=VMEM_LIMIT),
                cost_estimate=pl.CostEstimate(flops=0, transcendentals=0, bytes_accessed=1 << 10),
                name="frame",
            )(*operands)
        )
        if cfg["loads"]:
            now = resident(results.pop(0))
        out = results.pop(0) if cfg["sends"] else None
        spread = results.pop(0) if cfg["later"] else None
        tails = results[:finals]
        if cfg["sends"]:
            moving[slot] = lax.ppermute(out, "segment", [(s, s + 1) for s in senders_now])
        landed.update(zip(held, results[finals:]))
        if finals and last % own_frames == own_frames - 1:
            there = last // own_frames
            for index, value in enumerate(tails):
                landed[there, index] = leave(value, there, index)
        if cfg["later"]:
            loading = [pltpu.VMEM((TAPS * TAPS * channels, 2 * channels), weight.dtype)] if cfg["loads"] else []
            near, far, *loaded = pl.pallas_call(
                functools.partial(history_kernel, cfg),
                out_shape=[pltpu.VMEM(state, jnp.float32)] * 2 + loading,
                in_specs=[whole()] * 3 + [whole(pltpu.HBM if loading else pltpu.VMEM)],
                out_specs=[whole()] * (2 + len(loading)),
                scratch_shapes=[pltpu.SemaphoreType.DMA((2 * TAPS,))] if loading else [],
                input_output_aliases={1: 0, 2: 1},
                compiler_params=pltpu.CompilerParams(vmem_limit_bytes=VMEM_LIMIT),
                cost_estimate=pl.CostEstimate(flops=0, transcendentals=0, bytes_accessed=1 << 10),
                name="history",
            )(resident(spread), resident(near), resident(far), weight if loading else past)
            past = resident(loaded[0]) if loading else past

    result = None
    for (t, index), value in landed.items():
        here = jnp.logical_and(time == t, band % per_half == index)
        result = value if result is None else jnp.where(here, value, result)
    return result.reshape(1, own_frames, own_rows, cols, channels)


def solution(mesh):
    return jax.shard_map(
        local,
        mesh=mesh,
        in_specs=(
            P(None, "tm", "band", None, None),
            P("segment", None, None, None),
            P("segment", None),
            P("segment", None),
        ),
        out_specs=P("segment", "tm", "band", None, None),
        check_vma=False,
    )
```

```python
import functools

import jax
import jax.numpy as jnp
from jax import lax
from jax.experimental import pallas as pl
from jax.experimental.pallas import tpu as pltpu
from jax.sharding import PartitionSpec as P

HALVES = 2
DEPTH = 4
TAPS = 3
VMEM_LIMIT = 24 << 20
MESH_AXES = ("tm", "segment", "band")


def whole(space=pltpu.VMEM):
    return pl.BlockSpec(memory_space=space)


def resident(value):
    return pltpu.with_memory_space_constraint(value, pltpu.VMEM)


def working(slot, frames, segments, lag):
    return [s for s in range(segments) if 0 <= slot - lag * s < frames]


def on_unit(unit, holders):
    here = lax.axis_index("segment") == unit
    if holders < lax.axis_size("tm"):
        here = jnp.logical_and(here, lax.axis_index("tm") < holders)
    return here


def rows_at(start, count, cols):
    return pl.ds(pl.multiple_of(start * cols, cols), count * cols)


def sent_clips(side, lane, segment, choose):
    near, far = 2 * side, 2 - 2 * side
    behind = far + ((segment - 1) & 1)
    return (
        far + lane,
        choose(segment == 0, near + 1, choose(segment == 3, near, behind)),
        choose(segment == 0, near, choose(segment == 3, near + 1, behind)),
    )


def pick_kernel(holders, source, own, across, second, third, sems):
    time = lax.axis_index("tm")
    side = jnp.where(time < holders, time, 0)
    lane = lax.axis_index("band") & 1
    clips = (2 * side + lane, *sent_clips(side, lane, lax.axis_index("segment"), jnp.where))
    copies = [
        pltpu.make_async_copy(source.at[clip], target, sems.at[number])
        for number, (clip, target) in enumerate(zip(clips, (own, across, second, third)))
    ]
    for copy in copies:
        copy.start()
    for copy in copies:
        copy.wait()


def taps(spread, start, count, cols):
    return jnp.concatenate([spread[rows_at(start + row, count, cols), :] for row in range(TAPS)], axis=1)


def loader_kernel(weight, bias, gain, now, past, bias_out, gain_out, sems):
    channels = weight.shape[-1]
    copies = [(bias, bias_out), (gain, gain_out), (weight.at[2], now)]
    for age in range(2):
        copies.append((weight.at[age], past.at[:, pl.ds(age * channels, channels)]))
    copies = [
        pltpu.make_async_copy(source, target, sems.at[number])
        for number, (source, target) in enumerate(copies)
    ]
    for copy in copies:
        copy.start()
    for copy in copies:
        copy.wait()


def frame_kernel(cfg, *refs):
    refs = list(refs)
    groups = [refs.pop(0) for _ in range(cfg["groups"])]
    received = refs.pop(0) if cfg["came"] is not None else None
    partial, weight, bias, gain = refs[:4]
    refs = refs[4:]
    refs = refs[cfg["passing"] :]
    out = refs.pop(0) if cfg["sends"] else None
    spread = refs.pop(0 if cfg["later"] else -1)
    tails = [refs.pop(0) for _ in range(cfg["finals"])]
    merged = [refs.pop(0) for _ in range(cfg["keeps"])][cfg["merged"] :][: cfg["finals"]]
    entry = refs.pop(0)
    cols, window, segments = cfg["cols"], cfg["window"], cfg["segments"]
    channels = entry.shape[-1]
    half = lax.axis_index("band") // cfg["per_half"]

    def run(unit):
        have = window - unit
        need = have - 1
        size = have * cols
        if unit == 0:
            step = entry.shape[0] // TAPS

            def place(piece, code):
                number = (code >> (2 * lax.axis_index("band"))) & 3
                entry[pl.ds(pl.multiple_of(number * step, step), step), :] = piece[cfg["piece_at"]]

            *others, own, crossed = groups
            first, *rest = cfg["places"]
            near = lax.axis_index("tm") == cfg["near"]
            pl.when(near)(functools.partial(place, own, first))
            pl.when(jnp.logical_not(near))(functools.partial(place, crossed, first))
            for piece, code in zip(others, rest):
                place(piece, code)
            source, skip = entry, 0
        else:
            source, skip = received, half * (unit - 1 - cfg["came"])
        wide = source[rows_at(skip, have, cols), :].astype(jnp.float32)
        meansq = jnp.sum(wide * wide, axis=-1, keepdims=True) * (1.0 / channels)
        normed = wide * lax.rsqrt(meansq + 1e-06) * gain[...]
        ready = normed / (1.0 + jnp.exp(-normed))
        column = lax.broadcasted_iota(jnp.int32, ready.shape, 0) & (cols - 1)
        before = jnp.where(column == 0, 0.0, pltpu.roll(ready, 1, 0))
        after = jnp.where(column == cols - 1, 0.0, pltpu.roll(ready, size - 1, 0))
        edge = jnp.zeros((cols, TAPS * channels), jnp.bfloat16)
        spread[pl.ds(0, cols), :] = edge
        spread[pl.ds(size + cols, cols), :] = edge
        for number, value in enumerate((before, ready, after)):
            spread[pl.ds(cols, size), pl.ds(number * channels, channels)] = value.astype(jnp.bfloat16)
        kept = source[rows_at(skip + half, need, cols), :].astype(jnp.float32)
        total = partial[pl.ds(0, need * cols), :] + kept + bias[...]
        total += jnp.dot(taps(spread, half, need, cols), weight[...], preferred_element_type=jnp.float32)
        value = total.astype(jnp.bfloat16)
        if unit < segments - 1:
            out[rows_at(half * (unit - cfg["lowest"]), need, cols), :] = value
        else:
            length = value.shape[0] // len(tails)
            for number, tail in enumerate(tails):
                tail[cfg["tail_at"]] = value[number * length : (number + 1) * length]

            @pl.when(lax.axis_index("tm") == 0)
            def _():
                for tail, ref in zip(tails, merged):
                    ref[...] = tail[...]

    for unit in cfg["units"]:
        pl.when(on_unit(unit, cfg["holders"]))(functools.partial(run, unit))


def history_kernel(cfg, spread, near, far, weight, near_out, far_out):
    cols, window = cfg["cols"], cfg["window"]
    channels = near.shape[-1]
    half = lax.axis_index("band") // cfg["per_half"]

    def run(unit):
        need = window - unit - 1
        here = pl.ds(0, need * cols)
        total = jnp.dot(taps(spread, half, need, cols), weight[...], preferred_element_type=jnp.float32)
        near_out[here, :] = far[here, :] + total[:, channels:]
        far_out[here, :] = total[:, :channels]

    for unit in cfg["later"]:
        pl.when(on_unit(unit, cfg["holders"]))(functools.partial(run, unit))


def local(features, conv_weight, conv_bias, norm_gain):
    times, segments, bands = (lax.axis_size(name) for name in MESH_AXES)
    time, position, band = (lax.axis_index(name) for name in MESH_AXES)
    clips, own_frames, own_rows, cols, channels = features.shape
    frames = own_frames * times
    per_half = bands // HALVES
    window = own_rows * bands // HALVES + segments
    holders = clips // per_half
    piece = own_rows * cols
    assert clips == segments == bands == 4 == 2 * per_half and holders == 2 <= times and window == TAPS * own_rows

    def stream(clip, half):
        return clip // per_half, half * per_half + clip % per_half

    def spot(t, s, b):
        return (t * segments + s) * bands + b

    own, *sources = pl.pallas_call(
        functools.partial(pick_kernel, holders),
        out_shape=[pltpu.VMEM((own_frames, piece, channels), features.dtype)] * 4,
        in_specs=[whole(pltpu.HBM)],
        out_specs=[whole()] * 4,
        scratch_shapes=[pltpu.SemaphoreType.DMA((4,))],
        compiler_params=pltpu.CompilerParams(vmem_limit_bytes=1 << 20),
        name="pick",
    )(pltpu.with_memory_space_constraint(features.reshape(clips, own_frames, piece, channels), pltpu.HBM))
    wanted = [[2 * h + j for h in range(HALVES) for j in range(per_half)], [2, 0, 1, 2], [1, 2, 3, 1]]
    places = [sum((b - at // per_half) << (2 * at) for at, b in enumerate(row)) for row in wanted]

    def gather(number, members):
        routes = []
        for t, clip in members:
            side, (there, lane) = t if t < holders else 0, divmod(clip, per_half)
            if number == 0:
                segment = t if t < holders else 1
            elif there == side:
                segment = 3 if lane == number - 1 else 0
            else:
                segment = 1 + lane
            for h in range(HALVES):
                at = stream(clip, h)[1]
                source = wanted[number][at]
                assert clip == sent_clips(side, source & 1, segment, lambda a, b, c: b if a else c)[number]
                routes.append((spot(t, segment, source), spot(there, 0, at)))
        assert len({a for a, _ in routes}) == len({b for _, b in routes}) == len(routes)
        return lax.ppermute(sources[number], MESH_AXES, routes)

    def far_side(t):
        return [(t, clip) for clip in range(clips) if clip // per_half != (t if t < holders else 0)]

    entries = []
    for t in range(times):
        others = [gather(number, [(t, clip) for clip in range(clips)]) for number in (1, 2)]
        if t == 0:
            crossed = gather(0, [member for side in range(holders) for member in far_side(side)])
        if t < holders:
            entries.append(others + [own, crossed])
        else:
            routes = [(spot(t, 0, b), spot(0, 0, b)) for b in range(bands)]
            entries.append(others + [lax.ppermute(own, MESH_AXES, routes), gather(0, far_side(t))])

    stored = [conv_weight[0].reshape(TAPS, TAPS * TAPS * channels, channels), conv_bias, norm_gain]
    now, past, bias, gain = pl.pallas_call(
        loader_kernel,
        out_shape=[
            pltpu.VMEM((TAPS * TAPS * channels, channels), stored[0].dtype),
            pltpu.VMEM((TAPS * TAPS * channels, 2 * channels), stored[0].dtype),
            pltpu.VMEM(conv_bias.shape, conv_bias.dtype),
            pltpu.VMEM(norm_gain.shape, norm_gain.dtype),
        ],
        in_specs=[whole(pltpu.HBM)] * 3,
        out_specs=[whole()] * 4,
        scratch_shapes=[pltpu.SemaphoreType.DMA((5,))],
        compiler_params=pltpu.CompilerParams(vmem_limit_bytes=1 << 20),
        name="loader",
    )(*[pltpu.with_memory_space_constraint(value, pltpu.HBM) for value in stored])
    now, past, bias, gain = (resident(value) for value in (now, past, bias, gain))

    def leave(value, members):
        routes = []
        for there, index, clip in members:
            for h in range(HALVES):
                t, b = stream(clip, h)
                routes.append((spot(t, segments - 1, b), spot(there, clip, h * per_half + index)))
        assert len({a for a, _ in routes}) == len({b for _, b in routes}) == len(routes)
        return lax.ppermute(value, MESH_AXES, routes)

    state = ((window - 1) * cols, channels)
    near = jnp.zeros(state, jnp.float32)
    far = jnp.zeros(state, jnp.float32)
    lag = min(frames, DEPTH)
    slots = frames + lag * (segments - 1)
    moving = {}
    tails = []
    waiting = []
    landed = {}
    for slot in range(slots):
        units = working(slot, frames, segments, lag)
        senders_now = [s for s in units if s < segments - 1]
        last = slot - lag * (segments - 1)
        finals = per_half if last >= 0 else 0
        middle = finals and last % own_frames > 0
        keeps = len(landed) + len(waiting) if slot + 1 == slots else 0
        cfg = dict(
            units=units,
            later=[s for s in units if slot - lag * s < frames - 1],
            sends=bool(senders_now),
            lowest=min(senders_now, default=0),
            groups=len(entries[slot // own_frames]) if slot < frames else 0,
            places=places,
            piece_at=slot % own_frames,
            near=slot // own_frames if slot // own_frames < holders else 0,
            came=min(working(slot - lag, frames, segments, lag)) if slot >= lag else None,
            finals=finals,
            tail_at=last % own_frames,
            passing=(finals if middle else 0) + keeps,
            keeps=keeps,
            merged=len(landed),
            cols=cols,
            window=window,
            segments=segments,
                        per_half=per_half,
            holders=holders,
        )
        operands = []
        if slot < frames:
            operands += [resident(value) for value in entries[slot // own_frames]]
        if slot >= lag:
            operands.append(resident(moving.pop(slot - lag)))
        operands += [resident(near), now, bias, gain]
        shapes = []
        if cfg["sends"]:
            shapes.append(pltpu.VMEM(((window - 1 - cfg["lowest"]) * cols, channels), jnp.bfloat16))
        wide = pltpu.VMEM(((window + 2) * cols, TAPS * channels), jnp.bfloat16)
        if cfg["later"]:
            shapes.append(wide)
        shape = pltpu.VMEM((own_frames, piece, channels), jnp.bfloat16)
        aliases = {}
        if middle:
            for index, value in enumerate(tails):
                aliases[len(operands)] = len(shapes) + index
                operands.append(resident(value))
        shapes += [shape] * finals
        held = list(landed) if slot + 1 == slots else []
        kept = [landed[key][0] for key in held] + ([value for _, _, value in waiting] if held else [])
        for value in kept:
            aliases[len(operands)] = len(shapes)
            operands.append(resident(value))
            shapes.append(shape)
        results = list(
            pl.pallas_call(
                functools.partial(frame_kernel, cfg),
                out_shape=shapes,
                in_specs=[whole()] * len(operands),
                out_specs=[whole()] * len(shapes),
                scratch_shapes=[pltpu.VMEM((window * cols, channels), jnp.bfloat16)] + ([] if cfg["later"] else [wide]),
                input_output_aliases=aliases,
                compiler_params=pltpu.CompilerParams(vmem_limit_bytes=VMEM_LIMIT),
                cost_estimate=pl.CostEstimate(flops=0, transcendentals=0, bytes_accessed=1 << 10),
                name="frame",
            )(*operands)
        )
        out = results.pop(0) if cfg["sends"] else None
        spread = results.pop(0) if cfg["later"] else None
        tails = results[:finals]
        if cfg["sends"]:
            moving[slot] = lax.ppermute(out, "segment", [(s, s + 1) for s in senders_now])
        if slot + 1 == slots:
            kept = results[finals:]
            landed.update({key: [value] for key, value in zip(held, kept)})
            waiting = [(there, index, value) for (there, index, _), value in zip(waiting, kept[len(held) :])]
        if finals and last % own_frames == own_frames - 1:
            there = last // own_frames
            final = there == times - 1
            if not final:
                for index, value in enumerate(tails):
                    landed[there, index] = [leave(value, [(there, index, clip) for clip in range(per_half)])]
                waiting += [(there, index, value) for index, value in enumerate(tails)]
            else:
                late = range(per_half, clips)
                pairs_left = [((there, index, value), waiting.pop(0)) for index, value in enumerate(tails)]
                for (_, index, _), (before, _, value) in pairs_left:
                    both = [(there, index, clip) for clip in range(per_half)] + [(before, index, clip) for clip in late]
                    sent = leave(value, both)
                    landed[there, index] = [sent]
                    landed[before, index].append(sent)
                for before, index, value in waiting:
                    landed[before, index].append(leave(value, [(before, index, clip) for clip in late]))
                for (_, index, value), _ in pairs_left:
                    landed[there, index].append(leave(value, [(there, index, clip) for clip in late]))
        if cfg["later"]:
            near, far = pl.pallas_call(
                functools.partial(history_kernel, cfg),
                out_shape=[pltpu.VMEM(state, jnp.float32)] * 2,
                in_specs=[whole()] * 4,
                out_specs=[whole()] * 2,
                input_output_aliases={1: 0, 2: 1},
                compiler_params=pltpu.CompilerParams(vmem_limit_bytes=VMEM_LIMIT),
                cost_estimate=pl.CostEstimate(flops=0, transcendentals=0, bytes_accessed=1 << 10),
                name="history",
            )(resident(spread), resident(near), resident(far), past)

    result = None
    for (t, index), (early, late) in landed.items():
        here = jnp.logical_and(time == t, band % per_half == index)
        value = jnp.where(position < per_half, early, late)
        result = value if result is None else jnp.where(here, value, result)
    return result.reshape(1, own_frames, own_rows, cols, channels)


def solution(mesh):
    return jax.shard_map(
        local,
        mesh=mesh,
        in_specs=(
            P(None, "tm", "band", None, None),
            P("segment", None, None, None),
            P("segment", None),
            P("segment", None),
        ),
        out_specs=P("segment", "tm", "band", None, None),
        check_vma=False,
    )
```

```python
import functools

import jax
import jax.numpy as jnp
from jax import lax
from jax.experimental import pallas as pl
from jax.experimental.pallas import tpu as pltpu
from jax.sharding import PartitionSpec as P

HALVES = 2
DEPTH = 4
TAPS = 3
VMEM_LIMIT = 24 << 20
MESH_AXES = ("tm", "segment", "band")


def whole(space=pltpu.VMEM):
    return pl.BlockSpec(memory_space=space)


def resident(value):
    return pltpu.with_memory_space_constraint(value, pltpu.VMEM)


def working(slot, frames, segments, lag):
    return [s for s in range(segments) if 0 <= slot - lag * s < frames]


def on_unit(unit, holders):
    here = lax.axis_index("segment") == unit
    if holders < lax.axis_size("tm"):
        here = jnp.logical_and(here, lax.axis_index("tm") < holders)
    return here


def rows_at(start, count, cols):
    return pl.ds(pl.multiple_of(start * cols, cols), count * cols)


def sent_clips(side, lane, segment, choose):
    near, far = 2 * side, 2 - 2 * side
    behind = far + ((segment - 1) & 1)
    return (
        far + lane,
        choose(segment == 0, near + 1, choose(segment == 3, near, behind)),
        choose(segment == 0, near, choose(segment == 3, near + 1, behind)),
    )


def pick_kernel(holders, source, own, across, second, third, sems):
    time = lax.axis_index("tm")
    side = jnp.where(time < holders, time, 0)
    lane = lax.axis_index("band") & 1
    clips = (2 * side + lane, *sent_clips(side, lane, lax.axis_index("segment"), jnp.where))
    copies = [
        pltpu.make_async_copy(source.at[clip], target, sems.at[number])
        for number, (clip, target) in enumerate(zip(clips, (own, across, second, third)))
    ]
    for copy in copies:
        copy.start()
    for copy in copies:
        copy.wait()


def taps(spread, start, count, cols):
    return jnp.concatenate([spread[rows_at(start + row, count, cols), :] for row in range(TAPS)], axis=1)


def loader_kernel(weight, bias, gain, now, past, bias_out, gain_out, sems):
    channels = weight.shape[-1]
    copies = [(bias, bias_out), (gain, gain_out), (weight.at[2], now)]
    for age in range(2):
        copies.append((weight.at[age], past.at[:, pl.ds(age * channels, channels)]))
    copies = [
        pltpu.make_async_copy(source, target, sems.at[number])
        for number, (source, target) in enumerate(copies)
    ]
    for copy in copies:
        copy.start()
    for copy in copies:
        copy.wait()


def frame_kernel(cfg, *refs):
    refs = list(refs)
    groups = [refs.pop(0) for _ in range(cfg["groups"])]
    received = refs.pop(0) if cfg["came"] is not None else None
    partial, weight, bias, gain = refs[:4]
    refs = refs[4:]
    refs = refs[cfg["passing"] :]
    out = refs.pop(0) if cfg["sends"] else None
    spread = refs.pop(0 if cfg["later"] else -1)
    tails = [refs.pop(0) for _ in range(cfg["finals"])]
    merged = [refs.pop(0) for _ in range(cfg["keeps"])][cfg["merged"] :][: cfg["finals"]]
    entry = refs.pop(0)
    cols, window, segments = cfg["cols"], cfg["window"], cfg["segments"]
    channels = entry.shape[-1]
    half = lax.axis_index("band") // cfg["per_half"]

    def run(unit):
        have = window - unit
        need = have - 1
        size = have * cols
        if unit == 0:
            step = entry.shape[0] // TAPS

            def place(piece, code):
                number = (code >> (2 * lax.axis_index("band"))) & 3
                entry[pl.ds(pl.multiple_of(number * step, step), step), :] = piece[cfg["piece_at"]]

            *others, own, crossed = groups[:4]
            first, *rest = cfg["places"]
            near = lax.axis_index("tm") == cfg["near"]
            pl.when(near)(functools.partial(place, own, first))
            pl.when(jnp.logical_not(near))(functools.partial(place, crossed, first))
            for piece, code in zip(others, rest):
                place(piece, code)
            source, skip = entry, 0
        else:
            source, skip = received, half * (unit - 1 - cfg["came"])
        wide = source[rows_at(skip, have, cols), :].astype(jnp.float32)
        meansq = jnp.sum(wide * wide, axis=-1, keepdims=True) * (1.0 / channels)
        normed = wide * lax.rsqrt(meansq + 1e-06) * gain[...]
        ready = normed / (1.0 + jnp.exp(-normed))
        column = lax.broadcasted_iota(jnp.int32, ready.shape, 0) & (cols - 1)
        before = jnp.where(column == 0, 0.0, pltpu.roll(ready, 1, 0))
        after = jnp.where(column == cols - 1, 0.0, pltpu.roll(ready, size - 1, 0))
        edge = jnp.zeros((cols, TAPS * channels), jnp.bfloat16)
        spread[pl.ds(0, cols), :] = edge
        spread[pl.ds(size + cols, cols), :] = edge
        for number, value in enumerate((before, ready, after)):
            spread[pl.ds(cols, size), pl.ds(number * channels, channels)] = value.astype(jnp.bfloat16)
        kept = source[rows_at(skip + half, need, cols), :].astype(jnp.float32)
        total = partial[pl.ds(0, need * cols), :] + kept + bias[...]
        total += jnp.dot(taps(spread, half, need, cols), weight[...], preferred_element_type=jnp.float32)
        value = total.astype(jnp.bfloat16)
        if unit < segments - 1:
            out[rows_at(half * (unit - cfg["lowest"]), need, cols), :] = value
        else:
            length = value.shape[0] // len(tails)
            for number, tail in enumerate(tails):
                tail[cfg["tail_at"]] = value[number * length : (number + 1) * length]

            @pl.when(lax.axis_index("tm") == 0)
            def _():
                for tail, ref in zip(tails, merged):
                    ref[...] = tail[...]

    for unit in cfg["units"]:
        pl.when(on_unit(unit, cfg["holders"]))(functools.partial(run, unit))


def history_kernel(cfg, spread, near, far, weight, near_out, far_out):
    cols, window = cfg["cols"], cfg["window"]
    channels = near.shape[-1]
    half = lax.axis_index("band") // cfg["per_half"]

    def run(unit):
        need = window - unit - 1
        here = pl.ds(0, need * cols)
        ready = taps(spread, half, need, cols)
        if unit in cfg["ending"]:
            total = jnp.dot(ready, weight[:, channels:], preferred_element_type=jnp.float32)
            near_out[here, :] = far[here, :] + total
        else:
            total = jnp.dot(ready, weight[...], preferred_element_type=jnp.float32)
            near_out[here, :] = far[here, :] + total[:, channels:]
            far_out[here, :] = total[:, :channels]

    for unit in cfg["later"]:
        pl.when(on_unit(unit, cfg["holders"]))(functools.partial(run, unit))


def local(features, conv_weight, conv_bias, norm_gain):
    times, segments, bands = (lax.axis_size(name) for name in MESH_AXES)
    time, position, band = (lax.axis_index(name) for name in MESH_AXES)
    clips, own_frames, own_rows, cols, channels = features.shape
    frames = own_frames * times
    per_half = bands // HALVES
    window = own_rows * bands // HALVES + segments
    holders = clips // per_half
    piece = own_rows * cols
    assert clips == segments == bands == 4 == 2 * per_half and holders == 2 <= times and window == TAPS * own_rows

    def stream(clip, half):
        return clip // per_half, half * per_half + clip % per_half

    def spot(t, s, b):
        return (t * segments + s) * bands + b

    own, *sources = pl.pallas_call(
        functools.partial(pick_kernel, holders),
        out_shape=[pltpu.VMEM((own_frames, piece, channels), features.dtype)] * 4,
        in_specs=[whole(pltpu.HBM)],
        out_specs=[whole()] * 4,
        scratch_shapes=[pltpu.SemaphoreType.DMA((4,))],
        compiler_params=pltpu.CompilerParams(vmem_limit_bytes=1 << 20),
        name="pick",
    )(pltpu.with_memory_space_constraint(features.reshape(clips, own_frames, piece, channels), pltpu.HBM))
    wanted = [[2 * h + j for h in range(HALVES) for j in range(per_half)], [2, 0, 1, 2], [1, 2, 3, 1]]
    places = [sum((b - at // per_half) << (2 * at) for at, b in enumerate(row)) for row in wanted]

    def gather(number, members):
        routes = []
        for t, clip in members:
            side, (there, lane) = t if t < holders else 0, divmod(clip, per_half)
            if number == 0:
                segment = t if t < holders else 1
            elif there == side:
                segment = 3 if lane == number - 1 else 0
            else:
                segment = 1 + lane
            for h in range(HALVES):
                at = stream(clip, h)[1]
                source = wanted[number][at]
                assert clip == sent_clips(side, source & 1, segment, lambda a, b, c: b if a else c)[number]
                routes.append((spot(t, segment, source), spot(there, 0, at)))
        assert len({a for a, _ in routes}) == len({b for _, b in routes}) == len(routes)
        return lax.ppermute(sources[number], MESH_AXES, routes)

    def far_side(t):
        return [(t, clip) for clip in range(clips) if clip // per_half != (t if t < holders else 0)]

    entries = []
    for t in range(times):
        others = [gather(number, [(t, clip) for clip in range(clips)]) for number in (1, 2)]
        if t == 0:
            crossed = gather(0, [member for side in range(holders) for member in far_side(side)])
        if t < holders:
            entries.append(others + [own, crossed] + (entries[0][:2] if t else []))
        else:
            routes = [(spot(t, 0, b), spot(0, 0, b)) for b in range(bands)]
            entries.append(others + [lax.ppermute(own, MESH_AXES, routes), gather(0, far_side(t))])

    stored = [conv_weight[0].reshape(TAPS, TAPS * TAPS * channels, channels), conv_bias, norm_gain]
    now, past, bias, gain = pl.pallas_call(
        loader_kernel,
        out_shape=[
            pltpu.VMEM((TAPS * TAPS * channels, channels), stored[0].dtype),
            pltpu.VMEM((TAPS * TAPS * channels, 2 * channels), stored[0].dtype),
            pltpu.VMEM(conv_bias.shape, conv_bias.dtype),
            pltpu.VMEM(norm_gain.shape, norm_gain.dtype),
        ],
        in_specs=[whole(pltpu.HBM)] * 3,
        out_specs=[whole()] * 4,
        scratch_shapes=[pltpu.SemaphoreType.DMA((5,))],
        compiler_params=pltpu.CompilerParams(vmem_limit_bytes=1 << 20),
        name="loader",
    )(*[pltpu.with_memory_space_constraint(value, pltpu.HBM) for value in stored])
    now, past, bias, gain = (resident(value) for value in (now, past, bias, gain))

    def leave(value, members):
        routes = []
        for there, index, clip in members:
            for h in range(HALVES):
                t, b = stream(clip, h)
                routes.append((spot(t, segments - 1, b), spot(there, clip, h * per_half + index)))
        assert len({a for a, _ in routes}) == len({b for _, b in routes}) == len(routes)
        return lax.ppermute(value, MESH_AXES, routes)

    state = ((window - 1) * cols, channels)
    near = jnp.zeros(state, jnp.float32)
    far = jnp.zeros(state, jnp.float32)
    lag = min(frames, DEPTH)
    slots = frames + lag * (segments - 1)
    moving = {}
    tails = []
    waiting = []
    landed = {}
    for slot in range(slots):
        units = working(slot, frames, segments, lag)
        senders_now = [s for s in units if s < segments - 1]
        last = slot - lag * (segments - 1)
        finals = per_half if last >= 0 else 0
        middle = finals and last % own_frames > 0
        keeps = len(landed) + len(waiting) if slot + 1 == slots else 0
        cfg = dict(
            units=units,
            later=[s for s in units if slot - lag * s < frames - 1],
            ending=[s for s in units if slot - lag * s == frames - 2],
            sends=bool(senders_now),
            lowest=min(senders_now, default=0),
            groups=len(entries[slot // own_frames]) if slot < frames else 0,
            places=places,
            piece_at=slot % own_frames,
            near=slot // own_frames if slot // own_frames < holders else 0,
            came=min(working(slot - lag, frames, segments, lag)) if slot >= lag else None,
            finals=finals,
            tail_at=last % own_frames,
            passing=(finals if middle else 0) + keeps,
            keeps=keeps,
            merged=len(landed),
            cols=cols,
            window=window,
            segments=segments,
                        per_half=per_half,
            holders=holders,
        )
        operands = []
        if slot < frames:
            operands += [resident(value) for value in entries[slot // own_frames]]
        if slot >= lag:
            operands.append(resident(moving.pop(slot - lag)))
        operands += [resident(near), now, bias, gain]
        shapes = []
        if cfg["sends"]:
            shapes.append(pltpu.VMEM(((window - 1 - cfg["lowest"]) * cols, channels), jnp.bfloat16))
        wide = pltpu.VMEM(((window + 2) * cols, TAPS * channels), jnp.bfloat16)
        if cfg["later"]:
            shapes.append(wide)
        shape = pltpu.VMEM((own_frames, piece, channels), jnp.bfloat16)
        aliases = {}
        if middle:
            for index, value in enumerate(tails):
                aliases[len(operands)] = len(shapes) + index
                operands.append(resident(value))
        shapes += [shape] * finals
        held = list(landed) if slot + 1 == slots else []
        kept = [landed[key][0] for key in held] + ([value for _, _, value in waiting] if held else [])
        for value in kept:
            aliases[len(operands)] = len(shapes)
            operands.append(resident(value))
            shapes.append(shape)
        results = list(
            pl.pallas_call(
                functools.partial(frame_kernel, cfg),
                out_shape=shapes,
                in_specs=[whole()] * len(operands),
                out_specs=[whole()] * len(shapes),
                scratch_shapes=[pltpu.VMEM((window * cols, channels), jnp.bfloat16)] + ([] if cfg["later"] else [wide]),
                input_output_aliases=aliases,
                compiler_params=pltpu.CompilerParams(vmem_limit_bytes=VMEM_LIMIT),
                cost_estimate=pl.CostEstimate(flops=0, transcendentals=0, bytes_accessed=1 << 10),
                name="frame",
            )(*operands)
        )
        out = results.pop(0) if cfg["sends"] else None
        spread = results.pop(0) if cfg["later"] else None
        tails = results[:finals]
        if cfg["sends"]:
            moving[slot] = lax.ppermute(out, "segment", [(s, s + 1) for s in senders_now])
        if slot + 1 == slots:
            kept = results[finals:]
            landed.update({key: [value] for key, value in zip(held, kept)})
            waiting = [(there, index, value) for (there, index, _), value in zip(waiting, kept[len(held) :])]
        if finals and last % own_frames == own_frames - 1:
            there = last // own_frames
            final = there == times - 1
            if not final:
                for index, value in enumerate(tails):
                    landed[there, index] = [leave(value, [(there, index, clip) for clip in range(per_half)])]
                waiting += [(there, index, value) for index, value in enumerate(tails)]
            else:
                late = range(per_half, clips)
                pairs_left = [((there, index, value), waiting.pop(0)) for index, value in enumerate(tails)]
                for (_, index, _), (before, _, value) in pairs_left:
                    both = [(there, index, clip) for clip in range(per_half)] + [(before, index, clip) for clip in late]
                    sent = leave(value, both)
                    landed[there, index] = [sent]
                    landed[before, index].append(sent)
                for before, index, value in waiting:
                    landed[before, index].append(leave(value, [(before, index, clip) for clip in late]))
                for (_, index, value), _ in pairs_left:
                    landed[there, index].append(leave(value, [(there, index, clip) for clip in late]))
        if cfg["later"]:
            near, far = pl.pallas_call(
                functools.partial(history_kernel, cfg),
                out_shape=[pltpu.VMEM(state, jnp.float32)] * 2,
                in_specs=[whole()] * 4,
                out_specs=[whole()] * 2,
                input_output_aliases={1: 0, 2: 1},
                compiler_params=pltpu.CompilerParams(vmem_limit_bytes=VMEM_LIMIT),
                cost_estimate=pl.CostEstimate(flops=0, transcendentals=0, bytes_accessed=1 << 10),
                name="history",
            )(resident(spread), resident(near), resident(far), past)

    chosen = []
    for (t, index), parts in landed.items():
        for late, value in enumerate(parts):
            here = jnp.logical_and(time == t, band % per_half == index)
            here = jnp.logical_and(here, (position >= per_half) == bool(late))
            same = [number for number, (_, other) in enumerate(chosen) if other is value]
            if same:
                chosen[same[0]] = (jnp.logical_or(here, chosen[same[0]][0]), value)
            else:
                chosen.append((here, value))
    shared = [value for parts in landed.values() for value in parts]
    chosen.sort(key=lambda pair: sum(value is pair[1] for value in shared))
    result = chosen[0][1]
    for here, value in chosen[1:]:
        result = jnp.where(here, value, result)
    return result.reshape(1, own_frames, own_rows, cols, channels)


def solution(mesh):
    return jax.shard_map(
        local,
        mesh=mesh,
        in_specs=(
            P(None, "tm", "band", None, None),
            P("segment", None, None, None),
            P("segment", None),
            P("segment", None),
        ),
        out_specs=P("segment", "tm", "band", None, None),
        check_vma=False,
    )
```

```python
import functools

import jax
import jax.numpy as jnp
from jax import lax
from jax.experimental import pallas as pl
from jax.experimental.pallas import tpu as pltpu
from jax.sharding import PartitionSpec as P

HALVES = 2
DEPTH = 4
TAPS = 3
VMEM_LIMIT = 24 << 20
MESH_AXES = ("tm", "segment", "band")


def whole(space=pltpu.VMEM):
    return pl.BlockSpec(memory_space=space)


def resident(value):
    return pltpu.with_memory_space_constraint(value, pltpu.VMEM)


def working(slot, frames, segments, lag):
    return [s for s in range(segments) if 0 <= slot - lag * s < frames]


def on_unit(unit, holders):
    here = lax.axis_index("segment") == unit
    if holders < lax.axis_size("tm"):
        here = jnp.logical_and(here, lax.axis_index("tm") < holders)
    return here


def rows_at(start, count, cols):
    return pl.ds(pl.multiple_of(start * cols, cols), count * cols)


def sent_clips(side, lane, segment, choose):
    near, far = 2 * side, 2 - 2 * side
    behind = far + ((segment - 1) & 1)
    return (
        far + lane,
        choose(segment == 0, near + 1, choose(segment == 3, near, behind)),
        choose(segment == 0, near, choose(segment == 3, near + 1, behind)),
    )


def pick_kernel(holders, source, own, across, second, third, sems):
    time = lax.axis_index("tm")
    side = jnp.where(time < holders, time, 0)
    lane = lax.axis_index("band") & 1
    clips = (2 * side + lane, *sent_clips(side, lane, lax.axis_index("segment"), jnp.where))
    copies = [
        pltpu.make_async_copy(source.at[clip], target, sems.at[number])
        for number, (clip, target) in enumerate(zip(clips, (own, across, second, third)))
    ]
    for copy in copies:
        copy.start()
    for copy in copies:
        copy.wait()


def taps(spread, start, count, cols):
    return jnp.concatenate([spread[rows_at(start + row, count, cols), :] for row in range(TAPS)], axis=1)


def loader_kernel(weight, bias, gain, now, past, bias_out, gain_out, sems):
    channels = weight.shape[-1]
    copies = [(bias, bias_out), (gain, gain_out), (weight.at[2], now)]
    for age in range(2):
        copies.append((weight.at[age], past.at[:, pl.ds(age * channels, channels)]))
    copies = [
        pltpu.make_async_copy(source, target, sems.at[number])
        for number, (source, target) in enumerate(copies)
    ]
    for copy in copies:
        copy.start()
    for copy in copies:
        copy.wait()


def frame_kernel(cfg, *refs):
    refs = list(refs)
    groups = [refs.pop(0) for _ in range(cfg["groups"])]
    received = refs.pop(0) if cfg["came"] is not None else None
    partial, weight, bias, gain = refs[:4]
    refs = refs[4:]
    refs = refs[cfg["passing"] :]
    out = refs.pop(0) if cfg["sends"] else None
    spread = refs.pop(0 if cfg["later"] else -1)
    tails = [refs.pop(0) for _ in range(cfg["finals"])]
    refs = refs[cfg["keeps"] :]
    doubles = [refs.pop(0) for _ in range(cfg["doubles"])]
    entry = refs.pop(0)
    cols, window, segments = cfg["cols"], cfg["window"], cfg["segments"]
    channels = entry.shape[-1]
    half = lax.axis_index("band") // cfg["per_half"]

    def run(unit):
        have = window - unit
        need = have - 1
        size = have * cols
        if unit == 0:
            step = entry.shape[0] // TAPS

            def place(piece, code):
                number = (code >> (2 * lax.axis_index("band"))) & 3
                entry[pl.ds(pl.multiple_of(number * step, step), step), :] = piece[cfg["piece_at"]]

            *others, own, crossed = groups[:4]
            first, *rest = cfg["places"]
            near = lax.axis_index("tm") == cfg["near"]
            pl.when(near)(functools.partial(place, own, first))
            pl.when(jnp.logical_not(near))(functools.partial(place, crossed, first))
            for piece, code in zip(others, rest):
                place(piece, code)
            source, skip = entry, 0
        else:
            source, skip = received, half * (unit - 1 - cfg["came"])
        wide = source[rows_at(skip, have, cols), :].astype(jnp.float32)
        meansq = jnp.sum(wide * wide, axis=-1, keepdims=True) * (1.0 / channels)
        normed = wide * lax.rsqrt(meansq + 1e-06) * gain[...]
        ready = normed / (1.0 + jnp.exp(-normed))
        column = lax.broadcasted_iota(jnp.int32, ready.shape, 0) & (cols - 1)
        before = jnp.where(column == 0, 0.0, pltpu.roll(ready, 1, 0))
        after = jnp.where(column == cols - 1, 0.0, pltpu.roll(ready, size - 1, 0))
        edge = jnp.zeros((cols, TAPS * channels), jnp.bfloat16)
        spread[pl.ds(0, cols), :] = edge
        spread[pl.ds(size + cols, cols), :] = edge
        for number, value in enumerate((before, ready, after)):
            spread[pl.ds(cols, size), pl.ds(number * channels, channels)] = value.astype(jnp.bfloat16)
        kept = source[rows_at(skip + half, need, cols), :].astype(jnp.float32)
        total = partial[pl.ds(0, need * cols), :] + kept + bias[...]
        total += jnp.dot(taps(spread, half, need, cols), weight[...], preferred_element_type=jnp.float32)
        value = total.astype(jnp.bfloat16)
        if unit < segments - 1:
            out[rows_at(half * (unit - cfg["lowest"]), need, cols), :] = value
        else:
            length = value.shape[0] // len(tails)
            for number, tail in enumerate(tails):
                tail[cfg["tail_at"]] = value[number * length : (number + 1) * length]
            for double, tail in zip(doubles, tails):
                double[...] = tail[...]

    for unit in cfg["units"]:
        pl.when(on_unit(unit, cfg["holders"]))(functools.partial(run, unit))


def history_kernel(cfg, spread, near, far, weight, near_out, far_out):
    cols, window = cfg["cols"], cfg["window"]
    channels = near.shape[-1]
    half = lax.axis_index("band") // cfg["per_half"]

    def run(unit):
        need = window - unit - 1
        here = pl.ds(0, need * cols)
        ready = taps(spread, half, need, cols)
        if unit in cfg["ending"]:
            total = jnp.dot(ready, weight[:, channels:], preferred_element_type=jnp.float32)
            near_out[here, :] = far[here, :] + total
        else:
            total = jnp.dot(ready, weight[...], preferred_element_type=jnp.float32)
            near_out[here, :] = far[here, :] + total[:, channels:]
            far_out[here, :] = total[:, :channels]

    for unit in cfg["later"]:
        pl.when(on_unit(unit, cfg["holders"]))(functools.partial(run, unit))


def local(features, conv_weight, conv_bias, norm_gain):
    times, segments, bands = (lax.axis_size(name) for name in MESH_AXES)
    time, position, band = (lax.axis_index(name) for name in MESH_AXES)
    clips, own_frames, own_rows, cols, channels = features.shape
    frames = own_frames * times
    per_half = bands // HALVES
    window = own_rows * bands // HALVES + segments
    holders = clips // per_half
    piece = own_rows * cols
    assert clips == segments == bands == 4 == 2 * per_half and holders == 2 <= times and window == TAPS * own_rows

    def stream(clip, half):
        return clip // per_half, half * per_half + clip % per_half

    def spot(t, s, b):
        return (t * segments + s) * bands + b

    own, *sources = pl.pallas_call(
        functools.partial(pick_kernel, holders),
        out_shape=[pltpu.VMEM((own_frames, piece, channels), features.dtype)] * 4,
        in_specs=[whole(pltpu.HBM)],
        out_specs=[whole()] * 4,
        scratch_shapes=[pltpu.SemaphoreType.DMA((4,))],
        compiler_params=pltpu.CompilerParams(vmem_limit_bytes=1 << 20),
        name="pick",
    )(pltpu.with_memory_space_constraint(features.reshape(clips, own_frames, piece, channels), pltpu.HBM))
    wanted = [[2 * h + j for h in range(HALVES) for j in range(per_half)], [2, 0, 1, 2], [1, 2, 3, 1]]
    places = [sum((b - at // per_half) << (2 * at) for at, b in enumerate(row)) for row in wanted]

    def gather(number, members):
        routes = []
        for t, clip in members:
            side, (there, lane) = t if t < holders else 0, divmod(clip, per_half)
            if number == 0:
                segment = t if t < holders else 1
            elif there == side:
                segment = 3 if lane == number - 1 else 0
            else:
                segment = 1 + lane
            for h in range(HALVES):
                at = stream(clip, h)[1]
                source = wanted[number][at]
                assert clip == sent_clips(side, source & 1, segment, lambda a, b, c: b if a else c)[number]
                routes.append((spot(t, segment, source), spot(there, 0, at)))
        assert len({a for a, _ in routes}) == len({b for _, b in routes}) == len(routes)
        return lax.ppermute(sources[number], MESH_AXES, routes)

    def far_side(t):
        return [(t, clip) for clip in range(clips) if clip // per_half != (t if t < holders else 0)]

    entries = []
    for t in range(times):
        others = [gather(number, [(t, clip) for clip in range(clips)]) for number in (1, 2)]
        if t == 0:
            crossed = gather(0, [member for side in range(holders) for member in far_side(side)])
        if t < holders:
            entries.append(others + [own, crossed] + (entries[0][:2] if t else []))
        else:
            routes = [(spot(t, 0, b), spot(0, 0, b)) for b in range(bands)]
            entries.append(others + [lax.ppermute(own, MESH_AXES, routes), gather(0, far_side(t))])

    stored = [conv_weight[0].reshape(TAPS, TAPS * TAPS * channels, channels), conv_bias, norm_gain]
    now, past, bias, gain = pl.pallas_call(
        loader_kernel,
        out_shape=[
            pltpu.VMEM((TAPS * TAPS * channels, channels), stored[0].dtype),
            pltpu.VMEM((TAPS * TAPS * channels, 2 * channels), stored[0].dtype),
            pltpu.VMEM(conv_bias.shape, conv_bias.dtype),
            pltpu.VMEM(norm_gain.shape, norm_gain.dtype),
        ],
        in_specs=[whole(pltpu.HBM)] * 3,
        out_specs=[whole()] * 4,
        scratch_shapes=[pltpu.SemaphoreType.DMA((5,))],
        compiler_params=pltpu.CompilerParams(vmem_limit_bytes=1 << 20),
        name="loader",
    )(*[pltpu.with_memory_space_constraint(value, pltpu.HBM) for value in stored])
    now, past, bias, gain = (resident(value) for value in (now, past, bias, gain))

    def leave(value, there, index, group):
        routes = []
        for clip in group:
            for h in range(HALVES):
                t, b = stream(clip, h)
                routes.append((spot(t, segments - 1, b), spot(there, clip, h * per_half + index)))
        return lax.ppermute(value, MESH_AXES, routes)

    state = ((window - 1) * cols, channels)
    near = jnp.zeros(state, jnp.float32)
    far = jnp.zeros(state, jnp.float32)
    lag = min(frames, DEPTH)
    slots = frames + lag * (segments - 1)
    moving = {}
    tails = []
    waiting = []
    landed = {}
    for slot in range(slots):
        units = working(slot, frames, segments, lag)
        senders_now = [s for s in units if s < segments - 1]
        last = slot - lag * (segments - 1)
        finals = per_half if last >= 0 else 0
        middle = finals and last % own_frames > 0
        closing = slot + 1 == slots
        old = [key for key, (_, since) in landed.items() if closing and since < slot - 1]
        keeps = len(old) + len(waiting)
        doubles = finals if finals and not closing and last % own_frames == own_frames - 1 else 0
        cfg = dict(
            units=units,
            later=[s for s in units if slot - lag * s < frames - 1],
            ending=[s for s in units if slot - lag * s == frames - 2],
            sends=bool(senders_now),
            lowest=min(senders_now, default=0),
            groups=len(entries[slot // own_frames]) if slot < frames else 0,
            places=places,
            piece_at=slot % own_frames,
            near=slot // own_frames if slot // own_frames < holders else 0,
            came=min(working(slot - lag, frames, segments, lag)) if slot >= lag else None,
            finals=finals,
            tail_at=last % own_frames,
            passing=(finals if middle else 0) + keeps,
            keeps=keeps,
            doubles=doubles,
            cols=cols,
            window=window,
            segments=segments,
                        per_half=per_half,
            holders=holders,
        )
        operands = []
        if slot < frames:
            operands += [resident(value) for value in entries[slot // own_frames]]
        if slot >= lag:
            operands.append(resident(moving.pop(slot - lag)))
        operands += [resident(near), now, bias, gain]
        shapes = []
        if cfg["sends"]:
            shapes.append(pltpu.VMEM(((window - 1 - cfg["lowest"]) * cols, channels), jnp.bfloat16))
        wide = pltpu.VMEM(((window + 2) * cols, TAPS * channels), jnp.bfloat16)
        if cfg["later"]:
            shapes.append(wide)
        shape = pltpu.VMEM((own_frames, piece, channels), jnp.bfloat16)
        aliases = {}
        if middle:
            for index, value in enumerate(tails):
                aliases[len(operands)] = len(shapes) + index
                operands.append(resident(value))
        shapes += [shape] * finals
        for value in [landed[key][0] for key in old] + [value for _, _, value in waiting]:
            aliases[len(operands)] = len(shapes)
            operands.append(resident(value))
            shapes.append(shape)
        shapes += [shape] * doubles
        results = list(
            pl.pallas_call(
                functools.partial(frame_kernel, cfg),
                out_shape=shapes,
                in_specs=[whole()] * len(operands),
                out_specs=[whole()] * len(shapes),
                scratch_shapes=[pltpu.VMEM((window * cols, channels), jnp.bfloat16)] + ([] if cfg["later"] else [wide]),
                input_output_aliases=aliases,
                compiler_params=pltpu.CompilerParams(vmem_limit_bytes=VMEM_LIMIT),
                cost_estimate=pl.CostEstimate(flops=0, transcendentals=0, bytes_accessed=1 << 10),
                name="frame",
            )(*operands)
        )
        out = results.pop(0) if cfg["sends"] else None
        spread = results.pop(0) if cfg["later"] else None
        tails = results[:finals]
        if cfg["sends"]:
            moving[slot] = lax.ppermute(out, "segment", [(s, s + 1) for s in senders_now])
        kept = results[finals:]
        for key, value in zip(old, kept):
            landed[key] = (value, slot)
        for (there, index, _), value in zip(waiting, kept[len(old) :]):
            landed[there, index, 1] = (leave(value, there, index, range(per_half, clips)), slot)
        waiting = []
        if finals and last % own_frames == own_frames - 1:
            there = last // own_frames
            if not closing:
                waiting = [(there, index, value) for index, value in enumerate(kept[keeps:])]
            for index, value in enumerate(tails):
                group = range(clips if closing else per_half)
                landed[there, index, 0] = (leave(value, there, index, group), slot)
        if cfg["later"]:
            near, far = pl.pallas_call(
                functools.partial(history_kernel, cfg),
                out_shape=[pltpu.VMEM(state, jnp.float32)] * 2,
                in_specs=[whole()] * 4,
                out_specs=[whole()] * 2,
                input_output_aliases={1: 0, 2: 1},
                compiler_params=pltpu.CompilerParams(vmem_limit_bytes=VMEM_LIMIT),
                cost_estimate=pl.CostEstimate(flops=0, transcendentals=0, bytes_accessed=1 << 10),
                name="history",
            )(resident(spread), resident(near), resident(far), past)

    result = None
    for (t, index, late), (value, _) in landed.items():
        here = jnp.logical_and(time == t, band % per_half == index)
        if t < times - 1:
            here = jnp.logical_and(here, (position >= per_half) == bool(late))
        result = value if result is None else jnp.where(here, value, result)
    return result.reshape(1, own_frames, own_rows, cols, channels)


def solution(mesh):
    return jax.shard_map(
        local,
        mesh=mesh,
        in_specs=(
            P(None, "tm", "band", None, None),
            P("segment", None, None, None),
            P("segment", None),
            P("segment", None),
        ),
        out_specs=P("segment", "tm", "band", None, None),
        check_vma=False,
    )
```

```python
import functools

import jax
import jax.numpy as jnp
from jax import lax
from jax.experimental import pallas as pl
from jax.experimental.pallas import tpu as pltpu
from jax.sharding import PartitionSpec as P

HALVES = 2
DEPTH = 4
TAPS = 3
VMEM_LIMIT = 24 << 20
MESH_AXES = ("tm", "segment", "band")


def whole(space=pltpu.VMEM):
    return pl.BlockSpec(memory_space=space)


def resident(value):
    return pltpu.with_memory_space_constraint(value, pltpu.VMEM)


def working(slot, frames, segments, lag):
    return [s for s in range(segments) if 0 <= slot - lag * s < frames]


def on_unit(unit, holders):
    here = lax.axis_index("segment") == unit
    if holders < lax.axis_size("tm"):
        here = jnp.logical_and(here, lax.axis_index("tm") < holders)
    return here


def rows_at(start, count, cols):
    return pl.ds(pl.multiple_of(start * cols, cols), count * cols)


def sent_clips(side, lane, segment, choose):
    near, far = 2 * side, 2 - 2 * side
    behind = far + ((segment - 1) & 1)
    return (
        choose(segment == 0, near, far) + 1 - lane,
        choose(side == 0, behind, far + 1 - lane),
        far + lane,
        choose(segment == 3, near, near + 1),
        choose(segment == 0, near + 1 - lane, behind),
    )


def pick_kernel(holders, source, *refs):
    targets, sems = refs[:-1], refs[-1]
    time = lax.axis_index("tm")
    side = jnp.where(time < holders, time, 0)
    lane = lax.axis_index("band") & 1
    clips = (*sent_clips(side, lane, lax.axis_index("segment"), jnp.where), 2 * side + lane)
    copies = [
        pltpu.make_async_copy(source.at[clip], target, sems.at[number])
        for number, (clip, target) in enumerate(zip(clips, targets))
    ]
    for copy in copies:
        copy.start()
    for copy in copies:
        copy.wait()


def taps(spread, start, count, cols):
    return jnp.concatenate([spread[rows_at(start + row, count, cols), :] for row in range(TAPS)], axis=1)


def loader_kernel(weight, bias, gain, now, past, bias_out, gain_out, sems):
    channels = weight.shape[-1]
    copies = [(bias, bias_out), (gain, gain_out), (weight.at[2], now)]
    for age in range(2):
        copies.append((weight.at[age], past.at[:, pl.ds(age * channels, channels)]))
    copies = [
        pltpu.make_async_copy(source, target, sems.at[number])
        for number, (source, target) in enumerate(copies)
    ]
    for copy in copies:
        copy.start()
    for copy in copies:
        copy.wait()


def frame_kernel(cfg, *refs):
    refs = list(refs)
    groups = [refs.pop(0) for _ in range(cfg["groups"])]
    received = refs.pop(0) if cfg["came"] is not None else None
    partial, weight, bias, gain = refs[:4]
    refs = refs[4:]
    refs = refs[cfg["passing"] :]
    out = refs.pop(0) if cfg["sends"] else None
    spread = refs.pop(0 if cfg["later"] else -1)
    tails = [refs.pop(0) for _ in range(cfg["finals"])]
    refs = refs[cfg["keeps"] :]
    doubles = [refs.pop(0) for _ in range(cfg["doubles"])]
    entry = refs.pop(0)
    cols, window, segments = cfg["cols"], cfg["window"], cfg["segments"]
    channels = entry.shape[-1]
    half = lax.axis_index("band") // cfg["per_half"]

    def run(unit):
        have = window - unit
        need = have - 1
        size = have * cols
        if unit == 0:
            step = entry.shape[0] // TAPS

            def place(piece, code):
                number = (code >> (2 * lax.axis_index("band"))) & 3
                entry[pl.ds(pl.multiple_of(number * step, step), step), :] = piece[cfg["piece_at"]]

            near = lax.axis_index("tm") == cfg["near"]
            for here, chosen in zip((near, jnp.logical_not(near)), cfg["chosen"]):

                @pl.when(here)
                def _():
                    for number, code in zip(chosen, cfg["places"]):
                        place(groups[number], code)

            source, skip = entry, 0
        else:
            source, skip = received, half * (unit - 1 - cfg["came"])
        wide = source[rows_at(skip, have, cols), :].astype(jnp.float32)
        meansq = jnp.sum(wide * wide, axis=-1, keepdims=True) * (1.0 / channels)
        normed = wide * lax.rsqrt(meansq + 1e-06) * gain[...]
        ready = normed / (1.0 + jnp.exp(-normed))
        column = lax.broadcasted_iota(jnp.int32, ready.shape, 0) & (cols - 1)
        before = jnp.where(column == 0, 0.0, pltpu.roll(ready, 1, 0))
        after = jnp.where(column == cols - 1, 0.0, pltpu.roll(ready, size - 1, 0))
        edge = jnp.zeros((cols, TAPS * channels), jnp.bfloat16)
        spread[pl.ds(0, cols), :] = edge
        spread[pl.ds(size + cols, cols), :] = edge
        for number, value in enumerate((before, ready, after)):
            spread[pl.ds(cols, size), pl.ds(number * channels, channels)] = value.astype(jnp.bfloat16)
        kept = source[rows_at(skip + half, need, cols), :].astype(jnp.float32)
        total = partial[pl.ds(0, need * cols), :] + kept + bias[...]
        total += jnp.dot(taps(spread, half, need, cols), weight[...], preferred_element_type=jnp.float32)
        value = total.astype(jnp.bfloat16)
        if unit < segments - 1:
            out[rows_at(half * (unit - cfg["lowest"]), need, cols), :] = value
        else:
            length = value.shape[0] // len(tails)
            for number, tail in enumerate(tails):
                tail[cfg["tail_at"]] = value[number * length : (number + 1) * length]
            for double, tail in zip(doubles, tails):
                double[...] = tail[...]

    for unit in cfg["units"]:
        pl.when(on_unit(unit, cfg["holders"]))(functools.partial(run, unit))


def history_kernel(cfg, spread, near, far, weight, near_out, far_out):
    cols, window = cfg["cols"], cfg["window"]
    channels = near.shape[-1]
    half = lax.axis_index("band") // cfg["per_half"]

    def run(unit):
        need = window - unit - 1
        here = pl.ds(0, need * cols)
        ready = taps(spread, half, need, cols)
        if unit in cfg["ending"]:
            total = jnp.dot(ready, weight[:, channels:], preferred_element_type=jnp.float32)
            near_out[here, :] = far[here, :] + total
        else:
            total = jnp.dot(ready, weight[...], preferred_element_type=jnp.float32)
            near_out[here, :] = far[here, :] + total[:, channels:]
            far_out[here, :] = total[:, :channels]

    for unit in cfg["later"]:
        pl.when(on_unit(unit, cfg["holders"]))(functools.partial(run, unit))


def local(features, conv_weight, conv_bias, norm_gain):
    times, segments, bands = (lax.axis_size(name) for name in MESH_AXES)
    time, position, band = (lax.axis_index(name) for name in MESH_AXES)
    clips, own_frames, own_rows, cols, channels = features.shape
    frames = own_frames * times
    per_half = bands // HALVES
    window = own_rows * bands // HALVES + segments
    holders = clips // per_half
    piece = own_rows * cols
    assert clips == segments == bands == 4 == 2 * per_half and holders == 2 <= times and window == TAPS * own_rows

    def stream(clip, half):
        return clip // per_half, half * per_half + clip % per_half

    def spot(t, s, b):
        return (t * segments + s) * bands + b

    *sources, own = pl.pallas_call(
        functools.partial(pick_kernel, holders),
        out_shape=[pltpu.VMEM((own_frames, piece, channels), features.dtype)] * 6,
        in_specs=[whole(pltpu.HBM)],
        out_specs=[whole()] * 6,
        scratch_shapes=[pltpu.SemaphoreType.DMA((6,))],
        compiler_params=pltpu.CompilerParams(vmem_limit_bytes=1 << 20),
        name="pick",
    )(pltpu.with_memory_space_constraint(features.reshape(clips, own_frames, piece, channels), pltpu.HBM))
    wanted = [[0, 1, 2, 3], [1, 0, 3, 2], [2, 2, 1, 1]]
    places = [sum((b - at // per_half) << (2 * at) for at, b in enumerate(row)) for row in wanted]

    def gather(number, *members):
        routes = []
        for t, side, kind, froms in members:
            for lane in range(per_half):
                clip = side * per_half + lane
                for h in range(HALVES):
                    at = stream(clip, h)[1]
                    source, segment = wanted[kind][at], froms[lane]
                    sent = sent_clips(t if t < holders else 0, source & 1, segment, lambda a, b, c: b if a else c)
                    assert sent[number] == clip
                    routes.append((spot(t, segment, source), spot(side, 0, at)))
        assert len({a for a, _ in routes}) == len({b for _, b in routes}) == len(routes)
        return lax.ppermute(sources[number], MESH_AXES, routes)

    siblings = gather(0, (0, 0, 1, (0, 0)), (0, 1, 1, (1, 1)))
    thirds = gather(1, (0, 1, 2, (1, 2)), (1, 0, 1, (1, 1)))
    crossed = gather(2, (0, 1, 0, (0, 0)), (1, 0, 0, (1, 1)))
    nearest = gather(3, (0, 0, 2, (3, 2)), (1, 1, 2, (3, 2)))
    latest = gather(4, (1, 0, 2, (1, 2)), (1, 1, 1, (0, 0)))
    early = [siblings, thirds, crossed, nearest, own]
    entries = [(early, ((4, 0, 3), (2, 0, 1))), (early + [latest], ((4, 5, 3), (2, 1, 5)))]
    for t in range(holders, times):
        routes = [(spot(t, 0, b), spot(0, 0, b)) for b in range(bands)]
        group = [lax.ppermute(own, MESH_AXES, routes), gather(2, (t, 1, 0, (1, 1)))]
        group += [gather(0, (t, 0, 1, (0, 0)), (t, 1, 1, (1, 1)))]
        group += [gather(3, (t, 0, 2, (3, 2))), gather(1, (t, 1, 2, (1, 2)))]
        entries.append((group, ((0, 2, 3), (1, 2, 4))))

    stored = [conv_weight[0].reshape(TAPS, TAPS * TAPS * channels, channels), conv_bias, norm_gain]
    now, past, bias, gain = pl.pallas_call(
        loader_kernel,
        out_shape=[
            pltpu.VMEM((TAPS * TAPS * channels, channels), stored[0].dtype),
            pltpu.VMEM((TAPS * TAPS * channels, 2 * channels), stored[0].dtype),
            pltpu.VMEM(conv_bias.shape, conv_bias.dtype),
            pltpu.VMEM(norm_gain.shape, norm_gain.dtype),
        ],
        in_specs=[whole(pltpu.HBM)] * 3,
        out_specs=[whole()] * 4,
        scratch_shapes=[pltpu.SemaphoreType.DMA((5,))],
        compiler_params=pltpu.CompilerParams(vmem_limit_bytes=1 << 20),
        name="loader",
    )(*[pltpu.with_memory_space_constraint(value, pltpu.HBM) for value in stored])
    now, past, bias, gain = (resident(value) for value in (now, past, bias, gain))

    def leave(value, there, index, group):
        routes = []
        for clip in group:
            for h in range(HALVES):
                t, b = stream(clip, h)
                routes.append((spot(t, segments - 1, b), spot(there, clip, h * per_half + index)))
        return lax.ppermute(value, MESH_AXES, routes)

    state = ((window - 1) * cols, channels)
    near = jnp.zeros(state, jnp.float32)
    far = jnp.zeros(state, jnp.float32)
    lag = min(frames, DEPTH)
    slots = frames + lag * (segments - 1)
    moving = {}
    tails = []
    waiting = []
    landed = {}
    for slot in range(slots):
        units = working(slot, frames, segments, lag)
        senders_now = [s for s in units if s < segments - 1]
        last = slot - lag * (segments - 1)
        finals = per_half if last >= 0 else 0
        middle = finals and last % own_frames > 0
        closing = slot + 1 == slots
        old = [key for key, (_, since) in landed.items() if closing and since < slot - 1]
        keeps = len(old) + len(waiting)
        doubles = finals if finals and not closing and last % own_frames == own_frames - 1 else 0
        cfg = dict(
            units=units,
            later=[s for s in units if slot - lag * s < frames - 1],
            ending=[s for s in units if slot - lag * s == frames - 2],
            sends=bool(senders_now),
            lowest=min(senders_now, default=0),
            groups=len(entries[slot // own_frames][0]) if slot < frames else 0,
            chosen=entries[slot // own_frames][1] if slot < frames else (),
            places=places,
            piece_at=slot % own_frames,
            near=slot // own_frames if slot // own_frames < holders else 0,
            came=min(working(slot - lag, frames, segments, lag)) if slot >= lag else None,
            finals=finals,
            tail_at=last % own_frames,
            passing=(finals if middle else 0) + keeps,
            keeps=keeps,
            doubles=doubles,
            cols=cols,
            window=window,
            segments=segments,
                        per_half=per_half,
            holders=holders,
        )
        operands = []
        if slot < frames:
            operands += [resident(value) for value in entries[slot // own_frames][0]]
        if slot >= lag:
            operands.append(resident(moving.pop(slot - lag)))
        operands += [resident(near), now, bias, gain]
        shapes = []
        if cfg["sends"]:
            shapes.append(pltpu.VMEM(((window - 1 - cfg["lowest"]) * cols, channels), jnp.bfloat16))
        wide = pltpu.VMEM(((window + 2) * cols, TAPS * channels), jnp.bfloat16)
        if cfg["later"]:
            shapes.append(wide)
        shape = pltpu.VMEM((own_frames, piece, channels), jnp.bfloat16)
        aliases = {}
        if middle:
            for index, value in enumerate(tails):
                aliases[len(operands)] = len(shapes) + index
                operands.append(resident(value))
        shapes += [shape] * finals
        for value in [landed[key][0] for key in old] + [value for _, _, value in waiting]:
            aliases[len(operands)] = len(shapes)
            operands.append(resident(value))
            shapes.append(shape)
        shapes += [shape] * doubles
        results = list(
            pl.pallas_call(
                functools.partial(frame_kernel, cfg),
                out_shape=shapes,
                in_specs=[whole()] * len(operands),
                out_specs=[whole()] * len(shapes),
                scratch_shapes=[pltpu.VMEM((window * cols, channels), jnp.bfloat16)] + ([] if cfg["later"] else [wide]),
                input_output_aliases=aliases,
                compiler_params=pltpu.CompilerParams(vmem_limit_bytes=VMEM_LIMIT),
                cost_estimate=pl.CostEstimate(flops=0, transcendentals=0, bytes_accessed=1 << 10),
                name="frame",
            )(*operands)
        )
        out = results.pop(0) if cfg["sends"] else None
        spread = results.pop(0) if cfg["later"] else None
        tails = results[:finals]
        if cfg["sends"]:
            moving[slot] = lax.ppermute(out, "segment", [(s, s + 1) for s in senders_now])
        kept = results[finals:]
        for key, value in zip(old, kept):
            landed[key] = (value, slot)
        for (there, index, _), value in zip(waiting, kept[len(old) :]):
            landed[there, index, 1] = (leave(value, there, index, range(per_half, clips)), slot)
        waiting = []
        if finals and last % own_frames == own_frames - 1:
            there = last // own_frames
            if not closing:
                waiting = [(there, index, value) for index, value in enumerate(kept[keeps:])]
            for index, value in enumerate(tails):
                group = range(clips if closing else per_half)
                landed[there, index, 0] = (leave(value, there, index, group), slot)
        if cfg["later"]:
            near, far = pl.pallas_call(
                functools.partial(history_kernel, cfg),
                out_shape=[pltpu.VMEM(state, jnp.float32)] * 2,
                in_specs=[whole()] * 4,
                out_specs=[whole()] * 2,
                input_output_aliases={1: 0, 2: 1},
                compiler_params=pltpu.CompilerParams(vmem_limit_bytes=VMEM_LIMIT),
                cost_estimate=pl.CostEstimate(flops=0, transcendentals=0, bytes_accessed=1 << 10),
                name="history",
            )(resident(spread), resident(near), resident(far), past)

    result = None
    for (t, index, late), (value, _) in landed.items():
        here = jnp.logical_and(time == t, band % per_half == index)
        if t < times - 1:
            here = jnp.logical_and(here, (position >= per_half) == bool(late))
        result = value if result is None else jnp.where(here, value, result)
    return result.reshape(1, own_frames, own_rows, cols, channels)


def solution(mesh):
    return jax.shard_map(
        local,
        mesh=mesh,
        in_specs=(
            P(None, "tm", "band", None, None),
            P("segment", None, None, None),
            P("segment", None),
            P("segment", None),
        ),
        out_specs=P("segment", "tm", "band", None, None),
        check_vma=False,
    )
```

```python
import functools

import jax
import jax.numpy as jnp
from jax import lax
from jax.experimental import pallas as pl
from jax.experimental.pallas import tpu as pltpu
from jax.sharding import PartitionSpec as P

HALVES = 2
DEPTH = 4
TAPS = 3
VMEM_LIMIT = 24 << 20
MESH_AXES = ("tm", "segment", "band")


def whole(space=pltpu.VMEM):
    return pl.BlockSpec(memory_space=space)


def resident(value):
    return pltpu.with_memory_space_constraint(value, pltpu.VMEM)


def working(slot, frames, segments, lag):
    return [s for s in range(segments) if 0 <= slot - lag * s < frames]


def on_unit(unit, holders):
    here = lax.axis_index("segment") == unit
    if holders < lax.axis_size("tm"):
        here = jnp.logical_and(here, lax.axis_index("tm") < holders)
    return here


def rows_at(start, count, cols):
    return pl.ds(pl.multiple_of(start * cols, cols), count * cols)


def sent_clips(side, lane, segment, choose):
    near, far = 2 * side, 2 - 2 * side
    behind = far + ((segment - 1) & 1)
    return (
        far + lane,
        choose(segment == 0, near + 1, choose(segment == 3, near, behind)),
        choose(segment == 0, near, choose(segment == 3, near + 1, behind)),
    )


def pick_kernel(holders, source, own, across, second, third, sems):
    time = lax.axis_index("tm")
    side = jnp.where(time < holders, time, 0)
    lane = lax.axis_index("band") & 1
    clips = (2 * side + lane, *sent_clips(side, lane, lax.axis_index("segment"), jnp.where))
    copies = [
        pltpu.make_async_copy(source.at[clip], target, sems.at[number])
        for number, (clip, target) in enumerate(zip(clips, (own, across, second, third)))
    ]
    for copy in copies:
        copy.start()
    for copy in copies:
        copy.wait()


def taps(spread, start, count, cols):
    return jnp.concatenate([spread[rows_at(start + row, count, cols), :] for row in range(TAPS)], axis=1)


def loader_kernel(weight, bias, gain, now, past, bias_out, gain_out, sems):
    channels = weight.shape[-1]
    copies = [(bias, bias_out), (gain, gain_out), (weight.at[2], now)]
    for age in range(2):
        copies.append((weight.at[age], past.at[:, pl.ds(age * channels, channels)]))
    copies = [
        pltpu.make_async_copy(source, target, sems.at[number])
        for number, (source, target) in enumerate(copies)
    ]
    for copy in copies:
        copy.start()
    for copy in copies:
        copy.wait()


def frame_kernel(cfg, *refs):
    refs = list(refs)
    groups = [refs.pop(0) for _ in range(cfg["groups"])]
    received = refs.pop(0) if cfg["came"] is not None else None
    partial, weight, bias, gain = refs[:4]
    refs = refs[4:]
    refs = refs[cfg["passing"] :]
    out = refs.pop(0) if cfg["sends"] else None
    spread = refs.pop(0 if cfg["later"] else -1)
    tails = [refs.pop(0) for _ in range(cfg["finals"])]
    refs = refs[cfg["keeps"] :]
    doubles = [refs.pop(0) for _ in range(cfg["doubles"])]
    entry = refs.pop(0)
    cols, window, segments = cfg["cols"], cfg["window"], cfg["segments"]
    channels = entry.shape[-1]
    half = lax.axis_index("band") // cfg["per_half"]

    def run(unit):
        have = window - unit
        need = have - 1
        size = have * cols
        if unit == 0:
            step = entry.shape[0] // TAPS

            def place(piece, code):
                number = (code >> (2 * lax.axis_index("band"))) & 3
                entry[pl.ds(pl.multiple_of(number * step, step), step), :] = piece[cfg["piece_at"]]

            *others, own, crossed = groups[:4]
            first, *rest = cfg["places"]
            near = lax.axis_index("tm") == cfg["near"]
            pl.when(near)(functools.partial(place, own, first))
            pl.when(jnp.logical_not(near))(functools.partial(place, crossed, first))
            for piece, code in zip(others, rest):
                place(piece, code)
            source, skip = entry, 0
        else:
            source, skip = received, half * (unit - 1 - cfg["came"])
        wide = source[rows_at(skip, have, cols), :].astype(jnp.float32)
        meansq = jnp.sum(wide * wide, axis=-1, keepdims=True) * (1.0 / channels)
        normed = wide * lax.rsqrt(meansq + 1e-06) * gain[...]
        half_normed = 0.5 * normed
        ready = half_normed + half_normed * jnp.tanh(half_normed)
        column = lax.broadcasted_iota(jnp.int32, ready.shape, 0) & (cols - 1)
        before = jnp.where(column == 0, 0.0, pltpu.roll(ready, 1, 0))
        after = jnp.where(column == cols - 1, 0.0, pltpu.roll(ready, size - 1, 0))
        edge = jnp.zeros((cols, TAPS * channels), jnp.bfloat16)
        spread[pl.ds(0, cols), :] = edge
        spread[pl.ds(size + cols, cols), :] = edge
        for number, value in enumerate((before, ready, after)):
            spread[pl.ds(cols, size), pl.ds(number * channels, channels)] = value.astype(jnp.bfloat16)
        kept = source[rows_at(skip + half, need, cols), :].astype(jnp.float32)
        total = partial[pl.ds(0, need * cols), :] + kept + bias[...]
        total += jnp.dot(taps(spread, half, need, cols), weight[...], preferred_element_type=jnp.float32)
        value = total.astype(jnp.bfloat16)
        if unit < segments - 1:
            out[rows_at(half * (unit - cfg["lowest"]), need, cols), :] = value
        else:
            length = value.shape[0] // len(tails)
            for number, tail in enumerate(tails):
                tail[cfg["tail_at"]] = value[number * length : (number + 1) * length]
            for double, tail in zip(doubles, tails):
                double[...] = tail[...]

    for unit in cfg["units"]:
        pl.when(on_unit(unit, cfg["holders"]))(functools.partial(run, unit))


def history_kernel(cfg, spread, near, far, weight, near_out, far_out):
    cols, window = cfg["cols"], cfg["window"]
    channels = near.shape[-1]
    half = lax.axis_index("band") // cfg["per_half"]

    def run(unit):
        need = window - unit - 1
        here = pl.ds(0, need * cols)
        ready = taps(spread, half, need, cols)
        if unit in cfg["ending"]:
            total = jnp.dot(ready, weight[:, channels:], preferred_element_type=jnp.float32)
            near_out[here, :] = far[here, :] + total
        else:
            total = jnp.dot(ready, weight[...], preferred_element_type=jnp.float32)
            near_out[here, :] = far[here, :] + total[:, channels:]
            far_out[here, :] = total[:, :channels]

    for unit in cfg["later"]:
        pl.when(on_unit(unit, cfg["holders"]))(functools.partial(run, unit))


def local(features, conv_weight, conv_bias, norm_gain):
    times, segments, bands = (lax.axis_size(name) for name in MESH_AXES)
    time, position, band = (lax.axis_index(name) for name in MESH_AXES)
    clips, own_frames, own_rows, cols, channels = features.shape
    frames = own_frames * times
    per_half = bands // HALVES
    window = own_rows * bands // HALVES + segments
    holders = clips // per_half
    piece = own_rows * cols
    assert clips == segments == bands == 4 == 2 * per_half and holders == 2 <= times and window == TAPS * own_rows

    def stream(clip, half):
        return clip // per_half, half * per_half + clip % per_half

    def spot(t, s, b):
        return (t * segments + s) * bands + b

    own, *sources = pl.pallas_call(
        functools.partial(pick_kernel, holders),
        out_shape=[pltpu.VMEM((own_frames, piece, channels), features.dtype)] * 4,
        in_specs=[whole(pltpu.HBM)],
        out_specs=[whole()] * 4,
        scratch_shapes=[pltpu.SemaphoreType.DMA((4,))],
        compiler_params=pltpu.CompilerParams(vmem_limit_bytes=1 << 20),
        name="pick",
    )(pltpu.with_memory_space_constraint(features.reshape(clips, own_frames, piece, channels), pltpu.HBM))
    wanted = [[2 * h + j for h in range(HALVES) for j in range(per_half)], [2, 0, 1, 2], [1, 2, 3, 1]]
    places = [sum((b - at // per_half) << (2 * at) for at, b in enumerate(row)) for row in wanted]

    def gather(number, members):
        routes = []
        for t, clip in members:
            side, (there, lane) = t if t < holders else 0, divmod(clip, per_half)
            if number == 0:
                segment = t if t < holders else 1
            elif there == side:
                segment = 3 if lane == number - 1 else 0
            else:
                segment = 1 + lane
            for h in range(HALVES):
                at = stream(clip, h)[1]
                source = wanted[number][at]
                assert clip == sent_clips(side, source & 1, segment, lambda a, b, c: b if a else c)[number]
                routes.append((spot(t, segment, source), spot(there, 0, at)))
        assert len({a for a, _ in routes}) == len({b for _, b in routes}) == len(routes)
        return lax.ppermute(sources[number], MESH_AXES, routes)

    def far_side(t):
        return [(t, clip) for clip in range(clips) if clip // per_half != (t if t < holders else 0)]

    entries = []
    for t in range(times):
        others = [gather(number, [(t, clip) for clip in range(clips)]) for number in (1, 2)]
        if t == 0:
            crossed = gather(0, [member for side in range(holders) for member in far_side(side)])
        if t < holders:
            entries.append(others + [own, crossed] + (entries[0][:2] if t else []))
        else:
            routes = [(spot(t, 0, b), spot(0, 0, b)) for b in range(bands)]
            entries.append(others + [lax.ppermute(own, MESH_AXES, routes), gather(0, far_side(t))])

    stored = [conv_weight[0].reshape(TAPS, TAPS * TAPS * channels, channels), conv_bias, norm_gain]
    now, past, bias, gain = pl.pallas_call(
        loader_kernel,
        out_shape=[
            pltpu.VMEM((TAPS * TAPS * channels, channels), stored[0].dtype),
            pltpu.VMEM((TAPS * TAPS * channels, 2 * channels), stored[0].dtype),
            pltpu.VMEM(conv_bias.shape, conv_bias.dtype),
            pltpu.VMEM(norm_gain.shape, norm_gain.dtype),
        ],
        in_specs=[whole(pltpu.HBM)] * 3,
        out_specs=[whole()] * 4,
        scratch_shapes=[pltpu.SemaphoreType.DMA((5,))],
        compiler_params=pltpu.CompilerParams(vmem_limit_bytes=1 << 20),
        name="loader",
    )(*[pltpu.with_memory_space_constraint(value, pltpu.HBM) for value in stored])
    now, past, bias, gain = (resident(value) for value in (now, past, bias, gain))

    def leave(value, there, index, group):
        routes = []
        for clip in group:
            for h in range(HALVES):
                t, b = stream(clip, h)
                routes.append((spot(t, segments - 1, b), spot(there, clip, h * per_half + index)))
        return lax.ppermute(value, MESH_AXES, routes)

    state = ((window - 1) * cols, channels)
    near = jnp.zeros(state, jnp.float32)
    far = jnp.zeros(state, jnp.float32)
    lag = min(frames, DEPTH)
    slots = frames + lag * (segments - 1)
    moving = {}
    tails = []
    waiting = []
    landed = {}
    for slot in range(slots):
        units = working(slot, frames, segments, lag)
        senders_now = [s for s in units if s < segments - 1]
        last = slot - lag * (segments - 1)
        finals = per_half if last >= 0 else 0
        middle = finals and last % own_frames > 0
        closing = slot + 1 == slots
        old = [key for key, (_, since) in landed.items() if closing and since < slot - 1]
        keeps = len(old) + len(waiting)
        doubles = finals if finals and not closing and last % own_frames == own_frames - 1 else 0
        cfg = dict(
            units=units,
            later=[s for s in units if slot - lag * s < frames - 1],
            ending=[s for s in units if slot - lag * s == frames - 2],
            sends=bool(senders_now),
            lowest=min(senders_now, default=0),
            groups=len(entries[slot // own_frames]) if slot < frames else 0,
            places=places,
            piece_at=slot % own_frames,
            near=slot // own_frames if slot // own_frames < holders else 0,
            came=min(working(slot - lag, frames, segments, lag)) if slot >= lag else None,
            finals=finals,
            tail_at=last % own_frames,
            passing=(finals if middle else 0) + keeps,
            keeps=keeps,
            doubles=doubles,
            cols=cols,
            window=window,
            segments=segments,
                        per_half=per_half,
            holders=holders,
        )
        operands = []
        if slot < frames:
            operands += [resident(value) for value in entries[slot // own_frames]]
        if slot >= lag:
            operands.append(resident(moving.pop(slot - lag)))
        operands += [resident(near), now, bias, gain]
        shapes = []
        if cfg["sends"]:
            shapes.append(pltpu.VMEM(((window - 1 - cfg["lowest"]) * cols, channels), jnp.bfloat16))
        wide = pltpu.VMEM(((window + 2) * cols, TAPS * channels), jnp.bfloat16)
        if cfg["later"]:
            shapes.append(wide)
        shape = pltpu.VMEM((own_frames, piece, channels), jnp.bfloat16)
        aliases = {}
        if middle:
            for index, value in enumerate(tails):
                aliases[len(operands)] = len(shapes) + index
                operands.append(resident(value))
        shapes += [shape] * finals
        for value in [landed[key][0] for key in old] + [value for _, _, value in waiting]:
            aliases[len(operands)] = len(shapes)
            operands.append(resident(value))
            shapes.append(shape)
        shapes += [shape] * doubles
        results = list(
            pl.pallas_call(
                functools.partial(frame_kernel, cfg),
                out_shape=shapes,
                in_specs=[whole()] * len(operands),
                out_specs=[whole()] * len(shapes),
                scratch_shapes=[pltpu.VMEM((window * cols, channels), jnp.bfloat16)] + ([] if cfg["later"] else [wide]),
                input_output_aliases=aliases,
                compiler_params=pltpu.CompilerParams(vmem_limit_bytes=VMEM_LIMIT),
                cost_estimate=pl.CostEstimate(flops=0, transcendentals=0, bytes_accessed=1 << 10),
                name="frame",
            )(*operands)
        )
        out = results.pop(0) if cfg["sends"] else None
        spread = results.pop(0) if cfg["later"] else None
        tails = results[:finals]
        if cfg["sends"]:
            moving[slot] = lax.ppermute(out, "segment", [(s, s + 1) for s in senders_now])
        kept = results[finals:]
        for key, value in zip(old, kept):
            landed[key] = (value, slot)
        for (there, index, _), value in zip(waiting, kept[len(old) :]):
            landed[there, index, 1] = (leave(value, there, index, range(per_half, clips)), slot)
        waiting = []
        if finals and last % own_frames == own_frames - 1:
            there = last // own_frames
            if not closing:
                waiting = [(there, index, value) for index, value in enumerate(kept[keeps:])]
            for index, value in enumerate(tails):
                group = range(clips if closing else per_half)
                landed[there, index, 0] = (leave(value, there, index, group), slot)
        if cfg["later"]:
            near, far = pl.pallas_call(
                functools.partial(history_kernel, cfg),
                out_shape=[pltpu.VMEM(state, jnp.float32)] * 2,
                in_specs=[whole()] * 4,
                out_specs=[whole()] * 2,
                input_output_aliases={1: 0, 2: 1},
                compiler_params=pltpu.CompilerParams(vmem_limit_bytes=VMEM_LIMIT),
                cost_estimate=pl.CostEstimate(flops=0, transcendentals=0, bytes_accessed=1 << 10),
                name="history",
            )(resident(spread), resident(near), resident(far), past)

    result = None
    for (t, index, late), (value, _) in landed.items():
        here = jnp.logical_and(time == t, band % per_half == index)
        if t < times - 1:
            here = jnp.logical_and(here, (position >= per_half) == bool(late))
        result = value if result is None else jnp.where(here, value, result)
    return result.reshape(1, own_frames, own_rows, cols, channels)


def solution(mesh):
    return jax.shard_map(
        local,
        mesh=mesh,
        in_specs=(
            P(None, "tm", "band", None, None),
            P("segment", None, None, None),
            P("segment", None),
            P("segment", None),
        ),
        out_specs=P("segment", "tm", "band", None, None),
        check_vma=False,
    )
```

```python
import functools

import jax
import jax.numpy as jnp
from jax import lax
from jax.experimental import pallas as pl
from jax.experimental.pallas import tpu as pltpu
from jax.sharding import PartitionSpec as P

HALVES = 2
DEPTH = 4
TAPS = 3
VMEM_LIMIT = 24 << 20
MESH_AXES = ("tm", "segment", "band")


def whole(space=pltpu.VMEM):
    return pl.BlockSpec(memory_space=space)


def resident(value):
    return pltpu.with_memory_space_constraint(value, pltpu.VMEM)


def working(slot, frames, segments, lag):
    return [s for s in range(segments) if 0 <= slot - lag * s < frames]


def on_unit(unit, holders):
    here = lax.axis_index("segment") == unit
    if holders < lax.axis_size("tm"):
        here = jnp.logical_and(here, lax.axis_index("tm") < holders)
    return here


def rows_at(start, count, cols):
    return pl.ds(pl.multiple_of(start * cols, cols), count * cols)


def sent_clips(side, lane, segment, choose):
    near, far = 2 * side, 2 - 2 * side
    behind = far + ((segment - 1) & 1)
    return (
        choose(segment == 0, near, far) + 1 - lane,
        choose(side == 0, behind, far + 1 - lane),
        far + lane,
        choose(segment == 3, near, near + 1),
        choose(segment == 0, near + 1 - lane, behind),
    )


def pick_kernel(holders, source, *refs):
    targets, sems = refs[:-1], refs[-1]
    time = lax.axis_index("tm")
    side = jnp.where(time < holders, time, 0)
    lane = lax.axis_index("band") & 1
    clips = (*sent_clips(side, lane, lax.axis_index("segment"), jnp.where), 2 * side + lane)
    copies = [
        pltpu.make_async_copy(source.at[clip], target, sems.at[number])
        for number, (clip, target) in enumerate(zip(clips, targets))
    ]
    for copy in copies:
        copy.start()
    for copy in copies:
        copy.wait()


def taps(spread, start, count, cols):
    return jnp.concatenate([spread[rows_at(start + row, count, cols), :] for row in range(TAPS)], axis=1)


def loader_kernel(weight, bias, gain, now, past, bias_out, gain_out, sems):
    channels = weight.shape[-1]
    copies = [(bias, bias_out), (gain, gain_out), (weight.at[2], now)]
    for age in range(2):
        copies.append((weight.at[age], past.at[:, pl.ds(age * channels, channels)]))
    copies = [
        pltpu.make_async_copy(source, target, sems.at[number])
        for number, (source, target) in enumerate(copies)
    ]
    for copy in copies:
        copy.start()
    for copy in copies:
        copy.wait()


def frame_kernel(cfg, *refs):
    refs = list(refs)
    groups = [refs.pop(0) for _ in range(cfg["groups"])]
    received = refs.pop(0) if cfg["came"] is not None else None
    partial, weight, bias, gain = refs[:4]
    refs = refs[4:]
    refs = refs[cfg["passing"] :]
    out = refs.pop(0) if cfg["sends"] else None
    spread = refs.pop(0 if cfg["later"] else -1)
    tails = [refs.pop(0) for _ in range(cfg["finals"])]
    refs = refs[cfg["keeps"] :]
    doubles = [refs.pop(0) for _ in range(cfg["doubles"])]
    entry = refs.pop(0)
    cols, window, segments = cfg["cols"], cfg["window"], cfg["segments"]
    channels = entry.shape[-1]
    half = lax.axis_index("band") // cfg["per_half"]

    def run(unit):
        have = window - unit
        need = have - 1
        size = have * cols
        if unit == 0:
            step = entry.shape[0] // TAPS

            def place(piece, code):
                number = (code >> (2 * lax.axis_index("band"))) & 3
                entry[pl.ds(pl.multiple_of(number * step, step), step), :] = piece[cfg["piece_at"]]

            near = lax.axis_index("tm") == cfg["near"]
            for here, chosen in zip((near, jnp.logical_not(near)), cfg["chosen"]):

                @pl.when(here)
                def _():
                    for number, code in zip(chosen, cfg["places"]):
                        place(groups[number], code)

            source, skip = entry, 0
        else:
            source, skip = received, half * (unit - 1 - cfg["came"])
        wide = source[rows_at(skip, have, cols), :].astype(jnp.float32)
        meansq = jnp.sum(wide * wide, axis=-1, keepdims=True) * (1.0 / channels)
        normed = wide * lax.rsqrt(meansq + 1e-06) * gain[...]
        half_normed = 0.5 * normed
        ready = half_normed + half_normed * jnp.tanh(half_normed)
        column = lax.broadcasted_iota(jnp.int32, ready.shape, 0) & (cols - 1)
        before = jnp.where(column == 0, 0.0, pltpu.roll(ready, 1, 0))
        after = jnp.where(column == cols - 1, 0.0, pltpu.roll(ready, size - 1, 0))
        edge = jnp.zeros((cols, TAPS * channels), jnp.bfloat16)
        spread[pl.ds(0, cols), :] = edge
        spread[pl.ds(size + cols, cols), :] = edge
        for number, value in enumerate((before, ready, after)):
            spread[pl.ds(cols, size), pl.ds(number * channels, channels)] = value.astype(jnp.bfloat16)
        kept = source[rows_at(skip + half, need, cols), :].astype(jnp.float32)
        total = partial[pl.ds(0, need * cols), :] + kept + bias[...]
        total += jnp.dot(taps(spread, half, need, cols), weight[...], preferred_element_type=jnp.float32)
        value = total.astype(jnp.bfloat16)
        if unit < segments - 1:
            out[rows_at(half * (unit - cfg["lowest"]), need, cols), :] = value
        else:
            length = value.shape[0] // len(tails)
            for number, tail in enumerate(tails):
                tail[cfg["tail_at"]] = value[number * length : (number + 1) * length]
            for double, tail in zip(doubles, tails):
                double[...] = tail[...]

    for unit in cfg["units"]:
        pl.when(on_unit(unit, cfg["holders"]))(functools.partial(run, unit))


def history_kernel(cfg, spread, near, far, weight, near_out, far_out):
    cols, window = cfg["cols"], cfg["window"]
    channels = near.shape[-1]
    half = lax.axis_index("band") // cfg["per_half"]

    def run(unit):
        need = window - unit - 1
        here = pl.ds(0, need * cols)
        ready = taps(spread, half, need, cols)
        if unit in cfg["ending"]:
            total = jnp.dot(ready, weight[:, channels:], preferred_element_type=jnp.float32)
            near_out[here, :] = far[here, :] + total
        else:
            total = jnp.dot(ready, weight[...], preferred_element_type=jnp.float32)
            near_out[here, :] = far[here, :] + total[:, channels:]
            far_out[here, :] = total[:, :channels]

    for unit in cfg["later"]:
        pl.when(on_unit(unit, cfg["holders"]))(functools.partial(run, unit))


def local(features, conv_weight, conv_bias, norm_gain):
    times, segments, bands = (lax.axis_size(name) for name in MESH_AXES)
    time, position, band = (lax.axis_index(name) for name in MESH_AXES)
    clips, own_frames, own_rows, cols, channels = features.shape
    frames = own_frames * times
    per_half = bands // HALVES
    window = own_rows * bands // HALVES + segments
    holders = clips // per_half
    piece = own_rows * cols
    assert clips == segments == bands == 4 == 2 * per_half and holders == 2 <= times and window == TAPS * own_rows

    def stream(clip, half):
        return clip // per_half, half * per_half + clip % per_half

    def spot(t, s, b):
        return (t * segments + s) * bands + b

    *sources, own = pl.pallas_call(
        functools.partial(pick_kernel, holders),
        out_shape=[pltpu.VMEM((own_frames, piece, channels), features.dtype)] * 6,
        in_specs=[whole(pltpu.HBM)],
        out_specs=[whole()] * 6,
        scratch_shapes=[pltpu.SemaphoreType.DMA((6,))],
        compiler_params=pltpu.CompilerParams(vmem_limit_bytes=1 << 20),
        name="pick",
    )(pltpu.with_memory_space_constraint(features.reshape(clips, own_frames, piece, channels), pltpu.HBM))
    wanted = [[0, 1, 2, 3], [1, 0, 3, 2], [2, 2, 1, 1]]
    places = [sum((b - at // per_half) << (2 * at) for at, b in enumerate(row)) for row in wanted]

    def gather(number, *members):
        routes = []
        for t, side, kind, froms in members:
            for lane in range(per_half):
                clip = side * per_half + lane
                for h in range(HALVES):
                    at = stream(clip, h)[1]
                    source, segment = wanted[kind][at], froms[lane]
                    sent = sent_clips(t if t < holders else 0, source & 1, segment, lambda a, b, c: b if a else c)
                    assert sent[number] == clip
                    routes.append((spot(t, segment, source), spot(side, 0, at)))
        assert len({a for a, _ in routes}) == len({b for _, b in routes}) == len(routes)
        return lax.ppermute(sources[number], MESH_AXES, routes)

    siblings = gather(0, (0, 0, 1, (0, 0)), (0, 1, 1, (1, 1)))
    thirds = gather(1, (0, 1, 2, (1, 2)), (1, 0, 1, (1, 1)))
    crossed = gather(2, (0, 1, 0, (0, 0)), (1, 0, 0, (1, 1)))
    nearest = gather(3, (0, 0, 2, (3, 2)), (1, 1, 2, (3, 2)))
    latest = gather(4, (1, 0, 2, (1, 2)), (1, 1, 1, (0, 0)))
    early = [siblings, nearest, thirds, crossed, own]
    entries = [(early, ((4, 0, 1), (3, 0, 2))), (early + [latest], ((4, 5, 1), (3, 2, 5)))]
    for t in range(holders, times):
        routes = [(spot(t, 0, b), spot(0, 0, b)) for b in range(bands)]
        group = [lax.ppermute(own, MESH_AXES, routes), gather(2, (t, 1, 0, (1, 1)))]
        group += [gather(0, (t, 0, 1, (0, 0)), (t, 1, 1, (1, 1)))]
        group += [gather(3, (t, 0, 2, (3, 2))), gather(1, (t, 1, 2, (1, 2)))]
        entries.append((group, ((0, 2, 3), (1, 2, 4))))

    stored = [conv_weight[0].reshape(TAPS, TAPS * TAPS * channels, channels), conv_bias, norm_gain]
    now, past, bias, gain = pl.pallas_call(
        loader_kernel,
        out_shape=[
            pltpu.VMEM((TAPS * TAPS * channels, channels), stored[0].dtype),
            pltpu.VMEM((TAPS * TAPS * channels, 2 * channels), stored[0].dtype),
            pltpu.VMEM(conv_bias.shape, conv_bias.dtype),
            pltpu.VMEM(norm_gain.shape, norm_gain.dtype),
        ],
        in_specs=[whole(pltpu.HBM)] * 3,
        out_specs=[whole()] * 4,
        scratch_shapes=[pltpu.SemaphoreType.DMA((5,))],
        compiler_params=pltpu.CompilerParams(vmem_limit_bytes=1 << 20),
        name="loader",
    )(*[pltpu.with_memory_space_constraint(value, pltpu.HBM) for value in stored])
    now, past, bias, gain = (resident(value) for value in (now, past, bias, gain))

    def leave(value, there, index, group):
        routes = []
        for clip in group:
            for h in range(HALVES):
                t, b = stream(clip, h)
                routes.append((spot(t, segments - 1, b), spot(there, clip, h * per_half + index)))
        return lax.ppermute(value, MESH_AXES, routes)

    state = ((window - 1) * cols, channels)
    near = jnp.zeros(state, jnp.float32)
    far = jnp.zeros(state, jnp.float32)
    lag = min(frames, DEPTH)
    slots = frames + lag * (segments - 1)
    moving = {}
    tails = []
    waiting = []
    landed = {}
    for slot in range(slots):
        units = working(slot, frames, segments, lag)
        senders_now = [s for s in units if s < segments - 1]
        last = slot - lag * (segments - 1)
        finals = per_half if last >= 0 else 0
        middle = finals and last % own_frames > 0
        closing = slot + 1 == slots
        old = [key for key, (_, since) in landed.items() if closing and since < slot - 1]
        keeps = len(old) + len(waiting)
        doubles = finals if finals and not closing and last % own_frames == own_frames - 1 else 0
        cfg = dict(
            units=units,
            later=[s for s in units if slot - lag * s < frames - 1],
            ending=[s for s in units if slot - lag * s == frames - 2],
            sends=bool(senders_now),
            lowest=min(senders_now, default=0),
            groups=len(entries[slot // own_frames][0]) if slot < frames else 0,
            chosen=entries[slot // own_frames][1] if slot < frames else (),
            places=places,
            piece_at=slot % own_frames,
            near=slot // own_frames if slot // own_frames < holders else 0,
            came=min(working(slot - lag, frames, segments, lag)) if slot >= lag else None,
            finals=finals,
            tail_at=last % own_frames,
            passing=(finals if middle else 0) + keeps,
            keeps=keeps,
            doubles=doubles,
            cols=cols,
            window=window,
            segments=segments,
                        per_half=per_half,
            holders=holders,
        )
        operands = []
        if slot < frames:
            operands += [resident(value) for value in entries[slot // own_frames][0]]
        if slot >= lag:
            operands.append(resident(moving.pop(slot - lag)))
        operands += [resident(near), now, bias, gain]
        shapes = []
        if cfg["sends"]:
            shapes.append(pltpu.VMEM(((window - 1 - cfg["lowest"]) * cols, channels), jnp.bfloat16))
        wide = pltpu.VMEM(((window + 2) * cols, TAPS * channels), jnp.bfloat16)
        if cfg["later"]:
            shapes.append(wide)
        shape = pltpu.VMEM((own_frames, piece, channels), jnp.bfloat16)
        aliases = {}
        if middle:
            for index, value in enumerate(tails):
                aliases[len(operands)] = len(shapes) + index
                operands.append(resident(value))
        shapes += [shape] * finals
        for value in [landed[key][0] for key in old] + [value for _, _, value in waiting]:
            aliases[len(operands)] = len(shapes)
            operands.append(resident(value))
            shapes.append(shape)
        shapes += [shape] * doubles
        results = list(
            pl.pallas_call(
                functools.partial(frame_kernel, cfg),
                out_shape=shapes,
                in_specs=[whole()] * len(operands),
                out_specs=[whole()] * len(shapes),
                scratch_shapes=[pltpu.VMEM((window * cols, channels), jnp.bfloat16)] + ([] if cfg["later"] else [wide]),
                input_output_aliases=aliases,
                compiler_params=pltpu.CompilerParams(vmem_limit_bytes=VMEM_LIMIT),
                cost_estimate=pl.CostEstimate(flops=0, transcendentals=0, bytes_accessed=1 << 10),
                name="frame",
            )(*operands)
        )
        out = results.pop(0) if cfg["sends"] else None
        spread = results.pop(0) if cfg["later"] else None
        tails = results[:finals]
        if cfg["sends"]:
            moving[slot] = lax.ppermute(out, "segment", [(s, s + 1) for s in senders_now])
        kept = results[finals:]
        for key, value in zip(old, kept):
            landed[key] = (value, slot)
        for (there, index, _), value in zip(waiting, kept[len(old) :]):
            landed[there, index, 1] = (leave(value, there, index, range(per_half, clips)), slot)
        waiting = []
        if finals and last % own_frames == own_frames - 1:
            there = last // own_frames
            if not closing:
                waiting = [(there, index, value) for index, value in enumerate(kept[keeps:])]
            for index, value in enumerate(tails):
                group = range(clips if closing else per_half)
                landed[there, index, 0] = (leave(value, there, index, group), slot)
        if cfg["later"]:
            near, far = pl.pallas_call(
                functools.partial(history_kernel, cfg),
                out_shape=[pltpu.VMEM(state, jnp.float32)] * 2,
                in_specs=[whole()] * 4,
                out_specs=[whole()] * 2,
                input_output_aliases={1: 0, 2: 1},
                compiler_params=pltpu.CompilerParams(vmem_limit_bytes=VMEM_LIMIT),
                cost_estimate=pl.CostEstimate(flops=0, transcendentals=0, bytes_accessed=1 << 10),
                name="history",
            )(resident(spread), resident(near), resident(far), past)

    result = None
    for (t, index, late), (value, _) in landed.items():
        here = jnp.logical_and(time == t, band % per_half == index)
        if t < times - 1:
            here = jnp.logical_and(here, (position >= per_half) == bool(late))
        result = value if result is None else jnp.where(here, value, result)
    return result.reshape(1, own_frames, own_rows, cols, channels)


def solution(mesh):
    return jax.shard_map(
        local,
        mesh=mesh,
        in_specs=(
            P(None, "tm", "band", None, None),
            P("segment", None, None, None),
            P("segment", None),
            P("segment", None),
        ),
        out_specs=P("segment", "tm", "band", None, None),
        check_vma=False,
    )
```

```python
import functools

import jax
import jax.numpy as jnp
from jax import lax
from jax.experimental import pallas as pl
from jax.experimental.pallas import tpu as pltpu
from jax.sharding import PartitionSpec as P

HALVES = 2
DEPTH = 4
TAPS = 3
SUBLANES = 8
VMEM_LIMIT = 24 << 20
MESH_AXES = ("tm", "segment", "band")


def whole(space=pltpu.VMEM):
    return pl.BlockSpec(memory_space=space)


def resident(value):
    return pltpu.with_memory_space_constraint(value, pltpu.VMEM)


def working(slot, frames, segments, lag):
    return [s for s in range(segments) if 0 <= slot - lag * s < frames]


def on_unit(unit, holders):
    here = lax.axis_index("segment") == unit
    if holders < lax.axis_size("tm"):
        here = jnp.logical_and(here, lax.axis_index("tm") < holders)
    return here


def rows_at(start, count, cols):
    return pl.ds(pl.multiple_of(start * cols, cols), count * cols)


def sent_clips(side, lane, segment, choose):
    near, far = 2 * side, 2 - 2 * side
    behind = far + ((segment - 1) & 1)
    return (
        far + lane,
        choose(segment == 0, near + 1, choose(segment == 3, near, behind)),
        choose(segment == 0, near, choose(segment == 3, near + 1, behind)),
    )


def pick_kernel(holders, source, own, across, second, third, sems):
    time = lax.axis_index("tm")
    side = jnp.where(time < holders, time, 0)
    lane = lax.axis_index("band") & 1
    clips = (2 * side + lane, *sent_clips(side, lane, lax.axis_index("segment"), jnp.where))
    copies = [
        pltpu.make_async_copy(source.at[clip], target, sems.at[number])
        for number, (clip, target) in enumerate(zip(clips, (own, across, second, third)))
    ]
    for copy in copies:
        copy.start()
    for copy in copies:
        copy.wait()


def taps(spread, start, count, cols):
    return jnp.concatenate([spread[rows_at(start + row, count, cols), :] for row in range(TAPS)], axis=1)


def loader_kernel(weight, bias, gain, now, past, bias_out, gain_out, sems):
    channels = weight.shape[-1]
    copies = [(bias, bias_out), (gain, gain_out), (weight.at[2], now)]
    for age in range(2):
        copies.append((weight.at[age], past.at[:, pl.ds(age * channels, channels)]))
    copies = [
        pltpu.make_async_copy(source, target, sems.at[number])
        for number, (source, target) in enumerate(copies)
    ]
    for copy in copies:
        copy.start()
    for copy in copies:
        copy.wait()


def frame_kernel(cfg, *refs):
    refs = list(refs)
    groups = [refs.pop(0) for _ in range(cfg["groups"])]
    received = refs.pop(0) if cfg["came"] is not None else None
    partial, weight, bias, gain = refs[:4]
    refs = refs[4:]
    refs = refs[cfg["passing"] :]
    out = refs.pop(0) if cfg["sends"] else None
    spread = refs.pop(0 if cfg["later"] else -1)
    tails = [refs.pop(0) for _ in range(cfg["finals"])]
    refs = refs[cfg["keeps"] :]
    doubles = [refs.pop(0) for _ in range(cfg["doubles"])]
    entry, shifting = refs
    cols, window, segments = cfg["cols"], cfg["window"], cfg["segments"]
    channels = entry.shape[-1]
    half = lax.axis_index("band") // cfg["per_half"]

    def run(unit):
        have = window - unit
        need = have - 1
        size = have * cols
        if unit == 0:
            step = entry.shape[0] // TAPS

            def place(piece, code):
                number = (code >> (2 * lax.axis_index("band"))) & 3
                entry[pl.ds(pl.multiple_of(number * step, step), step), :] = piece[cfg["piece_at"]]

            *others, own, crossed = groups[:4]
            first, *rest = cfg["places"]
            near = lax.axis_index("tm") == cfg["near"]
            pl.when(near)(functools.partial(place, own, first))
            pl.when(jnp.logical_not(near))(functools.partial(place, crossed, first))
            for piece, code in zip(others, rest):
                place(piece, code)
            source, skip = entry, 0
        else:
            source, skip = received, half * (unit - 1 - cfg["came"])
        wide = source[rows_at(skip, have, cols), :].astype(jnp.float32)
        meansq = jnp.sum(wide * wide, axis=-1, keepdims=True) * (1.0 / channels)
        normed = wide * lax.rsqrt(meansq + 1e-06) * gain[...]
        half_normed = 0.5 * normed
        ready = half_normed + half_normed * jnp.tanh(half_normed)
        column = lax.broadcasted_iota(jnp.int32, ready.shape, 0) & (cols - 1)
        shifting[pl.ds(SUBLANES, size), :] = ready
        before = jnp.where(column == 0, 0.0, shifting[pl.ds(SUBLANES - 1, size), :])
        after = jnp.where(column == cols - 1, 0.0, shifting[pl.ds(SUBLANES + 1, size), :])
        edge = jnp.zeros((cols, TAPS * channels), jnp.bfloat16)
        spread[pl.ds(0, cols), :] = edge
        spread[pl.ds(size + cols, cols), :] = edge
        for number, value in enumerate((before, ready, after)):
            spread[pl.ds(cols, size), pl.ds(number * channels, channels)] = value.astype(jnp.bfloat16)
        kept = source[rows_at(skip + half, need, cols), :].astype(jnp.float32)
        total = partial[pl.ds(0, need * cols), :] + kept + bias[...]
        total += jnp.dot(taps(spread, half, need, cols), weight[...], preferred_element_type=jnp.float32)
        value = total.astype(jnp.bfloat16)
        if unit < segments - 1:
            out[rows_at(half * (unit - cfg["lowest"]), need, cols), :] = value
        else:
            length = value.shape[0] // len(tails)
            for number, tail in enumerate(tails):
                tail[cfg["tail_at"]] = value[number * length : (number + 1) * length]
            for double, tail in zip(doubles, tails):
                double[...] = tail[...]

    for unit in cfg["units"]:
        pl.when(on_unit(unit, cfg["holders"]))(functools.partial(run, unit))


def history_kernel(cfg, spread, near, far, weight, near_out, far_out):
    cols, window = cfg["cols"], cfg["window"]
    channels = near.shape[-1]
    half = lax.axis_index("band") // cfg["per_half"]

    def run(unit):
        need = window - unit - 1
        here = pl.ds(0, need * cols)
        ready = taps(spread, half, need, cols)
        if unit in cfg["ending"]:
            total = jnp.dot(ready, weight[:, channels:], preferred_element_type=jnp.float32)
            near_out[here, :] = far[here, :] + total
        else:
            total = jnp.dot(ready, weight[...], preferred_element_type=jnp.float32)
            near_out[here, :] = far[here, :] + total[:, channels:]
            far_out[here, :] = total[:, :channels]

    for unit in cfg["later"]:
        pl.when(on_unit(unit, cfg["holders"]))(functools.partial(run, unit))


def local(features, conv_weight, conv_bias, norm_gain):
    times, segments, bands = (lax.axis_size(name) for name in MESH_AXES)
    time, position, band = (lax.axis_index(name) for name in MESH_AXES)
    clips, own_frames, own_rows, cols, channels = features.shape
    frames = own_frames * times
    per_half = bands // HALVES
    window = own_rows * bands // HALVES + segments
    holders = clips // per_half
    piece = own_rows * cols
    assert clips == segments == bands == 4 == 2 * per_half and holders == 2 <= times and window == TAPS * own_rows

    def stream(clip, half):
        return clip // per_half, half * per_half + clip % per_half

    def spot(t, s, b):
        return (t * segments + s) * bands + b

    own, *sources = pl.pallas_call(
        functools.partial(pick_kernel, holders),
        out_shape=[pltpu.VMEM((own_frames, piece, channels), features.dtype)] * 4,
        in_specs=[whole(pltpu.HBM)],
        out_specs=[whole()] * 4,
        scratch_shapes=[pltpu.SemaphoreType.DMA((4,))],
        compiler_params=pltpu.CompilerParams(vmem_limit_bytes=1 << 20),
        name="pick",
    )(pltpu.with_memory_space_constraint(features.reshape(clips, own_frames, piece, channels), pltpu.HBM))
    wanted = [[2 * h + j for h in range(HALVES) for j in range(per_half)], [2, 0, 1, 2], [1, 2, 3, 1]]
    places = [sum((b - at // per_half) << (2 * at) for at, b in enumerate(row)) for row in wanted]

    def gather(number, members):
        routes = []
        for t, clip in members:
            side, (there, lane) = t if t < holders else 0, divmod(clip, per_half)
            if number == 0:
                segment = t if t < holders else 1
            elif there == side:
                segment = 3 if lane == number - 1 else 0
            else:
                segment = 1 + lane
            for h in range(HALVES):
                at = stream(clip, h)[1]
                source = wanted[number][at]
                assert clip == sent_clips(side, source & 1, segment, lambda a, b, c: b if a else c)[number]
                routes.append((spot(t, segment, source), spot(there, 0, at)))
        assert len({a for a, _ in routes}) == len({b for _, b in routes}) == len(routes)
        return lax.ppermute(sources[number], MESH_AXES, routes)

    def far_side(t):
        return [(t, clip) for clip in range(clips) if clip // per_half != (t if t < holders else 0)]

    entries = []
    for t in range(times):
        others = [gather(number, [(t, clip) for clip in range(clips)]) for number in (1, 2)]
        if t == 0:
            crossed = gather(0, [member for side in range(holders) for member in far_side(side)])
        if t < holders:
            entries.append(others + [own, crossed] + (entries[0][:2] if t else []))
        else:
            routes = [(spot(t, 0, b), spot(0, 0, b)) for b in range(bands)]
            entries.append(others + [lax.ppermute(own, MESH_AXES, routes), gather(0, far_side(t))])

    stored = [conv_weight[0].reshape(TAPS, TAPS * TAPS * channels, channels), conv_bias, norm_gain]
    now, past, bias, gain = pl.pallas_call(
        loader_kernel,
        out_shape=[
            pltpu.VMEM((TAPS * TAPS * channels, channels), stored[0].dtype),
            pltpu.VMEM((TAPS * TAPS * channels, 2 * channels), stored[0].dtype),
            pltpu.VMEM(conv_bias.shape, conv_bias.dtype),
            pltpu.VMEM(norm_gain.shape, norm_gain.dtype),
        ],
        in_specs=[whole(pltpu.HBM)] * 3,
        out_specs=[whole()] * 4,
        scratch_shapes=[pltpu.SemaphoreType.DMA((5,))],
        compiler_params=pltpu.CompilerParams(vmem_limit_bytes=1 << 20),
        name="loader",
    )(*[pltpu.with_memory_space_constraint(value, pltpu.HBM) for value in stored])
    now, past, bias, gain = (resident(value) for value in (now, past, bias, gain))

    def leave(value, there, index, group):
        routes = []
        for clip in group:
            for h in range(HALVES):
                t, b = stream(clip, h)
                routes.append((spot(t, segments - 1, b), spot(there, clip, h * per_half + index)))
        return lax.ppermute(value, MESH_AXES, routes)

    state = ((window - 1) * cols, channels)
    near = jnp.zeros(state, jnp.float32)
    far = jnp.zeros(state, jnp.float32)
    lag = min(frames, DEPTH)
    slots = frames + lag * (segments - 1)
    moving = {}
    tails = []
    waiting = []
    landed = {}
    for slot in range(slots):
        units = working(slot, frames, segments, lag)
        senders_now = [s for s in units if s < segments - 1]
        last = slot - lag * (segments - 1)
        finals = per_half if last >= 0 else 0
        middle = finals and last % own_frames > 0
        closing = slot + 1 == slots
        old = [key for key, (_, since) in landed.items() if closing and since < slot - 1]
        keeps = len(old) + len(waiting)
        doubles = finals if finals and not closing and last % own_frames == own_frames - 1 else 0
        cfg = dict(
            units=units,
            later=[s for s in units if slot - lag * s < frames - 1],
            ending=[s for s in units if slot - lag * s == frames - 2],
            sends=bool(senders_now),
            lowest=min(senders_now, default=0),
            groups=len(entries[slot // own_frames]) if slot < frames else 0,
            places=places,
            piece_at=slot % own_frames,
            near=slot // own_frames if slot // own_frames < holders else 0,
            came=min(working(slot - lag, frames, segments, lag)) if slot >= lag else None,
            finals=finals,
            tail_at=last % own_frames,
            passing=(finals if middle else 0) + keeps,
            keeps=keeps,
            doubles=doubles,
            cols=cols,
            window=window,
            segments=segments,
                        per_half=per_half,
            holders=holders,
        )
        operands = []
        if slot < frames:
            operands += [resident(value) for value in entries[slot // own_frames]]
        if slot >= lag:
            operands.append(resident(moving.pop(slot - lag)))
        operands += [resident(near), now, bias, gain]
        shapes = []
        if cfg["sends"]:
            shapes.append(pltpu.VMEM(((window - 1 - cfg["lowest"]) * cols, channels), jnp.bfloat16))
        wide = pltpu.VMEM(((window + 2) * cols, TAPS * channels), jnp.bfloat16)
        if cfg["later"]:
            shapes.append(wide)
        shape = pltpu.VMEM((own_frames, piece, channels), jnp.bfloat16)
        aliases = {}
        if middle:
            for index, value in enumerate(tails):
                aliases[len(operands)] = len(shapes) + index
                operands.append(resident(value))
        shapes += [shape] * finals
        for value in [landed[key][0] for key in old] + [value for _, _, value in waiting]:
            aliases[len(operands)] = len(shapes)
            operands.append(resident(value))
            shapes.append(shape)
        shapes += [shape] * doubles
        results = list(
            pl.pallas_call(
                functools.partial(frame_kernel, cfg),
                out_shape=shapes,
                in_specs=[whole()] * len(operands),
                out_specs=[whole()] * len(shapes),
                scratch_shapes=[
                    pltpu.VMEM((window * cols, channels), jnp.bfloat16),
                    pltpu.VMEM((window * cols + 2 * SUBLANES, channels), jnp.float32),
                ]
                + ([] if cfg["later"] else [wide]),
                input_output_aliases=aliases,
                compiler_params=pltpu.CompilerParams(vmem_limit_bytes=VMEM_LIMIT),
                cost_estimate=pl.CostEstimate(flops=0, transcendentals=0, bytes_accessed=1 << 10),
                name="frame",
            )(*operands)
        )
        out = results.pop(0) if cfg["sends"] else None
        spread = results.pop(0) if cfg["later"] else None
        tails = results[:finals]
        if cfg["sends"]:
            moving[slot] = lax.ppermute(out, "segment", [(s, s + 1) for s in senders_now])
        kept = results[finals:]
        for key, value in zip(old, kept):
            landed[key] = (value, slot)
        for (there, index, _), value in zip(waiting, kept[len(old) :]):
            landed[there, index, 1] = (leave(value, there, index, range(per_half, clips)), slot)
        waiting = []
        if finals and last % own_frames == own_frames - 1:
            there = last // own_frames
            if not closing:
                waiting = [(there, index, value) for index, value in enumerate(kept[keeps:])]
            for index, value in enumerate(tails):
                group = range(clips if closing else per_half)
                landed[there, index, 0] = (leave(value, there, index, group), slot)
        if cfg["later"]:
            near, far = pl.pallas_call(
                functools.partial(history_kernel, cfg),
                out_shape=[pltpu.VMEM(state, jnp.float32)] * 2,
                in_specs=[whole()] * 4,
                out_specs=[whole()] * 2,
                input_output_aliases={1: 0, 2: 1},
                compiler_params=pltpu.CompilerParams(vmem_limit_bytes=VMEM_LIMIT),
                cost_estimate=pl.CostEstimate(flops=0, transcendentals=0, bytes_accessed=1 << 10),
                name="history",
            )(resident(spread), resident(near), resident(far), past)

    result = None
    for (t, index, late), (value, _) in landed.items():
        here = jnp.logical_and(time == t, band % per_half == index)
        if t < times - 1:
            here = jnp.logical_and(here, (position >= per_half) == bool(late))
        result = value if result is None else jnp.where(here, value, result)
    return result.reshape(1, own_frames, own_rows, cols, channels)


def solution(mesh):
    return jax.shard_map(
        local,
        mesh=mesh,
        in_specs=(
            P(None, "tm", "band", None, None),
            P("segment", None, None, None),
            P("segment", None),
            P("segment", None),
        ),
        out_specs=P("segment", "tm", "band", None, None),
        check_vma=False,
    )
```

```python
import functools

import jax
import jax.numpy as jnp
from jax import lax
from jax.experimental import pallas as pl
from jax.experimental.pallas import tpu as pltpu
from jax.sharding import PartitionSpec as P

HALVES = 2
DEPTH = 4
TAPS = 3
VMEM_LIMIT = 24 << 20
MESH_AXES = ("tm", "segment", "band")


def whole(space=pltpu.VMEM):
    return pl.BlockSpec(memory_space=space)


def resident(value):
    return pltpu.with_memory_space_constraint(value, pltpu.VMEM)


def working(slot, frames, segments, lag):
    return [s for s in range(segments) if 0 <= slot - lag * s < frames]


def on_unit(unit, holders):
    here = lax.axis_index("segment") == unit
    if holders < lax.axis_size("tm"):
        here = jnp.logical_and(here, lax.axis_index("tm") < holders)
    return here


def rows_at(start, count, cols):
    return pl.ds(pl.multiple_of(start * cols, cols), count * cols)


def sent_clips(side, lane, segment, choose):
    near, far = 2 * side, 2 - 2 * side
    behind = far + ((segment - 1) & 1)
    return (
        far + lane,
        choose(segment == 0, near + 1, choose(segment == 3, near, behind)),
        choose(segment == 0, near, choose(segment == 3, near + 1, behind)),
    )


def pick_kernel(holders, source, own, across, second, third, sems):
    time = lax.axis_index("tm")
    side = jnp.where(time < holders, time, 0)
    lane = lax.axis_index("band") & 1
    clips = (2 * side + lane, *sent_clips(side, lane, lax.axis_index("segment"), jnp.where))
    copies = [
        pltpu.make_async_copy(source.at[clip], target, sems.at[number])
        for number, (clip, target) in enumerate(zip(clips, (own, across, second, third)))
    ]
    for copy in copies:
        copy.start()
    for copy in copies:
        copy.wait()


def taps(spread, start, count, cols):
    return jnp.concatenate([spread[rows_at(start + row, count, cols), :] for row in range(TAPS)], axis=1)


def loader_kernel(weight, bias, gain, now, past, bias_out, gain_out, sems):
    channels = weight.shape[-1]
    copies = [(bias, bias_out), (gain, gain_out), (weight.at[2], now)]
    for age in range(2):
        copies.append((weight.at[age], past.at[:, pl.ds(age * channels, channels)]))
    copies = [
        pltpu.make_async_copy(source, target, sems.at[number])
        for number, (source, target) in enumerate(copies)
    ]
    for copy in copies:
        copy.start()
    for copy in copies:
        copy.wait()


def frame_kernel(cfg, *refs):
    refs = list(refs)
    groups = [refs.pop(0) for _ in range(cfg["groups"])]
    received = refs.pop(0) if cfg["came"] is not None else None
    partial, weight, bias, gain = refs[:4]
    refs = refs[4:]
    refs = refs[cfg["passing"] :]
    out = refs.pop(0) if cfg["sends"] else None
    spread = refs.pop(0 if cfg["later"] else -1)
    tails = [refs.pop(0) for _ in range(cfg["finals"])]
    refs = refs[cfg["keeps"] :]
    doubles = [refs.pop(0) for _ in range(cfg["doubles"])]
    entry = refs.pop(0)
    cols, window, segments = cfg["cols"], cfg["window"], cfg["segments"]
    channels = entry.shape[-1]
    half = lax.axis_index("band") // cfg["per_half"]

    def run(unit):
        have = window - unit
        need = have - 1
        size = have * cols
        if unit == 0:
            step = entry.shape[0] // TAPS

            def place(piece, code):
                number = (code >> (2 * lax.axis_index("band"))) & 3
                entry[pl.ds(pl.multiple_of(number * step, step), step), :] = piece[cfg["piece_at"]]

            *others, own, crossed = groups[:4]
            first, *rest = cfg["places"]
            near = lax.axis_index("tm") == cfg["near"]
            pl.when(near)(functools.partial(place, own, first))
            pl.when(jnp.logical_not(near))(functools.partial(place, crossed, first))
            for piece, code in zip(others, rest):
                place(piece, code)
            source, skip = entry, 0
        else:
            source, skip = received, half * (unit - 1 - cfg["came"])
        wide = source[rows_at(skip, have, cols), :].astype(jnp.float32)
        meansq = jnp.sum(wide * wide, axis=-1, keepdims=True) * (1.0 / channels)
        normed = wide * lax.rsqrt(meansq + 1e-06) * gain[...]
        half_normed = 0.5 * normed
        ready = half_normed + half_normed * jnp.tanh(half_normed)
        column = lax.broadcasted_iota(jnp.int32, ready.shape, 0) & (cols - 1)
        before = jnp.where(column == 0, 0.0, pltpu.roll(ready, 1, 0))
        after = jnp.where(column == cols - 1, 0.0, pltpu.roll(ready, size - 1, 0))
        edge = jnp.zeros((cols, TAPS * channels), jnp.bfloat16)
        spread[pl.ds(0, cols), :] = edge
        spread[pl.ds(size + cols, cols), :] = edge
        for number, value in enumerate((before, ready, after)):
            spread[pl.ds(cols, size), pl.ds(number * channels, channels)] = value.astype(jnp.bfloat16)
        kept = source[rows_at(skip + half, need, cols), :].astype(jnp.float32)
        total = partial[pl.ds(0, need * cols), :] + kept + bias[...]
        total += jnp.dot(taps(spread, half, need, cols), weight[...], preferred_element_type=jnp.float32)
        value = total.astype(jnp.bfloat16)
        if unit < segments - 1:
            out[rows_at(half * (unit - cfg["lowest"]), need, cols), :] = value
        else:
            length = value.shape[0] // len(tails)
            for number, tail in enumerate(tails):
                tail[cfg["tail_at"]] = value[number * length : (number + 1) * length]
            if doubles:
                leads = lax.axis_index("tm") == 0
                for number, double in enumerate(doubles):
                    turned = tails[(number + 1) % len(tails)] if number == 0 else tails[number]
                    double[...] = jnp.where(leads, turned[...], tails[number][...])

    for unit in cfg["units"]:
        pl.when(on_unit(unit, cfg["holders"]))(functools.partial(run, unit))


def history_kernel(cfg, spread, near, far, weight, near_out, far_out):
    cols, window = cfg["cols"], cfg["window"]
    channels = near.shape[-1]
    half = lax.axis_index("band") // cfg["per_half"]

    def run(unit):
        need = window - unit - 1
        here = pl.ds(0, need * cols)
        ready = taps(spread, half, need, cols)
        if unit in cfg["ending"]:
            total = jnp.dot(ready, weight[:, channels:], preferred_element_type=jnp.float32)
            near_out[here, :] = far[here, :] + total
        else:
            total = jnp.dot(ready, weight[...], preferred_element_type=jnp.float32)
            near_out[here, :] = far[here, :] + total[:, channels:]
            far_out[here, :] = total[:, :channels]

    for unit in cfg["later"]:
        pl.when(on_unit(unit, cfg["holders"]))(functools.partial(run, unit))


def local(features, conv_weight, conv_bias, norm_gain):
    times, segments, bands = (lax.axis_size(name) for name in MESH_AXES)
    time, position, band = (lax.axis_index(name) for name in MESH_AXES)
    clips, own_frames, own_rows, cols, channels = features.shape
    frames = own_frames * times
    per_half = bands // HALVES
    window = own_rows * bands // HALVES + segments
    holders = clips // per_half
    piece = own_rows * cols
    assert clips == segments == bands == 4 == 2 * per_half and holders == 2 <= times and window == TAPS * own_rows

    def stream(clip, half):
        return clip // per_half, half * per_half + clip % per_half

    def spot(t, s, b):
        return (t * segments + s) * bands + b

    own, *sources = pl.pallas_call(
        functools.partial(pick_kernel, holders),
        out_shape=[pltpu.VMEM((own_frames, piece, channels), features.dtype)] * 4,
        in_specs=[whole(pltpu.HBM)],
        out_specs=[whole()] * 4,
        scratch_shapes=[pltpu.SemaphoreType.DMA((4,))],
        compiler_params=pltpu.CompilerParams(vmem_limit_bytes=1 << 20),
        name="pick",
    )(pltpu.with_memory_space_constraint(features.reshape(clips, own_frames, piece, channels), pltpu.HBM))
    wanted = [[2 * h + j for h in range(HALVES) for j in range(per_half)], [2, 0, 1, 2], [1, 2, 3, 1]]
    places = [sum((b - at // per_half) << (2 * at) for at, b in enumerate(row)) for row in wanted]

    def gather(number, members):
        routes = []
        for t, clip in members:
            side, (there, lane) = t if t < holders else 0, divmod(clip, per_half)
            if number == 0:
                segment = t if t < holders else 1
            elif there == side:
                segment = 3 if lane == number - 1 else 0
            else:
                segment = 1 + lane
            for h in range(HALVES):
                at = stream(clip, h)[1]
                source = wanted[number][at]
                assert clip == sent_clips(side, source & 1, segment, lambda a, b, c: b if a else c)[number]
                routes.append((spot(t, segment, source), spot(there, 0, at)))
        assert len({a for a, _ in routes}) == len({b for _, b in routes}) == len(routes)
        return lax.ppermute(sources[number], MESH_AXES, routes)

    def far_side(t):
        return [(t, clip) for clip in range(clips) if clip // per_half != (t if t < holders else 0)]

    entries = []
    for t in range(times):
        others = [gather(number, [(t, clip) for clip in range(clips)]) for number in (1, 2)]
        if t == 0:
            crossed = gather(0, [member for side in range(holders) for member in far_side(side)])
        if t < holders:
            entries.append(others + [own, crossed] + (entries[0][:2] if t else []))
        else:
            routes = [(spot(t, 0, b), spot(0, 0, b)) for b in range(bands)]
            entries.append(others + [lax.ppermute(own, MESH_AXES, routes), gather(0, far_side(t))])

    stored = [conv_weight[0].reshape(TAPS, TAPS * TAPS * channels, channels), conv_bias, norm_gain]
    now, past, bias, gain = pl.pallas_call(
        loader_kernel,
        out_shape=[
            pltpu.VMEM((TAPS * TAPS * channels, channels), stored[0].dtype),
            pltpu.VMEM((TAPS * TAPS * channels, 2 * channels), stored[0].dtype),
            pltpu.VMEM(conv_bias.shape, conv_bias.dtype),
            pltpu.VMEM(norm_gain.shape, norm_gain.dtype),
        ],
        in_specs=[whole(pltpu.HBM)] * 3,
        out_specs=[whole()] * 4,
        scratch_shapes=[pltpu.SemaphoreType.DMA((5,))],
        compiler_params=pltpu.CompilerParams(vmem_limit_bytes=1 << 20),
        name="loader",
    )(*[pltpu.with_memory_space_constraint(value, pltpu.HBM) for value in stored])
    now, past, bias, gain = (resident(value) for value in (now, past, bias, gain))

    def leave(value, there, *members):
        routes = []
        for index, group in members:
            for clip in group:
                for h in range(HALVES):
                    t, b = stream(clip, h)
                    routes.append((spot(t, segments - 1, b), spot(there, clip, h * per_half + index)))
        assert len({a for a, _ in routes}) == len({b for _, b in routes}) == len(routes)
        return lax.ppermute(value, MESH_AXES, routes)

    state = ((window - 1) * cols, channels)
    near = jnp.zeros(state, jnp.float32)
    far = jnp.zeros(state, jnp.float32)
    lag = min(frames, DEPTH)
    slots = frames + lag * (segments - 1)
    moving = {}
    tails = []
    waiting = []
    landed = {}
    for slot in range(slots):
        units = working(slot, frames, segments, lag)
        senders_now = [s for s in units if s < segments - 1]
        last = slot - lag * (segments - 1)
        finals = per_half if last >= 0 else 0
        middle = finals and last % own_frames > 0
        closing = slot + 1 == slots
        old = [key for key, (_, since) in landed.items() if closing and since < slot - 1]
        keeps = len(old) + len(waiting)
        doubles = finals if finals and not closing and last % own_frames == own_frames - 1 else 0
        cfg = dict(
            units=units,
            later=[s for s in units if slot - lag * s < frames - 1],
            ending=[s for s in units if slot - lag * s == frames - 2],
            sends=bool(senders_now),
            lowest=min(senders_now, default=0),
            groups=len(entries[slot // own_frames]) if slot < frames else 0,
            places=places,
            piece_at=slot % own_frames,
            near=slot // own_frames if slot // own_frames < holders else 0,
            came=min(working(slot - lag, frames, segments, lag)) if slot >= lag else None,
            finals=finals,
            tail_at=last % own_frames,
            passing=(finals if middle else 0) + keeps,
            keeps=keeps,
            doubles=doubles,
            cols=cols,
            window=window,
            segments=segments,
                        per_half=per_half,
            holders=holders,
        )
        operands = []
        if slot < frames:
            operands += [resident(value) for value in entries[slot // own_frames]]
        if slot >= lag:
            operands.append(resident(moving.pop(slot - lag)))
        operands += [resident(near), now, bias, gain]
        shapes = []
        if cfg["sends"]:
            shapes.append(pltpu.VMEM(((window - 1 - cfg["lowest"]) * cols, channels), jnp.bfloat16))
        wide = pltpu.VMEM(((window + 2) * cols, TAPS * channels), jnp.bfloat16)
        if cfg["later"]:
            shapes.append(wide)
        shape = pltpu.VMEM((own_frames, piece, channels), jnp.bfloat16)
        aliases = {}
        if middle:
            for index, value in enumerate(tails):
                aliases[len(operands)] = len(shapes) + index
                operands.append(resident(value))
        shapes += [shape] * finals
        for value in [landed[key][0] for key in old] + [value for _, _, value in waiting]:
            aliases[len(operands)] = len(shapes)
            operands.append(resident(value))
            shapes.append(shape)
        shapes += [shape] * doubles
        results = list(
            pl.pallas_call(
                functools.partial(frame_kernel, cfg),
                out_shape=shapes,
                in_specs=[whole()] * len(operands),
                out_specs=[whole()] * len(shapes),
                scratch_shapes=[pltpu.VMEM((window * cols, channels), jnp.bfloat16)] + ([] if cfg["later"] else [wide]),
                input_output_aliases=aliases,
                compiler_params=pltpu.CompilerParams(vmem_limit_bytes=VMEM_LIMIT),
                cost_estimate=pl.CostEstimate(flops=0, transcendentals=0, bytes_accessed=1 << 10),
                name="frame",
            )(*operands)
        )
        out = results.pop(0) if cfg["sends"] else None
        spread = results.pop(0) if cfg["later"] else None
        tails = results[:finals]
        if cfg["sends"]:
            moving[slot] = lax.ppermute(out, "segment", [(s, s + 1) for s in senders_now])
        kept = results[finals:]
        for key, value in zip(old, kept):
            landed[key] = (value, slot)
        ahead, behind = range(per_half), range(per_half, clips)
        if waiting:
            there, (shared, alone) = waiting[0][0], kept[len(old) : len(old) + per_half]
            both = leave(shared, there, (1, ahead), (0, behind))
            landed[there, 1, 0] = landed[there, 0, 1] = (both, slot)
            landed[there, 1, 1] = (leave(alone, there, (1, behind)), slot)
        waiting = []
        if finals and last % own_frames == own_frames - 1:
            there = last // own_frames
            if closing:
                for index, value in enumerate(tails):
                    landed[there, index, 0] = (leave(value, there, (index, range(clips))), slot)
            else:
                waiting = [(there, index, value) for index, value in enumerate(kept[keeps:])]
                landed[there, 0, 0] = (leave(tails[0], there, (0, ahead)), slot)
        if cfg["later"]:
            near, far = pl.pallas_call(
                functools.partial(history_kernel, cfg),
                out_shape=[pltpu.VMEM(state, jnp.float32)] * 2,
                in_specs=[whole()] * 4,
                out_specs=[whole()] * 2,
                input_output_aliases={1: 0, 2: 1},
                compiler_params=pltpu.CompilerParams(vmem_limit_bytes=VMEM_LIMIT),
                cost_estimate=pl.CostEstimate(flops=0, transcendentals=0, bytes_accessed=1 << 10),
                name="history",
            )(resident(spread), resident(near), resident(far), past)

    result = None
    for (t, index, late), (value, _) in landed.items():
        here = jnp.logical_and(time == t, band % per_half == index)
        if t < times - 1:
            here = jnp.logical_and(here, (position >= per_half) == bool(late))
        result = value if result is None else jnp.where(here, value, result)
    return result.reshape(1, own_frames, own_rows, cols, channels)


def solution(mesh):
    return jax.shard_map(
        local,
        mesh=mesh,
        in_specs=(
            P(None, "tm", "band", None, None),
            P("segment", None, None, None),
            P("segment", None),
            P("segment", None),
        ),
        out_specs=P("segment", "tm", "band", None, None),
        check_vma=False,
    )
```

```python
import functools

import jax
import jax.numpy as jnp
from jax import lax
from jax.experimental import pallas as pl
from jax.experimental.pallas import tpu as pltpu
from jax.sharding import PartitionSpec as P

HALVES = 2
DEPTH = 4
TAPS = 3
VMEM_LIMIT = 24 << 20
MESH_AXES = ("tm", "segment", "band")


def whole(space=pltpu.VMEM):
    return pl.BlockSpec(memory_space=space)


def resident(value):
    return pltpu.with_memory_space_constraint(value, pltpu.VMEM)


def working(slot, frames, segments, lag):
    return [s for s in range(segments) if 0 <= slot - lag * s < frames]


def on_unit(unit, holders):
    here = lax.axis_index("segment") == unit
    if holders < lax.axis_size("tm"):
        here = jnp.logical_and(here, lax.axis_index("tm") < holders)
    return here


def rows_at(start, count, cols):
    return pl.ds(pl.multiple_of(start * cols, cols), count * cols)


def sent_clips(side, lane, segment, choose):
    near, far = 2 * side, 2 - 2 * side
    behind = far + ((segment - 1) & 1)
    return (
        far + lane,
        choose(segment == 0, near + 1, choose(segment == 3, near, behind)),
        choose(segment == 0, near, choose(segment == 3, near + 1, behind)),
    )


def pick_kernel(holders, source, own, across, second, third, sems):
    time = lax.axis_index("tm")
    side = jnp.where(time < holders, time, 0)
    lane = lax.axis_index("band") & 1
    clips = (2 * side + lane, *sent_clips(side, lane, lax.axis_index("segment"), jnp.where))
    copies = [
        pltpu.make_async_copy(source.at[clip], target, sems.at[number])
        for number, (clip, target) in enumerate(zip(clips, (own, across, second, third)))
    ]
    for copy in copies:
        copy.start()
    for copy in copies:
        copy.wait()


def taps(spread, start, count, cols):
    return jnp.concatenate([spread[rows_at(start + row, count, cols), :] for row in range(TAPS)], axis=1)


def loader_kernel(weight, bias, gain, now, past, bias_out, gain_out, sems):
    channels = weight.shape[-1]
    copies = [(bias, bias_out), (gain, gain_out), (weight.at[2], now)]
    for age in range(2):
        copies.append((weight.at[age], past.at[:, pl.ds(age * channels, channels)]))
    copies = [
        pltpu.make_async_copy(source, target, sems.at[number])
        for number, (source, target) in enumerate(copies)
    ]
    for copy in copies:
        copy.start()
    for copy in copies:
        copy.wait()


def frame_kernel(cfg, *refs):
    refs = list(refs)
    groups = [refs.pop(0) for _ in range(cfg["groups"])]
    received = refs.pop(0) if cfg["came"] is not None else None
    partial, weight, bias, gain = refs[:4]
    refs = refs[4:]
    refs = refs[cfg["passing"] :]
    out = refs.pop(0) if cfg["sends"] else None
    spread = refs.pop(0 if cfg["later"] else -1)
    tails = [refs.pop(0) for _ in range(cfg["finals"])]
    refs = refs[cfg["keeps"] :]
    doubles = [refs.pop(0) for _ in range(cfg["doubles"])]
    entry = refs.pop(0)
    cols, window, segments = cfg["cols"], cfg["window"], cfg["segments"]
    channels = entry.shape[-1]
    half = lax.axis_index("band") // cfg["per_half"]

    def run(unit):
        have = window - unit
        need = have - 1
        size = have * cols
        if unit == 0:
            step = entry.shape[0] // TAPS

            def place(piece, code):
                number = (code >> (2 * lax.axis_index("band"))) & 3
                entry[pl.ds(pl.multiple_of(number * step, step), step), :] = piece[cfg["piece_at"]]

            *others, own, crossed = groups[:4]
            first, *rest = cfg["places"]
            near = lax.axis_index("tm") == cfg["near"]
            pl.when(near)(functools.partial(place, own, first))
            pl.when(jnp.logical_not(near))(functools.partial(place, crossed, first))
            for piece, code in zip(others, rest):
                place(piece, code)
            source, skip = entry, 0
        else:
            source, skip = received, half * (unit - 1 - cfg["came"])
        wide = source[rows_at(skip, have, cols), :].astype(jnp.float32)
        meansq = jnp.sum(wide * wide, axis=-1, keepdims=True) * (1.0 / channels)
        normed = wide * lax.rsqrt(meansq + 1e-06) * gain[...]
        ready = normed / (1.0 + jnp.exp(-normed))
        column = lax.broadcasted_iota(jnp.int32, ready.shape, 0) & (cols - 1)
        before = jnp.where(column == 0, 0.0, pltpu.roll(ready, 1, 0))
        after = jnp.where(column == cols - 1, 0.0, pltpu.roll(ready, size - 1, 0))
        edge = jnp.zeros((cols, TAPS * channels), jnp.bfloat16)
        spread[pl.ds(0, cols), :] = edge
        spread[pl.ds(size + cols, cols), :] = edge
        for number, value in enumerate((before, ready, after)):
            spread[pl.ds(cols, size), pl.ds(number * channels, channels)] = value.astype(jnp.bfloat16)
        kept = source[rows_at(skip + half, need, cols), :].astype(jnp.float32)
        total = partial[pl.ds(0, need * cols), :] + kept + bias[...]
        total += jnp.dot(taps(spread, half, need, cols), weight[...], preferred_element_type=jnp.float32)
        value = total.astype(jnp.bfloat16)
        if unit < segments - 1:
            out[rows_at(half * (unit - cfg["lowest"]), need, cols), :] = value
        else:
            length = value.shape[0] // len(tails)
            for number, tail in enumerate(tails):
                tail[cfg["tail_at"]] = value[number * length : (number + 1) * length]
            for double, tail in zip(doubles, tails):
                double[...] = tail[...]

    for unit in cfg["units"]:
        pl.when(on_unit(unit, cfg["holders"]))(functools.partial(run, unit))


def keep_kernel(keys, times, per_half, *refs):
    arrived, out, sem = refs[:-2], refs[-2], refs[-1]
    band, position = lax.axis_index("band"), lax.axis_index("segment")
    for (time, index, late), value in zip(keys, arrived):
        here = jnp.logical_and(lax.axis_index("tm") == time, band % per_half == index)
        if time < times - 1:
            here = jnp.logical_and(here, position >= per_half if late else position < per_half)

        @pl.when(here)
        def _():
            copy = pltpu.make_async_copy(value, out, sem)
            copy.start()
            copy.wait()


def history_kernel(cfg, spread, near, far, weight, near_out, far_out):
    cols, window = cfg["cols"], cfg["window"]
    channels = near.shape[-1]
    half = lax.axis_index("band") // cfg["per_half"]

    def run(unit):
        need = window - unit - 1
        here = pl.ds(0, need * cols)
        ready = taps(spread, half, need, cols)
        if unit in cfg["ending"]:
            total = jnp.dot(ready, weight[:, channels:], preferred_element_type=jnp.float32)
            near_out[here, :] = far[here, :] + total
        else:
            total = jnp.dot(ready, weight[...], preferred_element_type=jnp.float32)
            near_out[here, :] = far[here, :] + total[:, channels:]
            far_out[here, :] = total[:, :channels]

    for unit in cfg["later"]:
        pl.when(on_unit(unit, cfg["holders"]))(functools.partial(run, unit))


def local(features, conv_weight, conv_bias, norm_gain):
    times, segments, bands = (lax.axis_size(name) for name in MESH_AXES)
    time, position, band = (lax.axis_index(name) for name in MESH_AXES)
    clips, own_frames, own_rows, cols, channels = features.shape
    frames = own_frames * times
    per_half = bands // HALVES
    window = own_rows * bands // HALVES + segments
    holders = clips // per_half
    piece = own_rows * cols
    assert clips == segments == bands == 4 == 2 * per_half and holders == 2 <= times and window == TAPS * own_rows

    def stream(clip, half):
        return clip // per_half, half * per_half + clip % per_half

    def spot(t, s, b):
        return (t * segments + s) * bands + b

    own, *sources = pl.pallas_call(
        functools.partial(pick_kernel, holders),
        out_shape=[pltpu.VMEM((own_frames, piece, channels), features.dtype)] * 4,
        in_specs=[whole(pltpu.HBM)],
        out_specs=[whole()] * 4,
        scratch_shapes=[pltpu.SemaphoreType.DMA((4,))],
        compiler_params=pltpu.CompilerParams(vmem_limit_bytes=1 << 20),
        name="pick",
    )(pltpu.with_memory_space_constraint(features.reshape(clips, own_frames, piece, channels), pltpu.HBM))
    wanted = [[2 * h + j for h in range(HALVES) for j in range(per_half)], [2, 0, 1, 2], [1, 2, 3, 1]]
    places = [sum((b - at // per_half) << (2 * at) for at, b in enumerate(row)) for row in wanted]

    def gather(number, members):
        routes = []
        for t, clip in members:
            side, (there, lane) = t if t < holders else 0, divmod(clip, per_half)
            if number == 0:
                segment = t if t < holders else 1
            elif there == side:
                segment = 3 if lane == number - 1 else 0
            else:
                segment = 1 + lane
            for h in range(HALVES):
                at = stream(clip, h)[1]
                source = wanted[number][at]
                assert clip == sent_clips(side, source & 1, segment, lambda a, b, c: b if a else c)[number]
                routes.append((spot(t, segment, source), spot(there, 0, at)))
        assert len({a for a, _ in routes}) == len({b for _, b in routes}) == len(routes)
        return lax.ppermute(sources[number], MESH_AXES, routes)

    def far_side(t):
        return [(t, clip) for clip in range(clips) if clip // per_half != (t if t < holders else 0)]

    entries = []
    for t in range(times):
        others = [gather(number, [(t, clip) for clip in range(clips)]) for number in (1, 2)]
        if t == 0:
            crossed = gather(0, [member for side in range(holders) for member in far_side(side)])
        if t < holders:
            entries.append(others + [own, crossed] + (entries[0][:2] if t else []))
        else:
            routes = [(spot(t, 0, b), spot(0, 0, b)) for b in range(bands)]
            entries.append(others + [lax.ppermute(own, MESH_AXES, routes), gather(0, far_side(t))])

    stored = [conv_weight[0].reshape(TAPS, TAPS * TAPS * channels, channels), conv_bias, norm_gain]
    now, past, bias, gain = pl.pallas_call(
        loader_kernel,
        out_shape=[
            pltpu.VMEM((TAPS * TAPS * channels, channels), stored[0].dtype),
            pltpu.VMEM((TAPS * TAPS * channels, 2 * channels), stored[0].dtype),
            pltpu.VMEM(conv_bias.shape, conv_bias.dtype),
            pltpu.VMEM(norm_gain.shape, norm_gain.dtype),
        ],
        in_specs=[whole(pltpu.HBM)] * 3,
        out_specs=[whole()] * 4,
        scratch_shapes=[pltpu.SemaphoreType.DMA((5,))],
        compiler_params=pltpu.CompilerParams(vmem_limit_bytes=1 << 20),
        name="loader",
    )(*[pltpu.with_memory_space_constraint(value, pltpu.HBM) for value in stored])
    now, past, bias, gain = (resident(value) for value in (now, past, bias, gain))

    def leave(value, there, index, group):
        routes = []
        for clip in group:
            for h in range(HALVES):
                t, b = stream(clip, h)
                routes.append((spot(t, segments - 1, b), spot(there, clip, h * per_half + index)))
        return lax.ppermute(value, MESH_AXES, routes)

    state = ((window - 1) * cols, channels)
    near = jnp.zeros(state, jnp.float32)
    far = jnp.zeros(state, jnp.float32)
    lag = min(frames, DEPTH)
    slots = frames + lag * (segments - 1)
    moving = {}
    tails = []
    waiting = []
    landed = {}
    for slot in range(slots):
        units = working(slot, frames, segments, lag)
        senders_now = [s for s in units if s < segments - 1]
        last = slot - lag * (segments - 1)
        finals = per_half if last >= 0 else 0
        middle = finals and last % own_frames > 0
        closing = slot + 1 == slots
        old = [key for key, (_, since) in landed.items() if closing and since < slot - 1]
        keeps = len(old) + len(waiting)
        doubles = finals if finals and not closing and last % own_frames == own_frames - 1 else 0
        cfg = dict(
            units=units,
            later=[s for s in units if slot - lag * s < frames - 1],
            ending=[s for s in units if slot - lag * s == frames - 2],
            sends=bool(senders_now),
            lowest=min(senders_now, default=0),
            groups=len(entries[slot // own_frames]) if slot < frames else 0,
            places=places,
            piece_at=slot % own_frames,
            near=slot // own_frames if slot // own_frames < holders else 0,
            came=min(working(slot - lag, frames, segments, lag)) if slot >= lag else None,
            finals=finals,
            tail_at=last % own_frames,
            passing=(finals if middle else 0) + keeps,
            keeps=keeps,
            doubles=doubles,
            cols=cols,
            window=window,
            segments=segments,
                        per_half=per_half,
            holders=holders,
        )
        operands = []
        if slot < frames:
            operands += [resident(value) for value in entries[slot // own_frames]]
        if slot >= lag:
            operands.append(resident(moving.pop(slot - lag)))
        operands += [resident(near), now, bias, gain]
        shapes = []
        if cfg["sends"]:
            shapes.append(pltpu.VMEM(((window - 1 - cfg["lowest"]) * cols, channels), jnp.bfloat16))
        wide = pltpu.VMEM(((window + 2) * cols, TAPS * channels), jnp.bfloat16)
        if cfg["later"]:
            shapes.append(wide)
        shape = pltpu.VMEM((own_frames, piece, channels), jnp.bfloat16)
        aliases = {}
        if middle:
            for index, value in enumerate(tails):
                aliases[len(operands)] = len(shapes) + index
                operands.append(resident(value))
        shapes += [shape] * finals
        for value in [landed[key][0] for key in old] + [value for _, _, value in waiting]:
            aliases[len(operands)] = len(shapes)
            operands.append(resident(value))
            shapes.append(shape)
        shapes += [shape] * doubles
        results = list(
            pl.pallas_call(
                functools.partial(frame_kernel, cfg),
                out_shape=shapes,
                in_specs=[whole()] * len(operands),
                out_specs=[whole()] * len(shapes),
                scratch_shapes=[pltpu.VMEM((window * cols, channels), jnp.bfloat16)] + ([] if cfg["later"] else [wide]),
                input_output_aliases=aliases,
                compiler_params=pltpu.CompilerParams(vmem_limit_bytes=VMEM_LIMIT),
                cost_estimate=pl.CostEstimate(flops=0, transcendentals=0, bytes_accessed=1 << 10),
                name="frame",
            )(*operands)
        )
        out = results.pop(0) if cfg["sends"] else None
        spread = results.pop(0) if cfg["later"] else None
        tails = results[:finals]
        if cfg["sends"]:
            moving[slot] = lax.ppermute(out, "segment", [(s, s + 1) for s in senders_now])
        kept = results[finals:]
        for key, value in zip(old, kept):
            landed[key] = (value, slot)
        for (there, index, _), value in zip(waiting, kept[len(old) :]):
            landed[there, index, 1] = (leave(value, there, index, range(per_half, clips)), slot)
        waiting = []
        if finals and last % own_frames == own_frames - 1:
            there = last // own_frames
            if not closing:
                waiting = [(there, index, value) for index, value in enumerate(kept[keeps:])]
            for index, value in enumerate(tails):
                group = range(clips if closing else per_half)
                landed[there, index, 0] = (leave(value, there, index, group), slot)
        if cfg["later"]:
            near, far = pl.pallas_call(
                functools.partial(history_kernel, cfg),
                out_shape=[pltpu.VMEM(state, jnp.float32)] * 2,
                in_specs=[whole()] * 4,
                out_specs=[whole()] * 2,
                input_output_aliases={1: 0, 2: 1},
                compiler_params=pltpu.CompilerParams(vmem_limit_bytes=VMEM_LIMIT),
                cost_estimate=pl.CostEstimate(flops=0, transcendentals=0, bytes_accessed=1 << 10),
                name="history",
            )(resident(spread), resident(near), resident(far), past)

    result = pl.pallas_call(
        functools.partial(keep_kernel, list(landed), times, per_half),
        out_shape=jax.ShapeDtypeStruct((own_frames, piece, channels), features.dtype),
        in_specs=[whole()] * len(landed),
        out_specs=whole(pltpu.HBM),
        scratch_shapes=[pltpu.SemaphoreType.DMA],
        compiler_params=pltpu.CompilerParams(vmem_limit_bytes=1 << 20),
        cost_estimate=pl.CostEstimate(flops=0, transcendentals=0, bytes_accessed=1 << 10),
        name="keep",
    )(*[resident(value) for value, _ in landed.values()])
    return result.reshape(1, own_frames, own_rows, cols, channels)


def solution(mesh):
    return jax.shard_map(
        local,
        mesh=mesh,
        in_specs=(
            P(None, "tm", "band", None, None),
            P("segment", None, None, None),
            P("segment", None),
            P("segment", None),
        ),
        out_specs=P("segment", "tm", "band", None, None),
        check_vma=False,
    )
```

```python
import functools

import jax
import jax.numpy as jnp
from jax import lax
from jax.experimental import pallas as pl
from jax.experimental.pallas import tpu as pltpu
from jax.sharding import PartitionSpec as P

HALVES = 2
DEPTH = 4
TAPS = 3
VMEM_LIMIT = 24 << 20
MESH_AXES = ("tm", "segment", "band")


def whole(space=pltpu.VMEM):
    return pl.BlockSpec(memory_space=space)


def resident(value):
    return pltpu.with_memory_space_constraint(value, pltpu.VMEM)


def working(slot, frames, segments, lag):
    return [s for s in range(segments) if 0 <= slot - lag * s < frames]


def on_unit(unit, holders):
    here = lax.axis_index("segment") == unit
    if holders < lax.axis_size("tm"):
        here = jnp.logical_and(here, lax.axis_index("tm") < holders)
    return here


def rows_at(start, count, cols):
    return pl.ds(pl.multiple_of(start * cols, cols), count * cols)


def sent_clips(side, lane, segment, choose):
    near, far = 2 * side, 2 - 2 * side
    behind = far + (segment & 1)
    return (
        far + lane,
        choose(segment == 0, near + 1, choose(segment == 1, near, behind)),
        choose(segment == 0, near, choose(segment == 1, near + 1, behind)),
    )


def pick_kernel(holders, source, own, across, second, third, sems):
    time = lax.axis_index("tm")
    side = jnp.where(time < holders, time, 0)
    lane = lax.axis_index("band") & 1
    clips = (2 * side + lane, *sent_clips(side, lane, lax.axis_index("segment"), jnp.where))
    copies = [
        pltpu.make_async_copy(source.at[clip], target, sems.at[number])
        for number, (clip, target) in enumerate(zip(clips, (own, across, second, third)))
    ]
    for copy in copies:
        copy.start()
    for copy in copies:
        copy.wait()


def taps(spread, start, count, cols):
    return jnp.concatenate([spread[rows_at(start + row, count, cols), :] for row in range(TAPS)], axis=1)


def loader_kernel(weight, bias, gain, now, past, bias_out, gain_out, sems):
    channels = weight.shape[-1]
    copies = [(bias, bias_out), (gain, gain_out), (weight.at[2], now)]
    for age in range(2):
        copies.append((weight.at[age], past.at[:, pl.ds(age * channels, channels)]))
    copies = [
        pltpu.make_async_copy(source, target, sems.at[number])
        for number, (source, target) in enumerate(copies)
    ]
    for copy in copies:
        copy.start()
    for copy in copies:
        copy.wait()


def frame_kernel(cfg, *refs):
    refs = list(refs)
    groups = [refs.pop(0) for _ in range(cfg["groups"])]
    received = refs.pop(0) if cfg["came"] is not None else None
    partial, weight, bias, gain = refs[:4]
    refs = refs[4:]
    refs = refs[cfg["passing"] :]
    out = refs.pop(0) if cfg["sends"] else None
    spread = refs.pop(0 if cfg["later"] else -1)
    tails = [refs.pop(0) for _ in range(cfg["finals"])]
    refs = refs[cfg["keeps"] :]
    doubles = [refs.pop(0) for _ in range(cfg["doubles"])]
    entry = refs.pop(0)
    cols, window, segments = cfg["cols"], cfg["window"], cfg["segments"]
    channels = entry.shape[-1]
    half = lax.axis_index("band") // cfg["per_half"]

    def run(unit):
        have = window - unit
        need = have - 1
        size = have * cols
        if unit == 0:
            step = entry.shape[0] // TAPS

            def place(piece, code):
                number = (code >> (2 * lax.axis_index("band"))) & 3
                entry[pl.ds(pl.multiple_of(number * step, step), step), :] = piece[cfg["piece_at"]]

            *others, own, crossed = groups[:4]
            first, *rest = cfg["places"]
            near = lax.axis_index("tm") == cfg["near"]
            pl.when(near)(functools.partial(place, own, first))
            pl.when(jnp.logical_not(near))(functools.partial(place, crossed, first))
            for piece, code in zip(others, rest):
                place(piece, code)
            source, skip = entry, 0
        else:
            source, skip = received, half * (unit - 1 - cfg["came"])
        wide = source[rows_at(skip, have, cols), :].astype(jnp.float32)
        meansq = jnp.sum(wide * wide, axis=-1, keepdims=True) * (1.0 / channels)
        normed = wide * lax.rsqrt(meansq + 1e-06) * gain[...]
        ready = normed / (1.0 + jnp.exp(-normed))
        column = lax.broadcasted_iota(jnp.int32, ready.shape, 0) & (cols - 1)
        before = jnp.where(column == 0, 0.0, pltpu.roll(ready, 1, 0))
        after = jnp.where(column == cols - 1, 0.0, pltpu.roll(ready, size - 1, 0))
        edge = jnp.zeros((cols, TAPS * channels), jnp.bfloat16)
        spread[pl.ds(0, cols), :] = edge
        spread[pl.ds(size + cols, cols), :] = edge
        for number, value in enumerate((before, ready, after)):
            spread[pl.ds(cols, size), pl.ds(number * channels, channels)] = value.astype(jnp.bfloat16)
        kept = source[rows_at(skip + half, need, cols), :].astype(jnp.float32)
        total = partial[pl.ds(0, need * cols), :] + kept + bias[...]
        total += jnp.dot(taps(spread, half, need, cols), weight[...], preferred_element_type=jnp.float32)
        value = total.astype(jnp.bfloat16)
        if unit < segments - 1:
            out[rows_at(half * (unit - cfg["lowest"]), need, cols), :] = value
        else:
            length = value.shape[0] // len(tails)
            for number, tail in enumerate(tails):
                tail[cfg["tail_at"]] = value[number * length : (number + 1) * length]
            for double, tail in zip(doubles, tails):
                double[...] = tail[...]

    for unit in cfg["units"]:
        pl.when(on_unit(unit, cfg["holders"]))(functools.partial(run, unit))


def history_kernel(cfg, spread, near, far, weight, near_out, far_out):
    cols, window = cfg["cols"], cfg["window"]
    channels = near.shape[-1]
    half = lax.axis_index("band") // cfg["per_half"]

    def run(unit):
        need = window - unit - 1
        here = pl.ds(0, need * cols)
        ready = taps(spread, half, need, cols)
        if unit in cfg["ending"]:
            total = jnp.dot(ready, weight[:, channels:], preferred_element_type=jnp.float32)
            near_out[here, :] = far[here, :] + total
        else:
            total = jnp.dot(ready, weight[...], preferred_element_type=jnp.float32)
            near_out[here, :] = far[here, :] + total[:, channels:]
            far_out[here, :] = total[:, :channels]

    for unit in cfg["later"]:
        pl.when(on_unit(unit, cfg["holders"]))(functools.partial(run, unit))


def local(features, conv_weight, conv_bias, norm_gain):
    times, segments, bands = (lax.axis_size(name) for name in MESH_AXES)
    time, position, band = (lax.axis_index(name) for name in MESH_AXES)
    clips, own_frames, own_rows, cols, channels = features.shape
    frames = own_frames * times
    per_half = bands // HALVES
    window = own_rows * bands // HALVES + segments
    holders = clips // per_half
    piece = own_rows * cols
    assert clips == segments == bands == 4 == 2 * per_half and holders == 2 <= times and window == TAPS * own_rows

    def stream(clip, half):
        return clip // per_half, half * per_half + clip % per_half

    def spot(t, s, b):
        return (t * segments + s) * bands + b

    own, *sources = pl.pallas_call(
        functools.partial(pick_kernel, holders),
        out_shape=[pltpu.VMEM((own_frames, piece, channels), features.dtype)] * 4,
        in_specs=[whole(pltpu.HBM)],
        out_specs=[whole()] * 4,
        scratch_shapes=[pltpu.SemaphoreType.DMA((4,))],
        compiler_params=pltpu.CompilerParams(vmem_limit_bytes=1 << 20),
        name="pick",
    )(pltpu.with_memory_space_constraint(features.reshape(clips, own_frames, piece, channels), pltpu.HBM))
    wanted = [[2 * h + j for h in range(HALVES) for j in range(per_half)], [2, 0, 1, 2], [1, 2, 3, 1]]
    places = [sum((b - at // per_half) << (2 * at) for at, b in enumerate(row)) for row in wanted]

    def gather(number, members):
        routes = []
        for t, clip in members:
            side, (there, lane) = t if t < holders else 0, divmod(clip, per_half)
            if number == 0:
                segment = t if t < holders else 1
            elif there == side:
                segment = 1 if lane == number - 1 else 0
            else:
                segment = 2 + lane
            for h in range(HALVES):
                at = stream(clip, h)[1]
                source = wanted[number][at]
                assert clip == sent_clips(side, source & 1, segment, lambda a, b, c: b if a else c)[number]
                routes.append((spot(t, segment, source), spot(there, 0, at)))
        assert len({a for a, _ in routes}) == len({b for _, b in routes}) == len(routes)
        return lax.ppermute(sources[number], MESH_AXES, routes)

    def far_side(t):
        return [(t, clip) for clip in range(clips) if clip // per_half != (t if t < holders else 0)]

    entries = []
    for t in range(times):
        others = [gather(number, [(t, clip) for clip in range(clips)]) for number in (1, 2)]
        if t == 0:
            crossed = gather(0, [member for side in range(holders) for member in far_side(side)])
        if t < holders:
            entries.append(others + [own, crossed] + (entries[0][:2] if t else []))
        else:
            routes = [(spot(t, 0, b), spot(0, 0, b)) for b in range(bands)]
            entries.append(others + [lax.ppermute(own, MESH_AXES, routes), gather(0, far_side(t))])

    stored = [conv_weight[0].reshape(TAPS, TAPS * TAPS * channels, channels), conv_bias, norm_gain]
    now, past, bias, gain = pl.pallas_call(
        loader_kernel,
        out_shape=[
            pltpu.VMEM((TAPS * TAPS * channels, channels), stored[0].dtype),
            pltpu.VMEM((TAPS * TAPS * channels, 2 * channels), stored[0].dtype),
            pltpu.VMEM(conv_bias.shape, conv_bias.dtype),
            pltpu.VMEM(norm_gain.shape, norm_gain.dtype),
        ],
        in_specs=[whole(pltpu.HBM)] * 3,
        out_specs=[whole()] * 4,
        scratch_shapes=[pltpu.SemaphoreType.DMA((5,))],
        compiler_params=pltpu.CompilerParams(vmem_limit_bytes=1 << 20),
        name="loader",
    )(*[pltpu.with_memory_space_constraint(value, pltpu.HBM) for value in stored])
    now, past, bias, gain = (resident(value) for value in (now, past, bias, gain))

    def leave(value, there, index, group):
        routes = []
        for clip in group:
            for h in range(HALVES):
                t, b = stream(clip, h)
                routes.append((spot(t, segments - 1, b), spot(there, clip, h * per_half + index)))
        return lax.ppermute(value, MESH_AXES, routes)

    state = ((window - 1) * cols, channels)
    near = jnp.zeros(state, jnp.float32)
    far = jnp.zeros(state, jnp.float32)
    lag = min(frames, DEPTH)
    slots = frames + lag * (segments - 1)
    moving = {}
    tails = []
    waiting = []
    landed = {}
    for slot in range(slots):
        units = working(slot, frames, segments, lag)
        senders_now = [s for s in units if s < segments - 1]
        last = slot - lag * (segments - 1)
        finals = per_half if last >= 0 else 0
        middle = finals and last % own_frames > 0
        closing = slot + 1 == slots
        old = [key for key, (_, since) in landed.items() if closing and since < slot - 1]
        keeps = len(old) + len(waiting)
        doubles = finals if finals and not closing and last % own_frames == own_frames - 1 else 0
        cfg = dict(
            units=units,
            later=[s for s in units if slot - lag * s < frames - 1],
            ending=[s for s in units if slot - lag * s == frames - 2],
            sends=bool(senders_now),
            lowest=min(senders_now, default=0),
            groups=len(entries[slot // own_frames]) if slot < frames else 0,
            places=places,
            piece_at=slot % own_frames,
            near=slot // own_frames if slot // own_frames < holders else 0,
            came=min(working(slot - lag, frames, segments, lag)) if slot >= lag else None,
            finals=finals,
            tail_at=last % own_frames,
            passing=(finals if middle else 0) + keeps,
            keeps=keeps,
            doubles=doubles,
            cols=cols,
            window=window,
            segments=segments,
                        per_half=per_half,
            holders=holders,
        )
        operands = []
        if slot < frames:
            operands += [resident(value) for value in entries[slot // own_frames]]
        if slot >= lag:
            operands.append(resident(moving.pop(slot - lag)))
        operands += [resident(near), now, bias, gain]
        shapes = []
        if cfg["sends"]:
            shapes.append(pltpu.VMEM(((window - 1 - cfg["lowest"]) * cols, channels), jnp.bfloat16))
        wide = pltpu.VMEM(((window + 2) * cols, TAPS * channels), jnp.bfloat16)
        if cfg["later"]:
            shapes.append(wide)
        shape = pltpu.VMEM((own_frames, piece, channels), jnp.bfloat16)
        aliases = {}
        if middle:
            for index, value in enumerate(tails):
                aliases[len(operands)] = len(shapes) + index
                operands.append(resident(value))
        shapes += [shape] * finals
        for value in [landed[key][0] for key in old] + [value for _, _, value in waiting]:
            aliases[len(operands)] = len(shapes)
            operands.append(resident(value))
            shapes.append(shape)
        shapes += [shape] * doubles
        results = list(
            pl.pallas_call(
                functools.partial(frame_kernel, cfg),
                out_shape=shapes,
                in_specs=[whole()] * len(operands),
                out_specs=[whole()] * len(shapes),
                scratch_shapes=[pltpu.VMEM((window * cols, channels), jnp.bfloat16)] + ([] if cfg["later"] else [wide]),
                input_output_aliases=aliases,
                compiler_params=pltpu.CompilerParams(vmem_limit_bytes=VMEM_LIMIT),
                cost_estimate=pl.CostEstimate(flops=0, transcendentals=0, bytes_accessed=1 << 10),
                name="frame",
            )(*operands)
        )
        out = results.pop(0) if cfg["sends"] else None
        spread = results.pop(0) if cfg["later"] else None
        tails = results[:finals]
        if cfg["sends"]:
            moving[slot] = lax.ppermute(out, "segment", [(s, s + 1) for s in senders_now])
        kept = results[finals:]
        for key, value in zip(old, kept):
            landed[key] = (value, slot)
        for (there, index, _), value in zip(waiting, kept[len(old) :]):
            landed[there, index, 1] = (leave(value, there, index, range(per_half, clips)), slot)
        waiting = []
        if finals and last % own_frames == own_frames - 1:
            there = last // own_frames
            if not closing:
                waiting = [(there, index, value) for index, value in enumerate(kept[keeps:])]
            for index, value in enumerate(tails):
                group = range(clips if closing else per_half)
                landed[there, index, 0] = (leave(value, there, index, group), slot)
        if cfg["later"]:
            near, far = pl.pallas_call(
                functools.partial(history_kernel, cfg),
                out_shape=[pltpu.VMEM(state, jnp.float32)] * 2,
                in_specs=[whole()] * 4,
                out_specs=[whole()] * 2,
                input_output_aliases={1: 0, 2: 1},
                compiler_params=pltpu.CompilerParams(vmem_limit_bytes=VMEM_LIMIT),
                cost_estimate=pl.CostEstimate(flops=0, transcendentals=0, bytes_accessed=1 << 10),
                name="history",
            )(resident(spread), resident(near), resident(far), past)

    result = None
    for (t, index, late), (value, _) in landed.items():
        here = jnp.logical_and(time == t, band % per_half == index)
        if t < times - 1:
            here = jnp.logical_and(here, (position >= per_half) == bool(late))
        result = value if result is None else jnp.where(here, value, result)
    return result.reshape(1, own_frames, own_rows, cols, channels)


def solution(mesh):
    return jax.shard_map(
        local,
        mesh=mesh,
        in_specs=(
            P(None, "tm", "band", None, None),
            P("segment", None, None, None),
            P("segment", None),
            P("segment", None),
        ),
        out_specs=P("segment", "tm", "band", None, None),
        check_vma=False,
    )
```
